32 devices in a mesh: grid: 8 (over z, y), bead: 4 (over x, core).
Axes of the slice: x: 2, y: 2, z: 4, core: 2. Of those that a mesh axis runs over, the one named last changes fastest.
Arguments:
- positions: float32 [3, 32, 4096], P(None, 'bead', 'grid'), may hold values from -6 to 6
- momenta: float32 [3, 32, 4096], P(None, 'bead', 'grid'), may hold values from -6 to 6
- noise: float32 [3, 32, 4096], P(None, 'bead', 'grid'), may hold values from -6 to 6
- charges: float32 [4096], P('grid'), may hold values from -5 to 5
- slab_route: int32 [4096, 1], P('grid'), may hold values from 0 to 7; in each aligned block of 512 rows (0 to 511, 512 to 1023, ...) at most 128 rows name the same one
- cells: int32 [3, 4096], P(None, 'grid'), may hold values from 0 to 255, as said below
- offsets: float32 [3, 4096], P(None, 'grid'), may hold values from 0 to 0.999
- nbr_tiles: int32 [32, 4], P('grid'), may hold values from 0 to 3
Outputs:
- new_positions: float32 [3, 32, 4096], P(None, 'bead', 'grid')
- new_momenta: float32 [3, 32, 4096], P(None, 'bead', 'grid')
The draws below stay inside these ranges and needn't reach their ends.
Inputs may be any that keep to these rules, and one draw needn't show every extreme that they name: `slab_route`: among the 512 atoms of one domain at most 128 name the same slab, a bound that some block reaches of them. `cells`: row 0 lies below 32, row 1 below 256, row 2 below 256. `nbr_tiles`: tile numbers within the domain of the listing tile.
All inputs are finite; a program needn't handle non-finite values.
Results may differ from the reference program's by a relative error of at most 0.0003.
Values sent between devices are 32-bit elements; how exact they have to be, the bound alone decides.
A program may use at most 64 MiB of HBM per device.

```python
import math
import jax
import jax.numpy as jnp
import numpy as np
from jax import lax

GX = 256
GY = 256
GZ = 256
BEADS = 32
TILE = 128
NBR = 4
ATOM_DEV = 512
SLABS = 8
PLANES = 32
TILE_DEV = 4
CAP = 128
ATOMS = 4096


def draw_cells(key, part):
    keys = jax.random.split(jax.random.fold_in(key, 17), 3)
    plane_draw = jax.random.randint(keys[0], (ATOMS,), 0, PLANES)
    second_draw = jax.random.randint(keys[1], (ATOMS,), 0, GY)
    third_draw = jax.random.randint(keys[2], (ATOMS,), 0, GZ)
    return jnp.stack([plane_draw, second_draw, third_draw]).astype(jnp.int32)


def plant(values, key, least, high):
    longest = values.shape.index(max(values.shape))
    spots = []
    for shift in (0, 1):
        where = [jax.random.randint(jax.random.fold_in(key, axis), (), 0, length) for axis, length in enumerate(values.shape)]
        where[longest] = (where[longest] + shift) % values.shape[longest]
        spots.append(tuple(where))
    return values.at[spots[0]].set(least).at[spots[1]].set(high)


def levels(key, shape, cuts, least, high):
    gain, own = 1.0, jax.random.fold_in(key, 6)
    for axis_at, parts in cuts:
        steps = jnp.exp(jax.random.uniform(jax.random.fold_in(own, axis_at), (parts,), jnp.float32, least / len(cuts), high / len(cuts)))
        gain = gain * jnp.repeat(steps, shape[axis_at] // parts).reshape([-1 if axis == axis_at else 1 for axis in range(len(shape))])
    return gain


def shared_out(key, own, number, rows, count, top, reach, skew):
    order = jax.random.permutation(key, count)
    packed, common = load_shares(count, rows * top, reach, skew, True), load_shares(count, rows * top, reach, skew, False)
    places = jnp.arange(count)

    def named(lengths, turn):
        used = int((lengths > 0).sum())
        fixed = max(1, used // 4)
        moved = fixed + (places - fixed + turn * (used - fixed)) % max(1, count - fixed)
        return jnp.zeros((count,), jnp.int32).at[order[jnp.where(places < fixed, places, moved)]].set(jnp.asarray(lengths, jnp.int32))

    lengths = jnp.where(number % 4 == 0, named(packed, number // 4), named(common, number - number // 4 - 1))
    mixed = jax.random.permutation(jax.random.fold_in(own, 3), count)
    source_of, sink = mixed[0:count // 2 * 2:2], mixed[1:count // 2 * 2:2]
    slack = jnp.minimum(lengths[source_of] - 1, reach - lengths[sink]) // 2
    slack = jnp.where((source_of == order[0]) | (sink == order[0]) | (lengths[sink] == 0), 0, jnp.maximum(slack, 0))
    moved = jax.random.randint(jax.random.fold_in(own, 4), (count // 2,), 0, 1 << 20) % (slack + 1)
    lengths = lengths.at[source_of].add(-moved).at[sink].add(moved)
    members = jnp.searchsorted(jnp.cumsum(lengths), jnp.arange(rows * top), side="right").astype(jnp.int32)
    table = members.reshape(top, rows).T
    table = table[jax.random.permutation(jax.random.fold_in(own, 1), rows)]
    turn = jax.random.randint(jax.random.fold_in(own, 2), (rows, 1), 0, top)
    return jnp.take_along_axis(table, (jnp.arange(top)[None, :] + turn) % top, axis=1)


def load_shares(count, total, reach, skew, full):
    loads = [(1 << 20) // math.isqrt(rank ** skew) + 1 for rank in range(1, count + 1)]
    largest = reach if full else min(reach, max(-(-total // count), total * loads[0] // sum(loads)))
    least = 1 if total - largest >= count - 1 else 0
    given, surplus = [largest] + [least] * (count - 1), total - largest - least * (count - 1)
    while surplus > 0:
        candidates = [i for i in range(1, count) if given[i] < largest] or [i for i in range(1, count) if given[i] < reach]
        whole, budget = sum([loads[i] for i in candidates]), surplus
        for i in candidates:
            more = min(reach - given[i], max(1, budget * loads[i] // whole), surplus)
            given[i] = given[i] + more
            surplus = surplus - more
    return np.array(given)


def normal_values(rng, dims, deviation, bound, cuts=(), kind=jnp.bfloat16):
    drawn = jax.random.normal(rng, dims, jnp.float32) * deviation
    if len(cuts) > 0:
        drawn = levels(rng, dims, cuts, -0.22, 0.18) * drawn
    return jnp.clip(drawn, min=-bound, max=bound).astype(kind)


def setup_inputs(seed: int = 0) -> dict:
    streams_of = jax.random.split(jax.random.key(seed), 9)
    positions = normal_values(streams_of[0], (3, BEADS, ATOMS), 1.0, 6.0, ((1, 4), (2, 8)), jnp.float32)
    momenta = normal_values(streams_of[1], (3, BEADS, ATOMS), 1.0, 6.0, ((1, 4), (2, 8)), jnp.float32)
    noise = normal_values(streams_of[2], (3, BEADS, ATOMS), 1.0, 6.0, ((1, 4), (2, 8)), jnp.float32)
    charges = normal_values(streams_of[3], (ATOMS,), 1.0, 5.0, ((0, 8),), jnp.float32)
    slab_route_keys = jax.random.split(jax.random.fold_in(streams_of[4], 1), ATOMS // ATOM_DEV)
    slab_route_turns = jax.random.permutation(jax.random.fold_in(streams_of[4], 3), ATOMS // ATOM_DEV)
    slab_route = jax.vmap(lambda own, number: shared_out(jax.random.fold_in(streams_of[4], 2), own, number, ATOM_DEV, SLABS, 1, CAP, 2))(slab_route_keys, slab_route_turns).reshape((ATOMS, 1))
    cells = draw_cells(jax.random.fold_in(streams_of[8], 71), 0)
    offsets = jnp.clip(0.999 * jax.random.uniform(streams_of[6], (3, ATOMS), jnp.float32) ** levels(streams_of[6], (3, ATOMS), ((1, 8),), -0.2, 0.2), 0.0, 0.999)
    nbr_tiles = plant(jax.random.randint(streams_of[7], (SLABS * TILE_DEV, NBR), 0, TILE_DEV), jax.random.fold_in(streams_of[7], 1), 0, TILE_DEV - 1).astype(jnp.int32)
    return {"positions": positions, "momenta": momenta, "noise": noise, "charges": charges, "slab_route": slab_route, "cells": cells, "offsets": offsets, "nbr_tiles": nbr_tiles}


highest = lax.Precision.HIGHEST
time_step = 0.5
polymer_frequency = 1.0
centroid_friction = 0.5
coulomb_scale = 100000.0
screen_width = 200.0
pair_strength = 1.0 / 128.0
pair_range = 4.0

def spline(fraction):
    remain = 1.0 - fraction
    square = fraction * fraction
    cubic = square * fraction
    values = [remain * remain * remain / 6.0, (3.0 * cubic - 6.0 * square + 4.0) / 6.0, (-3.0 * cubic + 3.0 * square + 3.0 * fraction + 1.0) / 6.0, cubic / 6.0]
    slopes = [-0.5 * remain * remain, 0.5 * (3.0 * square - 4.0 * fraction), 0.5 * (-3.0 * square + 2.0 * fraction + 1.0), 0.5 * square]
    return (values, slopes)

def influence(index_x, index_y, index_z):
    wave_x = ((index_x + GX // 2) % GX - GX // 2).astype(jnp.float32)
    wave_y = ((index_y + GY // 2) % GY - GY // 2).astype(jnp.float32)
    wave_z = ((index_z + GZ // 2) % GZ - GZ // 2).astype(jnp.float32)
    wave_square = wave_x * wave_x + wave_y * wave_y + wave_z * wave_z
    centre = wave_square == 0.0
    safe_square = jnp.where(centre, 1.0, wave_square)
    return jnp.where(centre, 0.0, coulomb_scale * jnp.exp(-wave_square / (2.0 * screen_width * screen_width)) / safe_square)

def pair_force(centre, beside_all):
    separation = centre[:, :, :, None] - beside_all[:, :, None, :]
    distance_sq = lax.optimization_barrier(jnp.sum(separation * separation, axis=0))
    weight = pair_strength * jnp.exp(-distance_sq / pair_range)
    return lax.optimization_barrier(jnp.sum(weight[None] * separation, axis=3))

def domain_force(local_positions, neighbours):
    tile_count = neighbours.shape[0]
    bead_total = local_positions.shape[1]
    shaped = local_positions.reshape(3, bead_total, tile_count, TILE)

    def one_tile(tile_index):
        centre = lax.dynamic_index_in_dim(shaped, tile_index, 2, keepdims=False)
        beside_all = jnp.take(shaped, neighbours[tile_index], axis=2).reshape(3, bead_total, NBR * TILE)
        return pair_force(centre, beside_all)
    forces = lax.map(one_tile, jnp.arange(tile_count, dtype=jnp.int32))
    return jnp.moveaxis(forces, 0, 2).reshape(3, bead_total, tile_count * TILE)

def mode_matrix(bead_total):
    mode_index = jnp.arange(bead_total, dtype=jnp.int32)[:, None]
    bead_index = jnp.arange(bead_total, dtype=jnp.int32)[None, :]
    angle = (mode_index * bead_index % bead_total).astype(jnp.float32) * (2.0 * math.pi / bead_total)
    middle = bead_total // 2
    first = jnp.full(angle.shape, 1.0 / math.sqrt(bead_total), jnp.float32)
    scaled = math.sqrt(2.0 / bead_total)
    return jnp.where(mode_index == 0, first, jnp.where(mode_index < middle, scaled * jnp.cos(angle), jnp.where(mode_index == middle, jnp.cos(angle) / math.sqrt(bead_total), scaled * jnp.sin(angle))))

def evolve(position_modes, momentum_modes, kicks, mode_index, bead_total):
    frequency = (2.0 * polymer_frequency * jnp.sin(mode_index.astype(jnp.float32) * (math.pi / bead_total)))[None, :, None]
    centroid = (mode_index == 0)[None, :, None]
    half_step = 0.5 * time_step
    cosine_term = jnp.cos(frequency * half_step)
    sine_term = jnp.sin(frequency * half_step)
    safe_frequency = jnp.where(centroid, 1.0, frequency)
    drift_factor = jnp.where(centroid, half_step, sine_term / safe_frequency)

    def rotate(moved_q, moved_p):
        return (moved_q * cosine_term + moved_p * drift_factor, moved_p * cosine_term - moved_q * frequency * sine_term)
    position_modes, momentum_modes = rotate(position_modes, momentum_modes)
    friction = jnp.where(centroid, centroid_friction, 2.0 * frequency)
    damping = jnp.exp(-friction * time_step)
    momentum_modes = damping * momentum_modes + jnp.sqrt(1.0 - damping * damping) * kicks
    return rotate(position_modes, momentum_modes)

def grid_positions(target, cells, offsets, planes):
    first = (target * planes + cells[0]).astype(jnp.float32) + offsets[0]
    second = cells[1].astype(jnp.float32) + offsets[1]
    third = cells[2].astype(jnp.float32) + offsets[2]
    return jnp.stack([first, second, third])

def reference(positions, momenta, noise, charges, slab_route, cells, offsets, nbr_tiles):

    def domain_term(domain):
        domain_block = lax.dynamic_slice_in_dim(positions, domain * ATOM_DEV, ATOM_DEV, 2)
        domain_lists = lax.dynamic_slice_in_dim(nbr_tiles, domain * TILE_DEV, TILE_DEV, 0)
        return domain_force(domain_block, domain_lists)
    short_force = lax.map(domain_term, jnp.arange(SLABS, dtype=jnp.int32))
    short_force = jnp.moveaxis(short_force, 0, 2).reshape(3, BEADS, ATOMS)
    grid_pos = grid_positions(slab_route[:, 0], cells, offsets, PLANES)
    lowest = jnp.floor(grid_pos)
    fraction = grid_pos - lowest
    lowest_int = lowest.astype(jnp.int32)
    values, slopes = spline(fraction)
    charge_grid = jnp.zeros((GX, GY, GZ), jnp.float32)
    for step_x in range(4):
        cell_x = (lowest_int[0] + step_x - 1) % GX
        for step_y in range(4):
            cell_y = (lowest_int[1] + step_y - 1) % GY
            for step_z in range(4):
                cell_z = (lowest_int[2] + step_z - 1) % GZ
                amount = charges * values[step_x][0] * values[step_y][1] * values[step_z][2]
                charge_grid = charge_grid.at[cell_x, cell_y, cell_z].add(amount)
    screen = influence(jnp.arange(GX, dtype=jnp.int32)[:, None, None], jnp.arange(GY, dtype=jnp.int32)[None, :, None], jnp.arange(GZ, dtype=jnp.int32)[None, None, :])
    spectrum = jnp.fft.fftn(charge_grid)
    potential = jnp.real(jnp.fft.ifftn(spectrum * screen)).astype(jnp.float32)
    force_x = jnp.zeros((ATOMS,), jnp.float32)
    force_y = jnp.zeros((ATOMS,), jnp.float32)
    force_z = jnp.zeros((ATOMS,), jnp.float32)
    for step_x in range(4):
        cell_x = (lowest_int[0] + step_x - 1) % GX
        for step_y in range(4):
            cell_y = (lowest_int[1] + step_y - 1) % GY
            for step_z in range(4):
                cell_z = (lowest_int[2] + step_z - 1) % GZ
                sample = potential[cell_x, cell_y, cell_z]
                force_x = force_x + slopes[step_x][0] * values[step_y][1] * values[step_z][2] * sample
                force_y = force_y + values[step_x][0] * slopes[step_y][1] * values[step_z][2] * sample
                force_z = force_z + values[step_x][0] * values[step_y][1] * slopes[step_z][2] * sample
    mesh_force = -charges[None, :] * jnp.stack([force_x, force_y, force_z])
    kicked = momenta + 0.5 * time_step * (short_force + mesh_force[:, None, :])
    matrix = mode_matrix(BEADS)
    position_modes = jnp.einsum('kb,cba->cka', matrix, positions, precision=highest)
    momentum_modes = jnp.einsum('kb,cba->cka', matrix, kicked, precision=highest)
    position_modes, momentum_modes = evolve(position_modes, momentum_modes, noise, jnp.arange(BEADS, dtype=jnp.int32), BEADS)
    new_positions = jnp.einsum('kb,cka->cba', matrix, position_modes, precision=highest)
    new_momenta = jnp.einsum('kb,cka->cba', matrix, momentum_modes, precision=highest)
    return (new_positions, new_momenta)
```

```python
import functools
import math

import jax
import jax.numpy as jnp
import numpy as np
from jax import lax
from jax.experimental import pallas as pl
from jax.experimental.pallas import tpu as pltpu
from jax.sharding import PartitionSpec as P

GX = GY = GZ = 256
WAVES = 8
BIN = 32
WINDOW = 40
CAP = 128
coulomb_scale = 100000.0
screen_width = 200.0

def spline(fraction):
    remain = 1.0 - fraction
    square = fraction * fraction
    cubic = square * fraction
    values = [
        remain * remain * remain / 6.0,
        (3.0 * cubic - 6.0 * square + 4.0) / 6.0,
        (-3.0 * cubic + 3.0 * square + 3.0 * fraction + 1.0) / 6.0,
        cubic / 6.0,
    ]
    slopes = [
        -0.5 * remain * remain,
        0.5 * (3.0 * square - 4.0 * fraction),
        0.5 * (-3.0 * square + 2.0 * fraction + 1.0),
        0.5 * square,
    ]
    return (values, slopes)

def real_waves(length):
    half = length // 2
    row = np.arange(length)
    wave = np.where(row <= half, row, row - half)
    angle = (wave[:, None] * np.arange(length)[None, :] % length) * (2.0 * math.pi / length)
    return np.where((row <= half)[:, None], np.cos(angle), np.sin(angle))

def split_table(table):
    high = table.astype(jnp.bfloat16)
    low = (table - high.astype(np.float64)).astype(jnp.bfloat16)
    return high, low

def split(value):
    high = value.astype(jnp.bfloat16)
    low = (value - high.astype(jnp.float32)).astype(jnp.bfloat16)
    return high, low

NN = ((1,), (0,))
NT = ((1,), (1,))

def dot3(left, right, dims):
    def one(a, b):
        return lax.dot_general(a, b, (dims, ((), ())), preferred_element_type=jnp.float32)
    return one(left[0], right[0]) + (one(left[0], right[1]) + one(left[1], right[0]))

def stencil(position, length, with_slope):
    lowest = jnp.floor(position)
    values, slopes = spline(position - lowest)
    cell = lax.broadcasted_iota(jnp.int32, (length, position.shape[1]), 0)
    step = (cell - (lowest.astype(jnp.int32) - 1)) & (length - 1)
    step = step.astype(jnp.int16)
    hits = [step == jnp.asarray(offset, step.dtype) for offset in range(4)]

    def dense(members):
        out = jnp.zeros(step.shape, jnp.bfloat16)
        for offset in range(4):
            out = jnp.where(hits[offset], members[offset], out)
        return out

    def both(members):
        halves = [split(member) for member in members]
        return dense([half[0] for half in halves]), dense([half[1] for half in halves])

    return (both(values), both(slopes)) if with_slope else (both(values),)

def window(position, base, with_slope):
    lowest = jnp.floor(position)
    values, slopes = spline(position - lowest)
    cell = lax.broadcasted_iota(jnp.int32, (WINDOW, position.shape[1]), 0)
    step = cell - (lowest.astype(jnp.int32) - base)
    hits = [step == offset for offset in range(4)]

    def dense(members):
        out = jnp.zeros(step.shape, jnp.float32)
        for offset in range(4):
            out = jnp.where(hits[offset], members[offset], out)
        return out

    return (dense(values), dense(slopes)) if with_slope else (dense(values),)

def wave_of(group, shape):
    row = lax.broadcasted_iota(jnp.int32, shape, 0)
    half = WAVES // 2
    odd = (group == 0) & (row == half)
    wave = jnp.where(odd, GY // 2, group * half + (row & (half - 1)))
    turn = jnp.where((row < half) | odd, 0, -(GY // 4))
    return wave, turn

def turned(phase):
    phase = phase & (GY - 1)
    angle = (GY // 4 - jnp.abs(phase - GY // 2)).astype(jnp.float32) * (2.0 * math.pi / GY)
    square = angle * angle
    total = 1.0 / 6227020800.0
    for power in (39916800.0, 362880.0, 5040.0, 120.0, 6.0, 1.0):
        sign = -1.0 if power in (39916800.0, 5040.0, 6.0) else 1.0
        total = total * square + sign / power
    return -(angle * total)

def lines(position, group, with_slope):
    lowest = jnp.floor(position)
    values, slopes = spline(position - lowest)
    wave, turn = wave_of(group, (WAVES, position.shape[1]))
    phase = wave * (lowest.astype(jnp.int32) - 1) + turn
    value = slope = 0.0
    for offset in range(4):
        cosine = turned(phase)
        value = value + values[offset] * cosine
        if with_slope:
            slope = slope + slopes[offset] * cosine
        phase = phase + wave
    return (value, slope) if with_slope else (value,)

def mesh_kernel(axes, fields, fxh, fxl, fxth, fxtl, rh, rl, rth, rtl, out, total, filt, wave2):
    domains = fields.shape[0]
    grid_name, bead_name = axes
    bead_count = lax.axis_size(bead_name)
    device = lax.axis_index(grid_name) * bead_count + lax.axis_index(bead_name)
    groups = GY // WAVES
    parts = lax.axis_size(grid_name) * bead_count // groups
    group = lax.rem(device, groups)
    part = lax.div(device, groups)
    bins = GX // BIN
    pack = min(2, domains)
    unroll = min(8, domains) // pack
    chunks = domains // (pack * unroll)

    def block(first, where):
        own = [fields[first + i, :, where] for i in range(pack)]
        return jnp.concatenate(own, axis=1)

    row = lax.broadcasted_iota(jnp.int32, (GX, GZ), 0)
    col = lax.broadcasted_iota(jnp.int32, (GX, GZ), 1)
    wx = jnp.where(row <= GX // 2, row, row - GX // 2)
    wz = jnp.where(col <= GZ // 2, col, col - GZ // 2)
    square = (wx * wx + wz * wz).astype(jnp.float32)
    times = jnp.where((wx & (GX // 2 - 1)) == 0, 1.0, 2.0) * jnp.where((wz & (GZ // 2 - 1)) == 0, 1.0, 2.0)
    if parts > 1:
        times = jnp.where(lax.div(col * parts, GZ) == part, times, 0.0)
    wave2[...] = square
    filt[...] = times * jnp.exp(square * (-1.0 / (2.0 * screen_width * screen_width)))

    for r in range(WAVES):
        total[r, 0:GX + 8, :] = jnp.zeros((GX + 8, GZ), jnp.float32)

    def spread(step, carry):
        s = step // chunks
        where = pl.ds(pl.multiple_of(s * CAP, CAP), CAP)
        base = s * BIN
        part_sum = None
        for j in range(unroll):
            own = block((step % chunks) * (unroll * pack) + j * pack, where)
            x, = window(own[1:2], base, False)
            y, = lines(own[2:3], group, False)
            z, = stencil(own[3:4], GZ, False)
            y = y * own[0:1]
            rows = split(jnp.concatenate([x * y[r:r + 1] for r in range(WAVES)], axis=0))
            got = dot3(rows, z, NT)
            part_sum = got if part_sum is None else part_sum + got
        rows = pl.ds(pl.multiple_of(base, 8), WINDOW)
        for r in range(WAVES):
            total[r, rows, :] += part_sum[r * WINDOW:(r + 1) * WINDOW]
        return carry
    lax.fori_loop(0, bins * chunks, spread, 0)

    def transform(r, carry):
        wave, _ = wave_of_row(group, r)
        wave = jnp.full((1, GZ), wave, jnp.int32)
        wave_square = (wave * wave).astype(jnp.float32)
        count = jnp.where((wave & (GY // 2 - 1)) == 0, 1.0, 2.0)
        scale = count * jnp.exp(wave_square * (-1.0 / (2.0 * screen_width * screen_width))) * (coulomb_scale / (GX * GY * GZ))
        total[r, 0:8, :] += total[r, GX:GX + 8, :]
        t = dot3((fxh[...], fxl[...]), split(total[r, 0:GX, :]), NN)
        t = dot3(split(t), (rth[...], rtl[...]), NN)
        m2 = wave2[...] + wave_square
        t = t * jnp.where(m2 == 0.0, 0.0, filt[...] * scale / jnp.where(m2 == 0.0, 1.0, m2))
        t = dot3(split(t), (rh[...], rl[...]), NN)
        t = dot3((fxth[...], fxtl[...]), split(t), NN)
        total[r, 0:GX, :] = t
        total[r, GX:GX + 8, :] = t[0:8]
        return carry
    lax.fori_loop(0, WAVES, transform, 0)

    def gather(step, carry):
        s = step // chunks
        where = pl.ds(pl.multiple_of(s * CAP, CAP), CAP)
        base = s * BIN
        rows = pl.ds(pl.multiple_of(base, 8), WINDOW)
        near = split(jnp.concatenate([total[r, rows, :] for r in range(WAVES)], axis=0))
        for j in range(unroll):
            first = (step % chunks) * (unroll * pack) + j * pack
            own = block(first, where)
            x, xd = window(own[1:2], base, True)
            y, yd = lines(own[2:3], group, True)
            z, zd = stencil(own[3:4], GZ, True)
            plain = dot3(near, z, NN)
            steep = dot3(near, zd, NN)
            f = [0.0, 0.0, 0.0]
            for r in range(WAVES):
                q = plain[r * WINDOW:(r + 1) * WINDOW]
                f[0] = f[0] + q * y[r:r + 1]
                f[1] = f[1] + q * yd[r:r + 1]
                f[2] = f[2] + steep[r * WINDOW:(r + 1) * WINDOW] * y[r:r + 1]
            f = [f[0] * xd, f[1] * x, f[2] * x]
            for c in range(3):
                force = -own[0:1] * jnp.sum(f[c], axis=0, keepdims=True)
                for i in range(pack):
                    out[first + i, c:c + 1, where] = force[:, i * CAP:(i + 1) * CAP]
        return carry
    lax.fori_loop(0, bins * chunks, gather, 0)

def wave_of_row(group, row):
    half = WAVES // 2
    odd = (group == 0) & (row == half)
    wave = jnp.where(odd, GY // 2, group * half + (row & (half - 1)))
    return wave, odd

def mesh_forces(fields, axes=("grid", "bead")):
    domains = fields.shape[0]
    table = real_waves(GX)
    shifted = np.roll(table, 1, axis=1)
    tables = []
    for t in (shifted, shifted.T, table, table.T):
        tables += [jnp.asarray(v) for v in split_table(t)]
    vmem = pl.BlockSpec(memory_space=pltpu.VMEM)
    return pl.pallas_call(
        functools.partial(mesh_kernel, axes),
        out_shape=jax.ShapeDtypeStruct((domains, 3, GX // BIN * CAP), jnp.float32),
        in_specs=[vmem] * 9,
        out_specs=vmem,
        scratch_shapes=[
            pltpu.VMEM((WAVES, GX + 8, GZ), jnp.float32),
            pltpu.VMEM((GX, GZ), jnp.float32),
            pltpu.VMEM((GX, GZ), jnp.float32),
        ],
        compiler_params=pltpu.CompilerParams(vmem_limit_bytes=48 * 1024 * 1024),
    )(fields, *tables)


TILE = 128
highest = lax.Precision.HIGHEST
time_step = 0.5
polymer_frequency = 1.0
centroid_friction = 0.5
pair_strength = 1.0 / 128.0
pair_range = 4.0
MESH = pl.DeviceIdType.MESH


def greet(names):
    barrier = pltpu.get_barrier_semaphore()
    total = 0
    for name in names:
        count = lax.axis_size(name)
        me = lax.axis_index(name)

        def signal(step, carry):
            peer = lax.rem(me + step, count)
            pl.semaphore_signal(barrier, 1, device_id={name: peer}, device_id_type=MESH)
            return carry

        lax.fori_loop(1, count, signal, 0)
        total += count - 1
    pl.semaphore_wait(barrier, total)


def shares(name, source, target, send_sem, recv_sem):
    count = lax.axis_size(name)
    me = lax.axis_index(name)

    def copy(step, landing):
        peer = lax.rem(me + step, count)
        return pltpu.make_async_remote_copy(
            src_ref=source(peer),
            dst_ref=target(peer if landing else me),
            send_sem=send_sem.at[peer],
            recv_sem=recv_sem.at[peer if landing else me],
            device_id={name: peer},
            device_id_type=MESH,
        )

    def start():
        def one(step, carry):
            copy(step, False).start()
            return carry

        lax.fori_loop(1, count, one, 0)

    def wait():
        def one(step, carry):
            copy(step, True).wait_recv()
            return carry

        lax.fori_loop(1, count, one, 0)

    def drain():
        def one(step, carry):
            copy(step, False).wait_send()
            return carry

        lax.fori_loop(1, count, one, 0)

    return start, wait, drain


def split3(value):
    high = value.astype(jnp.bfloat16)
    rest = value - high.astype(jnp.float32)
    middle = rest.astype(jnp.bfloat16)
    return high, middle, (rest - middle.astype(jnp.float32)).astype(jnp.bfloat16)


def slots_of(route, per_bin):
    atoms = route.shape[1]
    bins = GX // BIN
    owner = lax.div(route, per_bin)
    bin_row = lax.broadcasted_iota(jnp.int32, (2 * bins, atoms), 0)
    mine = bin_row == owner
    before = lax.broadcasted_iota(jnp.int32, (atoms, atoms), 0)
    after = lax.broadcasted_iota(jnp.int32, (atoms, atoms), 1)
    earlier = jnp.where(before < after, 1.0, 0.0).astype(jnp.bfloat16)
    chosen = jnp.where(mine, 1.0, 0.0)
    rank = jnp.dot(chosen.astype(jnp.bfloat16), earlier, preferred_element_type=jnp.float32)
    rank = jnp.sum(chosen * rank, axis=0, keepdims=True)
    return owner * CAP + rank.astype(jnp.int32)


def placement(slot):
    spots = lax.broadcasted_iota(jnp.int32, (GX // BIN * CAP, slot.shape[1]), 0)
    return jnp.where(spots == slot, 1.0, 0.0).astype(jnp.bfloat16)


def pair_forces(weight_of, positions, momenta, kicked):
    beads, atoms = positions.shape[1:]
    tiles = atoms // TILE
    across = [positions[c].T for c in range(3)]

    def body(t, carry):
        where = pl.ds(pl.multiple_of(t * TILE, TILE), TILE)
        for b in range(beads):
            centre = [positions[c, b : b + 1, where] for c in range(3)]
            sums = [jnp.zeros((8, TILE), jnp.float32) for _ in range(3)]
            for m in range(tiles):
                apart = [
                    centre[c] - across[c][m * TILE : (m + 1) * TILE, b : b + 1] for c in range(3)
                ]
                square = apart[0] * apart[0] + apart[1] * apart[1] + apart[2] * apart[2]
                weight = jnp.exp(square * (-1.0 / pair_range))
                for c in range(3):
                    part = jnp.sum((weight * apart[c]).reshape(TILE // 8, 8, TILE), axis=0)
                    sums[c] = sums[c] + weight_of(t, m) * part
            for c in range(3):
                force = jnp.sum(sums[c], axis=0, keepdims=True)
                kicked[c, b : b + 1, where] = momenta[c, b : b + 1, where] + force
        return carry

    lax.fori_loop(0, tiles, body, 0)


def route_kernel(
    planes, neighbours, positions, momenta, noise, charges, route, cells, offsets,
    fields, sources, kicked, slot_out, field_send, field_recv, source_send, source_recv,
):
    grid_rank = lax.axis_index("grid")
    bead_rank = lax.axis_index("bead")
    rows = route[...]
    slot = slots_of(rows, BIN // planes)
    slot_out[...] = slot
    first = (rows * planes + cells[0:1]).astype(jnp.float32) + offsets[0:1]
    rest = cells[1:3].astype(jnp.float32) + offsets[1:3]
    own = jnp.concatenate([charges[...], first, rest], axis=0)
    halves = [part.astype(jnp.float32) for part in split3(own)]
    packed = jnp.concatenate(halves + [jnp.zeros_like(own)], axis=0).astype(jnp.bfloat16)
    got = lax.dot_general(packed, placement(slot), (NT, ((), ())), preferred_element_type=jnp.float32)
    fields[grid_rank] = (got[0:4] + got[4:8]) + got[8:12]
    sources[bead_rank, 0] = positions[...]
    sources[bead_rank, 1] = noise[...]

    greet(("grid", "bead"))
    move = shares("grid", lambda p: fields.at[grid_rank], lambda p: fields.at[p], field_send, field_recv)
    moved = shares("bead", lambda p: sources.at[bead_rank], lambda p: sources.at[p], source_send, source_recv)
    move[0]()
    moved[0]()

    def weight_of(t, m):
        total = 0.0
        for k in range(neighbours.shape[1]):
            total += jnp.where(neighbours[t, k] == m, 0.5 * time_step * pair_strength, 0.0)
        return total

    pair_forces(weight_of, positions, momenta, kicked)
    for step in (1, 2):
        move[step]()
        moved[step]()


def route_fields(positions, momenta, noise, charges, slab_route, cells, offsets, nbr_tiles):
    grid_count = lax.axis_size("grid")
    bead_count = lax.axis_size("bead")
    beads, atoms = positions.shape[1:]
    vmem = pl.BlockSpec(memory_space=pltpu.VMEM)
    dma = pltpu.SemaphoreType.DMA
    pairs = beads * atoms ** 2
    return pl.pallas_call(
        functools.partial(route_kernel, GX // grid_count),
        out_shape=[
            jax.ShapeDtypeStruct((grid_count, 4, GX // BIN * CAP), jnp.float32),
            jax.ShapeDtypeStruct((bead_count, 2, 3, beads, atoms), jnp.float32),
            jax.ShapeDtypeStruct((3, beads, atoms), jnp.float32),
            jax.ShapeDtypeStruct((1, atoms), jnp.int32),
        ],
        in_specs=[pl.BlockSpec(memory_space=pltpu.SMEM)] + [vmem] * 7,
        out_specs=[vmem] * 4,
        scratch_shapes=[dma((grid_count,)), dma((grid_count,)), dma((bead_count,)), dma((bead_count,))],
        compiler_params=pltpu.CompilerParams(
            collective_id=0, has_side_effects=True, vmem_limit_bytes=32 * 1024 * 1024
        ),
        cost_estimate=pl.CostEstimate(
            flops=20 * pairs, bytes_accessed=12 * positions.size, transcendentals=pairs
        ),
    )(
        nbr_tiles, positions, momenta, noise, charges.reshape(1, atoms),
        slab_route.reshape(1, atoms), cells, offsets,
    )


def step_tables(bead_total):
    mode = np.arange(bead_total)
    angle = (mode[:, None] * mode[None, :] % bead_total) * (2.0 * math.pi / bead_total)
    middle = bead_total // 2
    scaled = math.sqrt(2.0 / bead_total)
    column = mode[:, None]
    matrix = np.where(
        column == 0,
        1.0 / math.sqrt(bead_total),
        np.where(
            column < middle,
            scaled * np.cos(angle),
            np.where(
                column == middle, np.cos(angle) / math.sqrt(bead_total), scaled * np.sin(angle)
            ),
        ),
    )
    half = 0.5 * time_step
    frequency = 2.0 * polymer_frequency * np.sin(mode * (math.pi / bead_total))
    cosine = np.cos(frequency * half)
    drift = np.where(mode == 0, half, np.sin(frequency * half) / np.where(mode == 0, 1.0, frequency))
    pull = frequency * np.sin(frequency * half)
    friction = np.where(mode == 0, centroid_friction, 2.0 * frequency)
    damping = np.exp(-friction * time_step)
    kick = np.sqrt(1.0 - damping * damping)
    factors = [
        [cosine * cosine - drift * damping * pull, drift * cosine * (1.0 + damping), drift * kick],
        [-cosine * pull * (1.0 + damping), cosine * damping * cosine - pull * drift, cosine * kick],
    ]
    tables = np.stack(
        [
            np.stack(
                [
                    matrix.T @ (row[0][:, None] * matrix),
                    matrix.T @ (row[1][:, None] * matrix),
                    matrix.T * row[2][None, :],
                ]
            )
            for row in factors
        ]
    )
    return tables.astype(np.float32), (float(factors[0][1][0]), float(factors[1][1][0]))


def finish_kernel(
    centre, tables, partial, sources, kicked, slot, new_positions, new_momenta,
    landed, kicks, level, last, part_send, part_recv, kick_send, kick_recv, last_send, last_recv,
):
    grid_rank = lax.axis_index("grid")
    bead_rank = lax.axis_index("bead")
    bead_count = lax.axis_size("bead")
    domains = partial.shape[0]
    beads = kicked.shape[1]

    greet(("grid", "bead"))
    move = shares("grid", lambda p: partial.at[p], lambda p: landed.at[p], part_send, part_recv)
    moved = shares("bead", lambda p: kicked, lambda p: kicks.at[p], kick_send, kick_recv)
    summed = shares("bead", lambda p: level, lambda p: last.at[p], last_send, last_recv)
    move[0]()
    moved[0]()
    landed[grid_rank] = partial[grid_rank]
    kicks[bead_rank] = kicked[...]
    where = placement(slot[...])
    move[1]()
    total = landed[0]
    for d in range(1, domains):
        total = total + landed[d]
    level[...] = total
    last[bead_rank] = total
    summed[0]()

    moved[1]()
    own = tables[bead_rank]
    stepped = []
    for c in range(3):
        parts = [sources[k, 0, c] for k in range(bead_count)]
        parts += [kicks[k, c] for k in range(bead_count)]
        parts += [sources[k, 1, c] for k in range(bead_count)]
        stepped.append(
            jnp.dot(own, jnp.concatenate(parts, axis=0), precision=highest, preferred_element_type=jnp.float32)
        )
    summed[1]()
    total = last[0]
    for k in range(1, bead_count):
        total = total + last[k]
    halves = [part.astype(jnp.float32) for part in split3(total)]
    packed = jnp.concatenate(halves + [jnp.zeros((16 - 9, total.shape[1]), jnp.float32)], axis=0)
    got = jnp.dot(packed.astype(jnp.bfloat16), where, preferred_element_type=jnp.float32)
    force = (got[0:3] + got[3:6]) + got[6:9]
    for c in range(3):
        new_positions[c] = stepped[c][0:beads] + centre[0] * force[c : c + 1]
        new_momenta[c] = stepped[c][beads:] + centre[1] * force[c : c + 1]
    for each in (move, moved, summed):
        each[2]()


def finish(partial, sources, kicked, slot):
    grid_count = lax.axis_size("grid")
    bead_count = lax.axis_size("bead")
    beads, atoms = kicked.shape[1:]
    tables, centre = step_tables(beads * bead_count)
    shaped = tables.reshape(2, 3, bead_count, beads, -1).transpose(2, 0, 3, 1, 4)
    shaped = shaped.reshape(bead_count, 2 * beads, -1)
    centre = tuple(0.5 * time_step * value for value in centre)
    vmem = pl.BlockSpec(memory_space=pltpu.VMEM)
    dma = pltpu.SemaphoreType.DMA
    part = partial.shape[1:]
    return pl.pallas_call(
        functools.partial(finish_kernel, centre),
        out_shape=[jax.ShapeDtypeStruct(kicked.shape, jnp.float32)] * 2,
        in_specs=[vmem] * 5,
        out_specs=[vmem] * 2,
        scratch_shapes=[
            pltpu.VMEM((grid_count, *part), jnp.float32),
            pltpu.VMEM((bead_count, *kicked.shape), jnp.float32),
            pltpu.VMEM(part, jnp.float32),
            pltpu.VMEM((bead_count, *part), jnp.float32),
            dma((grid_count,)), dma((grid_count,)),
            dma((bead_count,)), dma((bead_count,)),
            dma((bead_count,)), dma((bead_count,)),
        ],
        compiler_params=pltpu.CompilerParams(
            collective_id=1, has_side_effects=True, vmem_limit_bytes=32 * 1024 * 1024
        ),
    )(jnp.asarray(shaped), partial, sources, kicked, slot)


def per_device(positions, momenta, noise, charges, slab_route, cells, offsets, nbr_tiles):
    fields, sources, kicked, slot = route_fields(
        positions, momenta, noise, charges, slab_route, cells, offsets, nbr_tiles
    )
    partial = mesh_forces(fields)
    return finish(partial, sources, kicked, slot)


def solution(mesh):
    in_specs = (
        P(None, "bead", "grid"),
        P(None, "bead", "grid"),
        P(None, "bead", "grid"),
        P("grid"),
        P("grid", None),
        P(None, "grid"),
        P(None, "grid"),
        P("grid", None),
    )
    out_specs = (P(None, "bead", "grid"), P(None, "bead", "grid"))

    def step(*args):
        return tuple(per_device(*args))

    return jax.shard_map(step, mesh=mesh, in_specs=in_specs, out_specs=out_specs, check_vma=False)
```

```python
import functools
import math

import jax
import jax.numpy as jnp
import numpy as np
from jax import lax
from jax.experimental import pallas as pl
from jax.experimental.pallas import tpu as pltpu
from jax.sharding import PartitionSpec as P

GX = GY = GZ = 256
WAVES = 8
BIN = 32
WINDOW = 40
CAP = 128
coulomb_scale = 100000.0
screen_width = 200.0

def spline(fraction):
    remain = 1.0 - fraction
    square = fraction * fraction
    cubic = square * fraction
    values = [
        remain * remain * remain / 6.0,
        (3.0 * cubic - 6.0 * square + 4.0) / 6.0,
        (-3.0 * cubic + 3.0 * square + 3.0 * fraction + 1.0) / 6.0,
        cubic / 6.0,
    ]
    slopes = [
        -0.5 * remain * remain,
        0.5 * (3.0 * square - 4.0 * fraction),
        0.5 * (-3.0 * square + 2.0 * fraction + 1.0),
        0.5 * square,
    ]
    return (values, slopes)

def real_waves(length):
    half = length // 2
    row = np.arange(length)
    wave = np.where(row <= half, row, row - half)
    angle = (wave[:, None] * np.arange(length)[None, :] % length) * (2.0 * math.pi / length)
    return np.where((row <= half)[:, None], np.cos(angle), np.sin(angle))

def split_table(table):
    high = table.astype(jnp.bfloat16)
    low = (table - high.astype(np.float64)).astype(jnp.bfloat16)
    return high, low

def split(value):
    high = value.astype(jnp.bfloat16)
    low = (value - high.astype(jnp.float32)).astype(jnp.bfloat16)
    return high, low

NN = ((1,), (0,))
NT = ((1,), (1,))

def dot3(left, right, dims):
    def one(a, b):
        return lax.dot_general(a, b, (dims, ((), ())), preferred_element_type=jnp.float32)
    return one(left[0], right[0]) + (one(left[0], right[1]) + one(left[1], right[0]))

def stencil(position, length, with_slope):
    lowest = jnp.floor(position)
    values, slopes = spline(position - lowest)
    cell = lax.broadcasted_iota(jnp.int32, (length, position.shape[1]), 0)
    step = (cell - (lowest.astype(jnp.int32) - 1)) & (length - 1)
    step = step.astype(jnp.int16)
    hits = [step == jnp.asarray(offset, step.dtype) for offset in range(4)]

    def dense(members):
        out = jnp.zeros(step.shape, jnp.bfloat16)
        for offset in range(4):
            out = jnp.where(hits[offset], members[offset], out)
        return out

    def both(members):
        halves = [split(member) for member in members]
        return dense([half[0] for half in halves]), dense([half[1] for half in halves])

    return (both(values), both(slopes)) if with_slope else (both(values),)

def window(position, base, with_slope):
    lowest = jnp.floor(position)
    values, slopes = spline(position - lowest)
    cell = lax.broadcasted_iota(jnp.int32, (WINDOW, position.shape[1]), 0)
    step = cell - (lowest.astype(jnp.int32) - base)
    hits = [step == offset for offset in range(4)]

    def dense(members):
        out = jnp.zeros(step.shape, jnp.float32)
        for offset in range(4):
            out = jnp.where(hits[offset], members[offset], out)
        return out

    return (dense(values), dense(slopes)) if with_slope else (dense(values),)

def wave_of(group, shape):
    row = lax.broadcasted_iota(jnp.int32, shape, 0)
    half = WAVES // 2
    odd = (group == 0) & (row == half)
    wave = jnp.where(odd, GY // 2, group * half + (row & (half - 1)))
    turn = jnp.where((row < half) | odd, 0, -(GY // 4))
    return wave, turn

def turned(phase):
    phase = phase & (GY - 1)
    angle = (GY // 4 - jnp.abs(phase - GY // 2)).astype(jnp.float32) * (2.0 * math.pi / GY)
    square = angle * angle
    total = 1.0 / 6227020800.0
    for power in (39916800.0, 362880.0, 5040.0, 120.0, 6.0, 1.0):
        sign = -1.0 if power in (39916800.0, 5040.0, 6.0) else 1.0
        total = total * square + sign / power
    return -(angle * total)

def lines(position, group, with_slope):
    lowest = jnp.floor(position)
    values, slopes = spline(position - lowest)
    wave, turn = wave_of(group, (WAVES, position.shape[1]))
    phase = wave * (lowest.astype(jnp.int32) - 1) + turn
    value = slope = 0.0
    for offset in range(4):
        cosine = turned(phase)
        value = value + values[offset] * cosine
        if with_slope:
            slope = slope + slopes[offset] * cosine
        phase = phase + wave
    return (value, slope) if with_slope else (value,)

def mesh_phases(fields, tables, out, total, filt, wave2, ready):
    domains = fields.shape[0]
    bead_count = lax.axis_size("bead")
    device = lax.axis_index("grid") * bead_count + lax.axis_index("bead")
    fx, fxt, rt, back = [tables.at[i] for i in range(4)]
    groups = GY // WAVES
    parts = lax.axis_size("grid") * bead_count // groups
    group = lax.rem(device, groups)
    part = lax.div(device, groups)
    bins = GX // BIN
    pack = min(2, domains)
    unroll = min(8, domains) // pack
    chunks = domains // (pack * unroll)

    def block(first, where):
        own = [fields[first + i, :, where] for i in range(pack)]
        return jnp.concatenate(own, axis=1)

    row = lax.broadcasted_iota(jnp.int32, (GX, GZ), 0)
    col = lax.broadcasted_iota(jnp.int32, (GX, GZ), 1)
    wx = jnp.where(row <= GX // 2, row, row - GX // 2)
    wz = jnp.where(col <= GZ // 2, col, col - GZ // 2)
    square = (wx * wx + wz * wz).astype(jnp.float32)
    times = jnp.where((wx & (GX // 2 - 1)) == 0, 1.0, 2.0) * jnp.where((wz & (GZ // 2 - 1)) == 0, 1.0, 2.0)
    if parts > 1:
        times = jnp.where(lax.div(col * parts, GZ) == part, times, 0.0)
    wave2[...] = square
    filt[...] = times * jnp.exp(square * (-1.0 / (2.0 * screen_width * screen_width)))

    for r in range(WAVES):
        total[r, 0:GX + 8, :] = jnp.zeros((GX + 8, GZ), jnp.float32)

    def spread(step, carry):
        s = step // chunks
        where = pl.ds(pl.multiple_of(s * CAP, CAP), CAP)
        base = s * BIN
        part_sum = None
        for j in range(unroll):
            own = block((step % chunks) * (unroll * pack) + j * pack, where)
            x, = window(own[1:2], base, False)
            y, = lines(own[2:3], group, False)
            z, = stencil(own[3:4], GZ, False)
            y = y * own[0:1]
            rows = split(jnp.concatenate([x * y[r:r + 1] for r in range(WAVES)], axis=0))
            got = dot3(rows, z, NT)
            part_sum = got if part_sum is None else part_sum + got
        rows = pl.ds(pl.multiple_of(base, 8), WINDOW)
        for r in range(WAVES):
            total[r, rows, :] += part_sum[r * WINDOW:(r + 1) * WINDOW]
        return carry
    lax.fori_loop(0, bins * chunks, spread, 0)

    ready()

    def transform(r, carry):
        wave, _ = wave_of_row(group, r)
        wave = jnp.full((1, GZ), wave, jnp.int32)
        wave_square = (wave * wave).astype(jnp.float32)
        count = jnp.where((wave & (GY // 2 - 1)) == 0, 1.0, 2.0)
        scale = count * jnp.exp(wave_square * (-1.0 / (2.0 * screen_width * screen_width))) * (coulomb_scale / (GX * GY * GZ))
        total[r, 0:8, :] += total[r, GX:GX + 8, :]
        t = dot3((fx[0], fx[1]), split(total[r, 0:GX, :]), NN)
        t = dot3(split(t), (rt[0], rt[1]), NN)
        m2 = wave2[...] + wave_square
        t = t * jnp.where(m2 == 0.0, 0.0, filt[...] * scale / jnp.where(m2 == 0.0, 1.0, m2))
        t = dot3(split(t), (back[0], back[1]), NN)
        t = dot3((fxt[0], fxt[1]), split(t), NN)
        total[r, 0:GX, :] = t
        total[r, GX:GX + 8, :] = t[0:8]
        return carry
    lax.fori_loop(0, WAVES, transform, 0)

    def gather(step, carry):
        s = step // chunks
        where = pl.ds(pl.multiple_of(s * CAP, CAP), CAP)
        base = s * BIN
        rows = pl.ds(pl.multiple_of(base, 8), WINDOW)
        near = split(jnp.concatenate([total[r, rows, :] for r in range(WAVES)], axis=0))
        for j in range(unroll):
            first = (step % chunks) * (unroll * pack) + j * pack
            own = block(first, where)
            x, xd = window(own[1:2], base, True)
            y, yd = lines(own[2:3], group, True)
            z, zd = stencil(own[3:4], GZ, True)
            plain = dot3(near, z, NN)
            steep = dot3(near, zd, NN)
            f = [0.0, 0.0, 0.0]
            for r in range(WAVES):
                q = plain[r * WINDOW:(r + 1) * WINDOW]
                f[0] = f[0] + q * y[r:r + 1]
                f[1] = f[1] + q * yd[r:r + 1]
                f[2] = f[2] + steep[r * WINDOW:(r + 1) * WINDOW] * y[r:r + 1]
            f = [f[0] * xd, f[1] * x, f[2] * x]
            for c in range(3):
                force = -own[0:1] * jnp.sum(f[c], axis=0, keepdims=True)
                for i in range(pack):
                    out[first + i, c:c + 1, where] = force[:, i * CAP:(i + 1) * CAP]
        return carry
    lax.fori_loop(0, bins * chunks, gather, 0)

def wave_of_row(group, row):
    half = WAVES // 2
    odd = (group == 0) & (row == half)
    wave = jnp.where(odd, GY // 2, group * half + (row & (half - 1)))
    return wave, odd


def wave_tables():
    table = real_waves(GX)
    shifted = np.roll(table, 1, axis=1)
    return jnp.stack([jnp.stack(split_table(t)) for t in (shifted, shifted.T, table.T, table)])


TILE = 128
highest = lax.Precision.HIGHEST
time_step = 0.5
polymer_frequency = 1.0
centroid_friction = 0.5
pair_strength = 1.0 / 128.0
pair_range = 4.0
MESH = pl.DeviceIdType.MESH


def greet(names):
    barrier = pltpu.get_barrier_semaphore()
    total = 0
    for name in names:
        count = lax.axis_size(name)
        me = lax.axis_index(name)

        def signal(step, carry):
            peer = lax.rem(me + step, count)
            pl.semaphore_signal(barrier, 1, device_id={name: peer}, device_id_type=MESH)
            return carry

        lax.fori_loop(1, count, signal, 0)
        total += count - 1
    pl.semaphore_wait(barrier, total)


def shares(name, source, target, send_sem, recv_sem):
    count = lax.axis_size(name)
    me = lax.axis_index(name)

    def copy(step, landing):
        peer = lax.rem(me + step, count)
        return pltpu.make_async_remote_copy(
            src_ref=source(peer),
            dst_ref=target(peer if landing else me),
            send_sem=send_sem.at[peer],
            recv_sem=recv_sem.at[peer if landing else me],
            device_id={name: peer},
            device_id_type=MESH,
        )

    def start():
        def one(step, carry):
            copy(step, False).start()
            return carry

        lax.fori_loop(1, count, one, 0)

    def wait():
        def one(step, carry):
            copy(step, True).wait_recv()
            return carry

        lax.fori_loop(1, count, one, 0)

    def drain():
        def one(step, carry):
            copy(step, False).wait_send()
            return carry

        lax.fori_loop(1, count, one, 0)

    return start, wait, drain


def split3(value):
    high = value.astype(jnp.bfloat16)
    rest = value - high.astype(jnp.float32)
    middle = rest.astype(jnp.bfloat16)
    return high, middle, (rest - middle.astype(jnp.float32)).astype(jnp.bfloat16)


def slots_of(route, per_bin):
    atoms = route.shape[1]
    bins = GX // BIN
    owner = lax.div(route, per_bin)
    bin_row = lax.broadcasted_iota(jnp.int32, (2 * bins, atoms), 0)
    mine = bin_row == owner
    before = lax.broadcasted_iota(jnp.int32, (atoms, atoms), 0)
    after = lax.broadcasted_iota(jnp.int32, (atoms, atoms), 1)
    earlier = jnp.where(before < after, 1.0, 0.0).astype(jnp.bfloat16)
    chosen = jnp.where(mine, 1.0, 0.0)
    rank = jnp.dot(chosen.astype(jnp.bfloat16), earlier, preferred_element_type=jnp.float32)
    rank = jnp.sum(chosen * rank, axis=0, keepdims=True)
    return owner * CAP + rank.astype(jnp.int32)


def placement(slot):
    spots = lax.broadcasted_iota(jnp.int32, (GX // BIN * CAP, slot.shape[1]), 0)
    return jnp.where(spots == slot, 1.0, 0.0).astype(jnp.bfloat16)


def pair_forces(weight_of, positions, momenta, kicked):
    beads, atoms = positions.shape[1:]
    tiles = atoms // TILE
    across = [positions[c].T for c in range(3)]

    def body(t, carry):
        where = pl.ds(pl.multiple_of(t * TILE, TILE), TILE)
        for b in range(beads):
            centre = [positions[c, b : b + 1, where] for c in range(3)]
            sums = [jnp.zeros((8, TILE), jnp.float32) for _ in range(3)]
            for m in range(tiles):
                apart = [
                    centre[c] - across[c][m * TILE : (m + 1) * TILE, b : b + 1] for c in range(3)
                ]
                square = apart[0] * apart[0] + apart[1] * apart[1] + apart[2] * apart[2]
                weight = jnp.exp(square * (-1.0 / pair_range))
                for c in range(3):
                    part = jnp.sum((weight * apart[c]).reshape(TILE // 8, 8, TILE), axis=0)
                    sums[c] = sums[c] + weight_of(t, m) * part
            for c in range(3):
                force = jnp.sum(sums[c], axis=0, keepdims=True)
                kicked[c, b : b + 1, where] = momenta[c, b : b + 1, where] + force
        return carry

    lax.fori_loop(0, tiles, body, 0)


def step_tables(bead_total):
    mode = np.arange(bead_total)
    angle = (mode[:, None] * mode[None, :] % bead_total) * (2.0 * math.pi / bead_total)
    middle = bead_total // 2
    scaled = math.sqrt(2.0 / bead_total)
    column = mode[:, None]
    matrix = np.where(
        column == 0,
        1.0 / math.sqrt(bead_total),
        np.where(
            column < middle,
            scaled * np.cos(angle),
            np.where(
                column == middle, np.cos(angle) / math.sqrt(bead_total), scaled * np.sin(angle)
            ),
        ),
    )
    half = 0.5 * time_step
    frequency = 2.0 * polymer_frequency * np.sin(mode * (math.pi / bead_total))
    cosine = np.cos(frequency * half)
    drift = np.where(mode == 0, half, np.sin(frequency * half) / np.where(mode == 0, 1.0, frequency))
    pull = frequency * np.sin(frequency * half)
    friction = np.where(mode == 0, centroid_friction, 2.0 * frequency)
    damping = np.exp(-friction * time_step)
    kick = np.sqrt(1.0 - damping * damping)
    factors = [
        [cosine * cosine - drift * damping * pull, drift * cosine * (1.0 + damping), drift * kick],
        [-cosine * pull * (1.0 + damping), cosine * damping * cosine - pull * drift, cosine * kick],
    ]
    tables = np.stack(
        [
            np.stack(
                [
                    matrix.T @ (row[0][:, None] * matrix),
                    matrix.T @ (row[1][:, None] * matrix),
                    matrix.T * row[2][None, :],
                ]
            )
            for row in factors
        ]
    )
    return tables.astype(np.float32), (float(factors[0][1][0]), float(factors[1][1][0]))


def step_kernel(
    planes, centre, neighbours, positions, momenta, noise, charges, route, cells, offsets, mixing, waves,
    new_positions, new_momenta,
    own_momenta, own_charges, own_route, own_cells, own_offsets, own_mixing, own_waves,
    fields, sources, kicks, partial, landed, level, last, total, filt, wave2,
    local_sem, field_send, field_recv, place_send, place_recv, noise_send, noise_recv,
    kick_send, kick_recv, part_send, part_recv, last_send, last_recv,
):
    grid_rank = lax.axis_index("grid")
    bead_rank = lax.axis_index("bead")
    bead_count = lax.axis_size("bead")
    domains = partial.shape[0]
    beads = kicks.shape[2]

    pairs = [
        (route, own_route), (charges, own_charges), (cells, own_cells), (offsets, own_offsets),
        (positions, sources.at[bead_rank, 0]), (momenta, own_momenta),
        (noise, sources.at[bead_rank, 1]), (mixing, own_mixing), (waves, own_waves),
    ]
    loads = [pltpu.make_async_copy(a, b, local_sem.at[i]) for i, (a, b) in enumerate(pairs)]
    for load in loads:
        load.start()
    for load in loads[0:4]:
        load.wait()

    rows = own_route[...]
    slot = slots_of(rows, BIN // planes)
    first = (rows * planes + own_cells[0:1]).astype(jnp.float32) + own_offsets[0:1]
    rest = own_cells[1:3].astype(jnp.float32) + own_offsets[1:3]
    own = jnp.concatenate([own_charges[...], first, rest], axis=0)
    halves = [part.astype(jnp.float32) for part in split3(own)]
    packed = jnp.concatenate(halves + [jnp.zeros_like(own)], axis=0).astype(jnp.bfloat16)
    got = lax.dot_general(packed, placement(slot), (NT, ((), ())), preferred_element_type=jnp.float32)
    fields[grid_rank] = (got[0:4] + got[4:8]) + got[8:12]

    greet(("grid", "bead"))
    field = shares("grid", lambda p: fields.at[grid_rank], lambda p: fields.at[p], field_send, field_recv)
    place = shares("bead", lambda p: positions, lambda p: sources.at[p, 0], place_send, place_recv)
    draw = shares("bead", lambda p: noise, lambda p: sources.at[p, 1], noise_send, noise_recv)
    kick = shares("bead", lambda p: kicks.at[bead_rank], lambda p: kicks.at[p], kick_send, kick_recv)
    part = shares("grid", lambda p: partial.at[p], lambda p: landed.at[p], part_send, part_recv)
    summed = shares("bead", lambda p: level, lambda p: last.at[p], last_send, last_recv)
    for each in (field, place, draw):
        each[0]()

    def weight_of(t, m):
        total = 0.0
        for k in range(neighbours.shape[1]):
            total += jnp.where(neighbours[t, k] == m, 0.5 * time_step * pair_strength, 0.0)
        return total

    loads[4].wait()
    loads[5].wait()
    pair_forces(weight_of, sources.at[bead_rank, 0], own_momenta, kicks.at[bead_rank])
    kick[0]()
    field[1]()

    mesh_phases(fields, own_waves, partial, total, filt, wave2, loads[8].wait)
    part[0]()

    landed[grid_rank] = partial[grid_rank]
    where = placement(slot)
    for each in (place, draw, kick):
        each[1]()
    loads[6].wait()
    loads[7].wait()
    mix = own_mixing[bead_rank]

    def stepped(c):
        parts = [sources[k, 0, c] for k in range(bead_count)]
        parts += [kicks[k, c] for k in range(bead_count)]
        parts += [sources[k, 1, c] for k in range(bead_count)]
        got = jnp.dot(mix, jnp.concatenate(parts, axis=0), precision=highest, preferred_element_type=jnp.float32)
        new_positions[c] = got[0:beads]
        new_momenta[c] = got[beads:]

    stepped(0)
    part[1]()
    forces = landed[0]
    for d in range(1, domains):
        forces = forces + landed[d]
    level[...] = forces
    last[bead_rank] = forces
    summed[0]()
    stepped(1)
    stepped(2)
    summed[1]()
    forces = last[0]
    for k in range(1, bead_count):
        forces = forces + last[k]
    halves = [part.astype(jnp.float32) for part in split3(forces)]
    packed = jnp.concatenate(halves + [jnp.zeros((16 - 9, forces.shape[1]), jnp.float32)], axis=0)
    got = jnp.dot(packed.astype(jnp.bfloat16), where, preferred_element_type=jnp.float32)
    force = (got[0:3] + got[3:6]) + got[6:9]
    for c in range(3):
        new_positions[c] += centre[0] * force[c : c + 1]
        new_momenta[c] += centre[1] * force[c : c + 1]
    for each in (field, place, draw, kick, part, summed):
        each[2]()


def per_device(positions, momenta, noise, charges, slab_route, cells, offsets, nbr_tiles):
    grid_count = lax.axis_size("grid")
    bead_count = lax.axis_size("bead")
    beads, atoms = positions.shape[1:]
    slots = GX // BIN * CAP
    tables, centre = step_tables(beads * bead_count)
    shaped = tables.reshape(2, 3, bead_count, beads, -1).transpose(2, 0, 3, 1, 4)
    shaped = jnp.asarray(shaped.reshape(bead_count, 2 * beads, -1))
    centre = tuple(0.5 * time_step * value for value in centre)
    waves = wave_tables()
    vmem = pl.BlockSpec(memory_space=pltpu.VMEM)
    anywhere = pl.BlockSpec(memory_space=pl.ANY)
    dma = pltpu.SemaphoreType.DMA
    whole = lambda array: pltpu.VMEM(array.shape, array.dtype)
    f32 = lambda *shape: pltpu.VMEM(shape, jnp.float32)
    charges = charges.reshape(1, atoms)
    slab_route = slab_route.reshape(1, atoms)
    return pl.pallas_call(
        functools.partial(step_kernel, GX // grid_count, centre),
        out_shape=[jax.ShapeDtypeStruct(positions.shape, jnp.float32)] * 2,
        in_specs=[pl.BlockSpec(memory_space=pltpu.SMEM)] + [anywhere] * 9,
        out_specs=[vmem] * 2,
        scratch_shapes=[
            whole(momenta), whole(charges), whole(slab_route), whole(cells), whole(offsets),
            whole(shaped), whole(waves),
            f32(grid_count, 4, slots),
            f32(bead_count, 2, *positions.shape),
            f32(bead_count, *positions.shape),
            f32(grid_count, 3, slots),
            f32(grid_count, 3, slots),
            f32(3, slots),
            f32(bead_count, 3, slots),
            f32(WAVES, GX + 8, GZ),
            f32(GX, GZ),
            f32(GX, GZ),
            dma((9,)),
            dma((grid_count,)), dma((grid_count,)),
            *[dma((bead_count,)) for _ in range(6)],
            dma((grid_count,)), dma((grid_count,)),
            *[dma((bead_count,)) for _ in range(2)],
        ],
        compiler_params=pltpu.CompilerParams(
            collective_id=0, has_side_effects=True, vmem_limit_bytes=60 * 1024 * 1024
        ),
    )(nbr_tiles, positions, momenta, noise, charges, slab_route, cells, offsets, shaped, waves)


def solution(mesh):
    in_specs = (
        P(None, "bead", "grid"),
        P(None, "bead", "grid"),
        P(None, "bead", "grid"),
        P("grid"),
        P("grid", None),
        P(None, "grid"),
        P(None, "grid"),
        P("grid", None),
    )
    out_specs = (P(None, "bead", "grid"), P(None, "bead", "grid"))

    def step(*args):
        return tuple(per_device(*args))

    return jax.shard_map(step, mesh=mesh, in_specs=in_specs, out_specs=out_specs, check_vma=False)
```

```python
import functools
import math

import jax
import jax.numpy as jnp
import numpy as np
from jax import lax
from jax.experimental import pallas as pl
from jax.experimental.pallas import tpu as pltpu
from jax.sharding import PartitionSpec as P

GX = GY = GZ = 256
WAVES = 8
BIN = 32
WINDOW = 36
CAP = 128
coulomb_scale = 100000.0
screen_width = 200.0

def spline(fraction):
    remain = 1.0 - fraction
    square = fraction * fraction
    cubic = square * fraction
    values = [
        remain * remain * remain / 6.0,
        (3.0 * cubic - 6.0 * square + 4.0) / 6.0,
        (-3.0 * cubic + 3.0 * square + 3.0 * fraction + 1.0) / 6.0,
        cubic / 6.0,
    ]
    slopes = [
        -0.5 * remain * remain,
        0.5 * (3.0 * square - 4.0 * fraction),
        0.5 * (-3.0 * square + 2.0 * fraction + 1.0),
        0.5 * square,
    ]
    return (values, slopes)

def real_waves(length):
    half = length // 2
    row = np.arange(length)
    wave = np.where(row <= half, row, row - half)
    angle = (wave[:, None] * np.arange(length)[None, :] % length) * (2.0 * math.pi / length)
    return np.where((row <= half)[:, None], np.cos(angle), np.sin(angle))

def split_table(table):
    high = table.astype(jnp.bfloat16)
    low = (table - high.astype(np.float64)).astype(jnp.bfloat16)
    return high, low

def split(value):
    high = value.astype(jnp.bfloat16)
    low = (value - high.astype(jnp.float32)).astype(jnp.bfloat16)
    return high, low

NN = ((1,), (0,))
NT = ((1,), (1,))

def dot3(left, right, dims):
    def one(a, b):
        return lax.dot_general(a, b, (dims, ((), ())), preferred_element_type=jnp.float32)
    return one(left[0], right[0]) + (one(left[0], right[1]) + one(left[1], right[0]))

def tracks(fields):
    lowest = jnp.floor(fields)
    values, slopes = spline(fields - lowest)
    return [lowest, *values, *slopes]


def stencil(cells, members, length):
    row = lax.broadcasted_iota(jnp.int32, (length, cells.shape[1]), 0).astype(jnp.int16)
    hits = []
    for offset in range(4):
        cell = ((cells + (offset - 1)) & (length - 1)).astype(jnp.int16)
        hits.append(row == cell)

    def dense(rows):
        out = jnp.zeros(row.shape, jnp.bfloat16)
        for offset in range(4):
            out = jnp.where(hits[offset], rows[offset], out)
        return out

    found = []
    for rows in members:
        halves = [split(each) for each in rows]
        found.append((dense([half[0] for half in halves]), dense([half[1] for half in halves])))
    return found


def window(cells, members):
    row = lax.broadcasted_iota(jnp.int32, (WINDOW, cells.shape[1]), 0)
    hits = [row == cells + offset for offset in range(4)]

    def dense(rows):
        out = jnp.zeros(row.shape, jnp.float32)
        for offset in range(4):
            out = jnp.where(hits[offset], rows[offset], out)
        return out

    return [dense(rows) for rows in members]


def wave_of(group, shape):
    row = lax.broadcasted_iota(jnp.int32, shape, 0)
    half = WAVES // 2
    odd = (group == 0) & (row == half)
    wave = jnp.where(odd, GY // 2, group * half + (row & (half - 1)))
    turn = jnp.where((row < half) | odd, 0, -(GY // 4))
    return wave, turn

def turned(phase):
    phase = phase & (GY - 1)
    angle = (GY // 4 - jnp.abs(phase - GY // 2)).astype(jnp.float32) * (2.0 * math.pi / GY)
    square = angle * angle
    total = 1.0 / 6227020800.0
    for power in (39916800.0, 362880.0, 5040.0, 120.0, 6.0, 1.0):
        sign = -1.0 if power in (39916800.0, 5040.0, 6.0) else 1.0
        total = total * square + sign / power
    return -(angle * total)

def lines(cells, members, group):
    wave, turn = wave_of(group, (WAVES, cells.shape[1]))
    phase = wave * (cells - 1) + turn
    found = [0.0 for _ in members]
    for offset in range(4):
        cosine = turned(phase)
        found = [total + rows[offset] * cosine for total, rows in zip(found, members)]
        phase = phase + wave
    return found


def mesh_phases(fields, tables, out, track, along, total, near, filt, wave2, ready, finished):
    domains = fields.shape[0]
    bead_count = lax.axis_size("bead")
    device = lax.axis_index("grid") * bead_count + lax.axis_index("bead")
    fx, fxt, rt, back = [tables.at[i] for i in range(4)]
    groups = GY // WAVES
    parts = lax.axis_size("grid") * bead_count // groups
    group = lax.rem(device, groups)
    part = lax.div(device, groups)
    bins = GX // BIN
    cells_all = GX * WAVES
    halo = (WINDOW - BIN) * WAVES
    pack = 2
    packs = domains // pack
    unroll = min(4, packs)
    chunks = packs // unroll

    for d in range(domains) if domains <= 8 else ():
        for k, rows in enumerate(tracks(fields[d])):
            track[d, k] = rows
    if domains > 8:
        def fill(d, carry):
            for k, rows in enumerate(tracks(fields[d])):
                track[d, k] = rows
            return carry
        lax.fori_loop(0, domains, fill, 0)

    def rows_of(first, where, dim):
        def one(k):
            return jnp.concatenate(
                [track[first + i, k, dim:dim + 1, where] for i in range(pack)], axis=1
            )
        return one(0).astype(jnp.int32), [one(1 + k) for k in range(4)], [one(5 + k) for k in range(4)]

    def span(s):
        return pl.ds(pl.multiple_of(s * CAP, CAP), CAP)

    row = lax.broadcasted_iota(jnp.int32, (GX, GZ), 0)
    col = lax.broadcasted_iota(jnp.int32, (GX, GZ), 1)
    wx = jnp.where(row <= GX // 2, row, row - GX // 2)
    wz = jnp.where(col <= GZ // 2, col, col - GZ // 2)
    square = (wx * wx + wz * wz).astype(jnp.float32)
    times = jnp.where((wx & (GX // 2 - 1)) == 0, 1.0, 2.0) * jnp.where((wz & (GZ // 2 - 1)) == 0, 1.0, 2.0)
    if parts > 1:
        times = jnp.where(lax.div(col * parts, GZ) == part, times, 0.0)
    wave2[...] = square
    filt[...] = times * jnp.exp(square * (-1.0 / (2.0 * screen_width * screen_width)))
    total[...] = jnp.zeros_like(total)
    lanes = total.shape[2]
    tiles = total.shape[0]

    def load(rows):
        return jnp.concatenate([total[i, rows, :] for i in range(tiles)], axis=1)

    def store(rows, value):
        for i in range(tiles):
            total[i, rows, :] = value[:, i * lanes:(i + 1) * lanes]

    def spread(i, carry):
        for k in range(2):
            spread_bin(2 * i + k)
        return carry

    def spread_bin(step):
        s = step // chunks
        where = span(s)
        got = None
        for j in range(unroll):
            pair = (step % chunks) * unroll + j
            first = pair * pack
            cells, values, _ = rows_of(first, where, 1)
            x, = window(cells - s * BIN, [values])
            cells, values, slopes = rows_of(first, where, 2)
            y, yd = lines(cells, [values, slopes], group)
            along[pair, s, 0] = y
            along[pair, s, 1] = yd
            charge = jnp.concatenate([fields[first + i, 0:1, where] for i in range(pack)], axis=1)
            y = y * charge
            cells, values, _ = rows_of(first, where, 3)
            z, = stencil(cells, [values], GZ)
            rows = split(jnp.concatenate([x[i:i + 1] * y for i in range(WINDOW)], axis=0))
            more = dot3(rows, z, NT)
            got = more if got is None else got + more
        rows = pl.ds(pl.multiple_of(s * (BIN * WAVES), BIN * WAVES), WINDOW * WAVES)
        store(rows, load(rows) + got)

    lax.fori_loop(0, bins * chunks // 2, spread, 0)
    total[:, 0:halo, :] += total[:, cells_all:cells_all + halo, :]
    ready()

    chains = 4
    size = cells_all // (2 * chains)

    def row_blocks(i):
        return [pl.ds(pl.multiple_of((i * chains + k) * size, size), size) for k in range(chains)]

    def forward(i, carry):
        at = row_blocks(i)
        got = [dot3(split(load(rows)), (rt[0], rt[1]), NN) for rows in at]
        for rows, each in zip(at, got):
            store(rows, each)
        return carry

    lax.fori_loop(0, 2, forward, 0)

    def middle(i, carry):
        at = [pl.ds(i * chains + k, GX, stride=WAVES) for k in range(chains)]
        got = [dot3((fx[0], fx[1]), split(load(rows)), NN) for rows in at]
        for k in range(chains):
            wave, _ = wave_of_row(group, i * chains + k)
            wave = jnp.full((1, GZ), wave, jnp.int32)
            wave_square = (wave * wave).astype(jnp.float32)
            count = jnp.where((wave & (GY // 2 - 1)) == 0, 1.0, 2.0)
            scale = count * jnp.exp(wave_square * (-1.0 / (2.0 * screen_width * screen_width)))
            scale = scale * (coulomb_scale / (GX * GY * GZ))
            m2 = wave2[...] + wave_square
            got[k] = got[k] * jnp.where(m2 == 0.0, 0.0, filt[...] * scale / jnp.where(m2 == 0.0, 1.0, m2))
        got = [dot3((fxt[0], fxt[1]), split(each), NN) for each in got]
        for rows, each in zip(at, got):
            store(rows, each)
        return carry

    lax.fori_loop(0, WAVES // chains, middle, 0)

    def inverse(i, carry):
        at = row_blocks(i)
        got = [dot3(split(load(rows)), (back[0], back[1]), NN) for rows in at]
        for rows, each in zip(at, got):
            high, low = split(each)
            near[0, rows, :] = high
            near[1, rows, :] = low
        return carry

    lax.fori_loop(0, 2, inverse, 0)
    near[:, cells_all:cells_all + halo, :] = near[:, 0:halo, :]

    half = min(8, bins)
    own_pack = lax.axis_index("grid") // pack

    def gather(step, carry):
        pair = lax.rem(own_pack + 1 + step // (bins // half), packs)
        first = pair * pack
        for j in range(half):
            s = (step % (bins // half)) * half + j
            where = span(s)
            rows = pl.ds(pl.multiple_of(s * (BIN * WAVES), BIN * WAVES), WINDOW * WAVES)
            field = (near[0, rows, :], near[1, rows, :])
            cells, values, slopes = rows_of(first, where, 1)
            x, xd = window(cells - s * BIN, [values, slopes])
            cells, values, slopes = rows_of(first, where, 3)
            z, zd = stencil(cells, [values, slopes], GZ)
            plain = dot3(field, z, NN)
            steep = dot3(field, zd, NN)
            f = [0.0, 0.0, 0.0]
            for i in range(WINDOW):
                q = plain[i * WAVES:(i + 1) * WAVES]
                f[0] = f[0] + q * xd[i:i + 1]
                f[1] = f[1] + q * x[i:i + 1]
                f[2] = f[2] + steep[i * WAVES:(i + 1) * WAVES] * x[i:i + 1]
            y, yd = along[pair, s, 0], along[pair, s, 1]
            f = [f[0] * y, f[1] * yd, f[2] * y]
            charge = jnp.concatenate([fields[first + i, 0:1, where] for i in range(pack)], axis=1)
            for c in range(3):
                force = -charge * jnp.sum(f[c], axis=0, keepdims=True)
                for i in range(pack):
                    out[first + i, c:c + 1, where] = force[:, i * CAP:(i + 1) * CAP]

        @pl.when(step % (bins // half) == bins // half - 1)
        def _():
            for i in range(pack):
                finished(first + i)

        return carry

    lax.fori_loop(0, packs * (bins // half), gather, 0)


def wave_of_row(group, row):
    half = WAVES // 2
    odd = (group == 0) & (row == half)
    wave = jnp.where(odd, GY // 2, group * half + (row & (half - 1)))
    return wave, odd


def wave_tables():
    table = real_waves(GX)
    shifted = np.roll(table, 1, axis=1)
    return jnp.stack([jnp.stack(split_table(t)) for t in (shifted, shifted.T, table.T, table)])


TILE = 128
highest = lax.Precision.HIGHEST
time_step = 0.5
polymer_frequency = 1.0
centroid_friction = 0.5
pair_strength = 1.0 / 128.0
pair_range = 4.0
MESH = pl.DeviceIdType.MESH


def greet(names):
    barrier = pltpu.get_barrier_semaphore()
    total = 0
    for name in names:
        count = lax.axis_size(name)
        me = lax.axis_index(name)

        def signal(step, carry):
            peer = lax.rem(me + step, count)
            pl.semaphore_signal(barrier, 1, device_id={name: peer}, device_id_type=MESH)
            return carry

        lax.fori_loop(1, count, signal, 0)
        total += count - 1
    pl.semaphore_wait(barrier, total)


def shares(name, source, target, send_sem, recv_sem):
    count = lax.axis_size(name)
    me = lax.axis_index(name)

    def copy(step, landing):
        return send(lax.rem(me + step, count), landing)

    def send(peer, landing):
        return pltpu.make_async_remote_copy(
            src_ref=source(peer),
            dst_ref=target(peer if landing else me),
            send_sem=send_sem.at[peer],
            recv_sem=recv_sem.at[peer if landing else me],
            device_id={name: peer},
            device_id_type=MESH,
        )

    def start():
        def one(step, carry):
            copy(step, False).start()
            return carry

        lax.fori_loop(1, count, one, 0)

    def wait():
        def one(step, carry):
            copy(step, True).wait_recv()
            return carry

        lax.fori_loop(1, count, one, 0)

    def drain():
        def one(step, carry):
            copy(step, False).wait_send()
            return carry

        lax.fori_loop(1, count, one, 0)

    return start, wait, drain, lambda peer: send(peer, False).start()


def split3(value):
    high = value.astype(jnp.bfloat16)
    rest = value - high.astype(jnp.float32)
    middle = rest.astype(jnp.bfloat16)
    return high, middle, (rest - middle.astype(jnp.float32)).astype(jnp.bfloat16)


def slots_of(route, per_bin):
    atoms = route.shape[1]
    bins = GX // BIN
    owner = lax.div(route, per_bin)
    bin_row = lax.broadcasted_iota(jnp.int32, (2 * bins, atoms), 0)
    mine = bin_row == owner
    before = lax.broadcasted_iota(jnp.int32, (atoms, atoms), 0)
    after = lax.broadcasted_iota(jnp.int32, (atoms, atoms), 1)
    earlier = jnp.where(before < after, 1.0, 0.0).astype(jnp.bfloat16)
    chosen = jnp.where(mine, 1.0, 0.0)
    rank = jnp.dot(chosen.astype(jnp.bfloat16), earlier, preferred_element_type=jnp.float32)
    rank = jnp.sum(chosen * rank, axis=0, keepdims=True)
    return owner * CAP + rank.astype(jnp.int32)


def placement(slot):
    spots = lax.broadcasted_iota(jnp.int32, (GX // BIN * CAP, slot.shape[1]), 0)
    return jnp.where(spots == slot, 1.0, 0.0).astype(jnp.bfloat16)


def pair_forces(weight_of, positions, momenta, kicked):
    beads, atoms = positions.shape[1:]
    tiles = atoms // TILE
    across = [positions[c].T for c in range(3)]

    def body(t, carry):
        where = pl.ds(pl.multiple_of(t * TILE, TILE), TILE)
        for b in range(beads):
            centre = [positions[c, b : b + 1, where] for c in range(3)]
            sums = [jnp.zeros((8, TILE), jnp.float32) for _ in range(3)]
            for m in range(tiles):
                apart = [
                    centre[c] - across[c][m * TILE : (m + 1) * TILE, b : b + 1] for c in range(3)
                ]
                square = apart[0] * apart[0] + apart[1] * apart[1] + apart[2] * apart[2]
                weight = jnp.exp(square * (-1.0 / pair_range))
                for c in range(3):
                    part = jnp.sum((weight * apart[c]).reshape(TILE // 8, 8, TILE), axis=0)
                    sums[c] = sums[c] + weight_of(t, m) * part
            for c in range(3):
                force = jnp.sum(sums[c], axis=0, keepdims=True)
                kicked[c, b : b + 1, where] = momenta[c, b : b + 1, where] + force
        return carry

    lax.fori_loop(0, tiles, body, 0)


def step_tables(bead_total):
    mode = np.arange(bead_total)
    angle = (mode[:, None] * mode[None, :] % bead_total) * (2.0 * math.pi / bead_total)
    middle = bead_total // 2
    scaled = math.sqrt(2.0 / bead_total)
    column = mode[:, None]
    matrix = np.where(
        column == 0,
        1.0 / math.sqrt(bead_total),
        np.where(
            column < middle,
            scaled * np.cos(angle),
            np.where(
                column == middle, np.cos(angle) / math.sqrt(bead_total), scaled * np.sin(angle)
            ),
        ),
    )
    half = 0.5 * time_step
    frequency = 2.0 * polymer_frequency * np.sin(mode * (math.pi / bead_total))
    cosine = np.cos(frequency * half)
    drift = np.where(mode == 0, half, np.sin(frequency * half) / np.where(mode == 0, 1.0, frequency))
    pull = frequency * np.sin(frequency * half)
    friction = np.where(mode == 0, centroid_friction, 2.0 * frequency)
    damping = np.exp(-friction * time_step)
    kick = np.sqrt(1.0 - damping * damping)
    factors = [
        [cosine * cosine - drift * damping * pull, drift * cosine * (1.0 + damping), drift * kick],
        [-cosine * pull * (1.0 + damping), cosine * damping * cosine - pull * drift, cosine * kick],
    ]
    tables = np.stack(
        [
            np.stack(
                [
                    matrix.T @ (row[0][:, None] * matrix),
                    matrix.T @ (row[1][:, None] * matrix),
                    matrix.T * row[2][None, :],
                ]
            )
            for row in factors
        ]
    )
    return tables.astype(np.float32), (float(factors[0][1][0]), float(factors[1][1][0]))


def step_kernel(
    planes, centre, neighbours, positions, momenta, noise, charges, route, cells, offsets, mixing, waves,
    new_positions, new_momenta,
    own_momenta, own_charges, own_route, own_cells, own_offsets, own_mixing, own_waves,
    fields, sources, kicks, partial, landed, level, last, track, along, total, near, filt, wave2,
    local_sem, field_send, field_recv, place_send, place_recv, noise_send, noise_recv,
    kick_send, kick_recv, part_send, part_recv, last_send, last_recv,
):
    grid_rank = lax.axis_index("grid")
    bead_rank = lax.axis_index("bead")
    bead_count = lax.axis_size("bead")
    domains = partial.shape[0]
    beads = kicks.shape[2]

    pairs = [
        (route, own_route), (charges, own_charges), (cells, own_cells), (offsets, own_offsets),
        (positions, sources.at[bead_rank, 0]), (momenta, own_momenta),
        (noise, sources.at[bead_rank, 1]), (mixing, own_mixing), (waves, own_waves),
    ]
    loads = [pltpu.make_async_copy(a, b, local_sem.at[i]) for i, (a, b) in enumerate(pairs)]
    for load in loads:
        load.start()
    for load in loads[0:4]:
        load.wait()

    rows = own_route[...]
    slot = slots_of(rows, BIN // planes)
    first = (rows * planes + own_cells[0:1]).astype(jnp.float32) + own_offsets[0:1]
    rest = own_cells[1:3].astype(jnp.float32) + own_offsets[1:3]
    own = jnp.concatenate([own_charges[...], first, rest], axis=0)
    halves = [part.astype(jnp.float32) for part in split3(own)]
    packed = jnp.concatenate(halves + [jnp.zeros_like(own)], axis=0).astype(jnp.bfloat16)
    got = lax.dot_general(packed, placement(slot), (NT, ((), ())), preferred_element_type=jnp.float32)
    fields[grid_rank] = (got[0:4] + got[4:8]) + got[8:12]

    greet(("grid", "bead"))
    field = shares("grid", lambda p: fields.at[grid_rank], lambda p: fields.at[p], field_send, field_recv)
    place = shares("bead", lambda p: positions, lambda p: sources.at[p, 0], place_send, place_recv)
    draw = shares("bead", lambda p: noise, lambda p: sources.at[p, 1], noise_send, noise_recv)
    kick = shares("bead", lambda p: kicks.at[bead_rank], lambda p: kicks.at[p], kick_send, kick_recv)
    part = shares("grid", lambda p: partial.at[p], lambda p: landed.at[p], part_send, part_recv)
    summed = shares("bead", lambda p: level, lambda p: last.at[p], last_send, last_recv)
    for each in (field, place, draw):
        each[0]()

    def weight_of(t, m):
        total = 0.0
        for k in range(neighbours.shape[1]):
            total += jnp.where(neighbours[t, k] == m, 0.5 * time_step * pair_strength, 0.0)
        return total

    loads[4].wait()
    loads[5].wait()
    pair_forces(weight_of, sources.at[bead_rank, 0], own_momenta, kicks.at[bead_rank])
    kick[0]()
    field[1]()

    def finished(d):
        @pl.when(d != grid_rank)
        def _():
            part[3](d)

    mesh_phases(
        fields, own_waves, partial, track, along, total, near, filt, wave2, loads[8].wait, finished
    )

    landed[grid_rank] = partial[grid_rank]
    where = placement(slot)
    for each in (place, draw, kick):
        each[1]()
    loads[6].wait()
    loads[7].wait()
    mix = own_mixing[bead_rank]

    def stepped(c):
        parts = [sources[k, 0, c] for k in range(bead_count)]
        parts += [kicks[k, c] for k in range(bead_count)]
        parts += [sources[k, 1, c] for k in range(bead_count)]
        got = jnp.dot(mix, jnp.concatenate(parts, axis=0), precision=highest, preferred_element_type=jnp.float32)
        new_positions[c] = got[0:beads]
        new_momenta[c] = got[beads:]

    stepped(0)
    part[1]()
    forces = landed[0]
    for d in range(1, domains):
        forces = forces + landed[d]
    level[...] = forces
    last[bead_rank] = forces
    summed[0]()
    stepped(1)
    stepped(2)
    summed[1]()
    forces = last[0]
    for k in range(1, bead_count):
        forces = forces + last[k]
    halves = [part.astype(jnp.float32) for part in split3(forces)]
    packed = jnp.concatenate(halves + [jnp.zeros((16 - 9, forces.shape[1]), jnp.float32)], axis=0)
    got = jnp.dot(packed.astype(jnp.bfloat16), where, preferred_element_type=jnp.float32)
    force = (got[0:3] + got[3:6]) + got[6:9]
    for c in range(3):
        new_positions[c] += centre[0] * force[c : c + 1]
        new_momenta[c] += centre[1] * force[c : c + 1]
    for each in (field, place, draw, kick, part, summed):
        each[2]()


def per_device(positions, momenta, noise, charges, slab_route, cells, offsets, nbr_tiles):
    grid_count = lax.axis_size("grid")
    bead_count = lax.axis_size("bead")
    beads, atoms = positions.shape[1:]
    slots = GX // BIN * CAP
    tables, centre = step_tables(beads * bead_count)
    shaped = tables.reshape(2, 3, bead_count, beads, -1).transpose(2, 0, 3, 1, 4)
    shaped = jnp.asarray(shaped.reshape(bead_count, 2 * beads, -1))
    centre = tuple(0.5 * time_step * value for value in centre)
    waves = wave_tables()
    vmem = pl.BlockSpec(memory_space=pltpu.VMEM)
    anywhere = pl.BlockSpec(memory_space=pl.ANY)
    dma = pltpu.SemaphoreType.DMA
    whole = lambda array: pltpu.VMEM(array.shape, array.dtype)
    f32 = lambda *shape: pltpu.VMEM(shape, jnp.float32)
    charges = charges.reshape(1, atoms)
    slab_route = slab_route.reshape(1, atoms)
    return pl.pallas_call(
        functools.partial(step_kernel, GX // grid_count, centre),
        out_shape=[jax.ShapeDtypeStruct(positions.shape, jnp.float32)] * 2,
        in_specs=[pl.BlockSpec(memory_space=pltpu.SMEM)] + [anywhere] * 9,
        out_specs=[vmem] * 2,
        scratch_shapes=[
            whole(momenta), whole(charges), whole(slab_route), whole(cells), whole(offsets),
            whole(shaped), whole(waves),
            f32(grid_count, 4, slots),
            f32(bead_count, 2, *positions.shape),
            f32(bead_count, *positions.shape),
            f32(grid_count, 3, slots),
            f32(grid_count, 3, slots),
            f32(3, slots),
            f32(bead_count, 3, slots),
            f32(grid_count, 9, 4, slots),
            f32(grid_count // 2, GX // BIN, 2, WAVES, 2 * CAP),
            f32(GZ // 128, (GX + WINDOW - BIN) * WAVES, 128),
            pltpu.VMEM((2, (GX + WINDOW - BIN) * WAVES, GZ), jnp.bfloat16),
            f32(GX, GZ),
            f32(GX, GZ),
            dma((9,)),
            dma((grid_count,)), dma((grid_count,)),
            *[dma((bead_count,)) for _ in range(6)],
            dma((grid_count,)), dma((grid_count,)),
            *[dma((bead_count,)) for _ in range(2)],
        ],
        compiler_params=pltpu.CompilerParams(
            collective_id=0, has_side_effects=True, vmem_limit_bytes=60 * 1024 * 1024
        ),
    )(nbr_tiles, positions, momenta, noise, charges, slab_route, cells, offsets, shaped, waves)


def solution(mesh):
    in_specs = (
        P(None, "bead", "grid"),
        P(None, "bead", "grid"),
        P(None, "bead", "grid"),
        P("grid"),
        P("grid", None),
        P(None, "grid"),
        P(None, "grid"),
        P("grid", None),
    )
    out_specs = (P(None, "bead", "grid"), P(None, "bead", "grid"))

    def step(*args):
        return tuple(per_device(*args))

    return jax.shard_map(step, mesh=mesh, in_specs=in_specs, out_specs=out_specs, check_vma=False)
```

```python
import functools
import math

import jax
import jax.numpy as jnp
import numpy as np
from jax import lax
from jax.experimental import pallas as pl
from jax.experimental.pallas import tpu as pltpu
from jax.sharding import PartitionSpec as P

GX = GY = GZ = 256
WAVES = 8
BIN = 32
WINDOW = 36
CAP = 128
coulomb_scale = 100000.0
screen_width = 200.0

def spline(fraction):
    remain = 1.0 - fraction
    square = fraction * fraction
    cubic = square * fraction
    values = [
        remain * remain * remain / 6.0,
        (3.0 * cubic - 6.0 * square + 4.0) / 6.0,
        (-3.0 * cubic + 3.0 * square + 3.0 * fraction + 1.0) / 6.0,
        cubic / 6.0,
    ]
    slopes = [
        -0.5 * remain * remain,
        0.5 * (3.0 * square - 4.0 * fraction),
        0.5 * (-3.0 * square + 2.0 * fraction + 1.0),
        0.5 * square,
    ]
    return (values, slopes)

def real_waves(length):
    half = length // 2
    row = np.arange(length)
    wave = np.where(row <= half, row, row - half)
    angle = (wave[:, None] * np.arange(length)[None, :] % length) * (2.0 * math.pi / length)
    return np.where((row <= half)[:, None], np.cos(angle), np.sin(angle))

def split_table(table):
    high = table.astype(jnp.bfloat16)
    low = (table - high.astype(np.float64)).astype(jnp.bfloat16)
    return high, low

def split(value):
    high = value.astype(jnp.bfloat16)
    low = (value - high.astype(jnp.float32)).astype(jnp.bfloat16)
    return high, low

NN = ((1,), (0,))
NT = ((1,), (1,))

def dot3(left, right, dims):
    def one(a, b):
        return lax.dot_general(a, b, (dims, ((), ())), preferred_element_type=jnp.float32)
    return one(left[0], right[0]) + (one(left[0], right[1]) + one(left[1], right[0]))

def tracks(fields):
    lowest = jnp.floor(fields)
    values, slopes = spline(fields - lowest)
    return [lowest, *values, *slopes]


def stencil(cells, members, length):
    row = lax.broadcasted_iota(jnp.int32, (length, cells.shape[1]), 0).astype(jnp.int16)
    hits = []
    for offset in range(4):
        cell = ((cells + (offset - 1)) & (length - 1)).astype(jnp.int16)
        hits.append(row == cell)

    def dense(rows):
        out = jnp.zeros(row.shape, jnp.bfloat16)
        for offset in range(4):
            out = jnp.where(hits[offset], rows[offset], out)
        return out

    found = []
    for rows in members:
        halves = [split(each) for each in rows]
        found.append((dense([half[0] for half in halves]), dense([half[1] for half in halves])))
    return found


def window(cells, members):
    row = lax.broadcasted_iota(jnp.int32, (WINDOW, cells.shape[1]), 0)
    hits = [row == cells + offset for offset in range(4)]

    def dense(rows):
        out = jnp.zeros(row.shape, jnp.float32)
        for offset in range(4):
            out = jnp.where(hits[offset], rows[offset], out)
        return out

    return [dense(rows) for rows in members]


def wave_of(group, shape):
    row = lax.broadcasted_iota(jnp.int32, shape, 0)
    half = WAVES // 2
    odd = (group == 0) & (row == half)
    wave = jnp.where(odd, GY // 2, group * half + (row & (half - 1)))
    turn = jnp.where((row < half) | odd, 0, -(GY // 4))
    return wave, turn

def turned(phase):
    phase = phase & (GY - 1)
    angle = (GY // 4 - jnp.abs(phase - GY // 2)).astype(jnp.float32) * (2.0 * math.pi / GY)
    square = angle * angle
    total = 1.0 / 6227020800.0
    for power in (39916800.0, 362880.0, 5040.0, 120.0, 6.0, 1.0):
        sign = -1.0 if power in (39916800.0, 5040.0, 6.0) else 1.0
        total = total * square + sign / power
    return -(angle * total)

def lines(cells, members, group):
    wave, turn = wave_of(group, (WAVES, cells.shape[1]))
    phase = wave * (cells - 1) + turn
    found = [0.0 for _ in members]
    for offset in range(4):
        cosine = turned(phase)
        found = [total + rows[offset] * cosine for total, rows in zip(found, members)]
        phase = phase + wave
    return found


def mesh_filter(total, filt):
    bead_count = lax.axis_size("bead")
    device = lax.axis_index("grid") * bead_count + lax.axis_index("bead")
    groups = GY // WAVES
    parts = lax.axis_size("grid") * bead_count // groups
    group = lax.rem(device, groups)
    part = lax.div(device, groups)
    reach = -1.0 / (2.0 * screen_width * screen_width)
    row = lax.broadcasted_iota(jnp.int32, (GX, GZ), 0)
    col = lax.broadcasted_iota(jnp.int32, (GX, GZ), 1)
    wx = jnp.where(row <= GX // 2, row, row - GX // 2)
    wz = jnp.where(col <= GZ // 2, col, col - GZ // 2)
    square = (wx * wx + wz * wz).astype(jnp.float32)
    times = jnp.where((wx & (GX // 2 - 1)) == 0, 1.0, 2.0) * jnp.where((wz & (GZ // 2 - 1)) == 0, 1.0, 2.0)
    if parts > 1:
        times = jnp.where(lax.div(col * parts, GZ) == part, times, 0.0)
    plain = times * jnp.exp(square * reach)
    filt[0] = plain
    filt[1] = square
    total[...] = jnp.zeros_like(total)


def mesh_phases(fields, tables, out, track, along, total, near, filt, ready, finished):
    domains = fields.shape[0]
    bead_count = lax.axis_size("bead")
    device = lax.axis_index("grid") * bead_count + lax.axis_index("bead")
    fx, fxt, rt, back = [tables.at[i] for i in range(4)]
    group = lax.rem(device, GY // WAVES)
    bins = GX // BIN
    cells_all = GX * WAVES
    halo = (WINDOW - BIN) * WAVES
    pack = 2
    packs = domains // pack
    unroll = min(4, packs)
    chunks = packs // unroll

    for d in range(domains) if domains <= 8 else ():
        for k, rows in enumerate(tracks(fields[d])):
            track[d, k] = rows
    if domains > 8:
        def fill(d, carry):
            for k, rows in enumerate(tracks(fields[d])):
                track[d, k] = rows
            return carry
        lax.fori_loop(0, domains, fill, 0)

    def rows_of(first, where, dim):
        def one(k):
            return jnp.concatenate(
                [track[first + i, k, dim:dim + 1, where] for i in range(pack)], axis=1
            )
        return one(0).astype(jnp.int32), [one(1 + k) for k in range(4)], [one(5 + k) for k in range(4)]

    def span(s):
        return pl.ds(pl.multiple_of(s * CAP, CAP), CAP)

    lanes = total.shape[2]
    tiles = total.shape[0]

    def load(rows):
        return jnp.concatenate([total[i, rows, :] for i in range(tiles)], axis=1)

    def store(rows, value):
        for i in range(tiles):
            total[i, rows, :] = value[:, i * lanes:(i + 1) * lanes]

    def spread(i, carry):
        for k in range(4):
            spread_bin(4 * i + k)
        return carry

    def spread_bin(step):
        s = step // chunks
        where = span(s)
        got = None
        for j in range(unroll):
            pair = (step % chunks) * unroll + j
            first = pair * pack
            cells, values, _ = rows_of(first, where, 1)
            x, = window(cells - s * BIN, [values])
            cells, values, slopes = rows_of(first, where, 2)
            y, yd = lines(cells, [values, slopes], group)
            along[pair, s, 0] = y
            along[pair, s, 1] = yd
            charge = jnp.concatenate([fields[first + i, 0:1, where] for i in range(pack)], axis=1)
            y = y * charge
            cells, values, _ = rows_of(first, where, 3)
            z, = stencil(cells, [values], GZ)
            rows = split(jnp.concatenate([x[i:i + 1] * y for i in range(WINDOW)], axis=0))
            more = dot3(rows, z, NT)
            got = more if got is None else got + more
        rows = pl.ds(pl.multiple_of(s * (BIN * WAVES), BIN * WAVES), WINDOW * WAVES)
        store(rows, load(rows) + got)

    lax.fori_loop(0, bins * chunks // 4, spread, 0)
    total[:, 0:halo, :] += total[:, cells_all:cells_all + halo, :]
    ready()

    chains = WAVES
    size = cells_all // chains

    def row_blocks(i):
        return [pl.ds(pl.multiple_of((i * chains + k) * size, size), size) for k in range(chains)]

    def forward(i, carry):
        at = row_blocks(i)
        got = [dot3(split(load(rows)), (rt[0], rt[1]), NN) for rows in at]
        for rows, each in zip(at, got):
            store(rows, each)
        return carry

    forward(0, 0)

    def middle(i, carry):
        at = [pl.ds(i * chains + k, GX, stride=WAVES) for k in range(chains)]
        got = [dot3((fx[0], fx[1]), split(load(rows)), NN) for rows in at]
        for k in range(chains):
            wave, _ = wave_of_row(group, i * chains + k)
            wave = jnp.full((1, GZ), wave, jnp.int32)
            wave_square = (wave * wave).astype(jnp.float32)
            count = jnp.where((wave & (GY // 2 - 1)) == 0, 1.0, 2.0)
            scale = count * jnp.exp(wave_square * (-1.0 / (2.0 * screen_width * screen_width)))
            scale = scale * (coulomb_scale / (GX * GY * GZ))
            m2 = filt[1] + wave_square
            got[k] = got[k] * jnp.where(m2 == 0.0, 0.0, filt[0] * scale / jnp.where(m2 == 0.0, 1.0, m2))
        got = [dot3((fxt[0], fxt[1]), split(each), NN) for each in got]
        for rows, each in zip(at, got):
            store(rows, each)
        return carry

    middle(0, 0)

    def inverse(i, carry):
        at = row_blocks(i)
        got = [dot3(split(load(rows)), (back[0], back[1]), NN) for rows in at]
        for rows, each in zip(at, got):
            high, low = split(each)
            near[0, rows, :] = high
            near[1, rows, :] = low
        return carry

    inverse(0, 0)
    near[:, cells_all:cells_all + halo, :] = near[:, 0:halo, :]

    half = min(8, bins)
    own_pack = lax.axis_index("grid") // pack

    def gather(step, carry):
        pair = lax.rem(own_pack + 1 + step // (bins // half), packs)
        first = pair * pack
        for j in range(half):
            s = (step % (bins // half)) * half + j
            where = span(s)
            rows = pl.ds(pl.multiple_of(s * (BIN * WAVES), BIN * WAVES), WINDOW * WAVES)
            field = (near[0, rows, :], near[1, rows, :])
            cells, values, slopes = rows_of(first, where, 1)
            x, xd = window(cells - s * BIN, [values, slopes])
            cells, values, slopes = rows_of(first, where, 3)
            z, zd = stencil(cells, [values, slopes], GZ)
            plain = dot3(field, z, NN)
            steep = dot3(field, zd, NN)
            f = [0.0, 0.0, 0.0]
            for i in range(WINDOW):
                q = plain[i * WAVES:(i + 1) * WAVES]
                f[0] = f[0] + q * xd[i:i + 1]
                f[1] = f[1] + q * x[i:i + 1]
                f[2] = f[2] + steep[i * WAVES:(i + 1) * WAVES] * x[i:i + 1]
            y, yd = along[pair, s, 0], along[pair, s, 1]
            f = [f[0] * y, f[1] * yd, f[2] * y]
            charge = jnp.concatenate([fields[first + i, 0:1, where] for i in range(pack)], axis=1)
            for c in range(3):
                force = -charge * jnp.sum(f[c], axis=0, keepdims=True)
                for i in range(pack):
                    out[first + i, c:c + 1, where] = force[:, i * CAP:(i + 1) * CAP]

        @pl.when(step % (bins // half) == bins // half - 1)
        def _():
            for i in range(pack):
                finished(first + i)

        return carry

    lax.fori_loop(0, packs * (bins // half), gather, 0)


def wave_of_row(group, row):
    half = WAVES // 2
    odd = (group == 0) & (row == half)
    wave = jnp.where(odd, GY // 2, group * half + (row & (half - 1)))
    return wave, odd


def wave_tables():
    table = real_waves(GX)
    shifted = np.roll(table, 1, axis=1)
    return jnp.stack([jnp.stack(split_table(t)) for t in (shifted, shifted.T, table.T, table)])


TILE = 128
highest = lax.Precision.HIGHEST
time_step = 0.5
polymer_frequency = 1.0
centroid_friction = 0.5
pair_strength = 1.0 / 128.0
pair_range = 4.0
MESH = pl.DeviceIdType.MESH


def everyone(act):
    grid_count, bead_count = lax.axis_size("grid"), lax.axis_size("bead")
    me = lax.axis_index("grid") * bead_count + lax.axis_index("bead")

    def one(step, carry):
        peer = lax.rem(me + step, grid_count * bead_count)
        act(lax.div(peer, bead_count), lax.rem(peer, bead_count))
        return carry

    lax.fori_loop(1, grid_count * bead_count, one, 0)
    return grid_count * bead_count - 1


def hail():
    barrier = pltpu.get_barrier_semaphore()

    def signal(g, b):
        pl.semaphore_signal(barrier, 1, device_id=(g, b), device_id_type=MESH)

    return everyone(signal)


def shares(name, source, target, send_sem, recv_sem):
    count = lax.axis_size(name)
    me = lax.axis_index(name)

    def copy(step, landing):
        peer = lax.rem(me + step, count)
        return pltpu.make_async_remote_copy(
            src_ref=source(peer),
            dst_ref=target(peer if landing else me),
            send_sem=send_sem.at[peer],
            recv_sem=recv_sem.at[peer if landing else me],
            device_id={name: peer},
            device_id_type=MESH,
        )

    def start():
        def one(step, carry):
            copy(step, False).start()
            return carry

        lax.fori_loop(1, count, one, 0)

    def wait():
        def one(step, carry):
            copy(step, True).wait_recv()
            return carry

        lax.fori_loop(1, count, one, 0)

    def drain():
        def one(step, carry):
            copy(step, False).wait_send()
            return carry

        lax.fori_loop(1, count, one, 0)

    return start, wait, drain


def split3(value):
    high = value.astype(jnp.bfloat16)
    rest = value - high.astype(jnp.float32)
    middle = rest.astype(jnp.bfloat16)
    return high, middle, (rest - middle.astype(jnp.float32)).astype(jnp.bfloat16)


def slots_of(route, per_bin):
    atoms = route.shape[1]
    bins = GX // BIN
    owner = lax.div(route, per_bin)
    bin_row = lax.broadcasted_iota(jnp.int32, (2 * bins, atoms), 0)
    mine = bin_row == owner
    before = lax.broadcasted_iota(jnp.int32, (atoms, atoms), 0)
    after = lax.broadcasted_iota(jnp.int32, (atoms, atoms), 1)
    earlier = jnp.where(before < after, 1.0, 0.0).astype(jnp.bfloat16)
    chosen = jnp.where(mine, 1.0, 0.0)
    rank = jnp.dot(chosen.astype(jnp.bfloat16), earlier, preferred_element_type=jnp.float32)
    rank = jnp.sum(chosen * rank, axis=0, keepdims=True)
    return owner * CAP + rank.astype(jnp.int32)


def placement(slot):
    spots = lax.broadcasted_iota(jnp.int32, (GX // BIN * CAP, slot.shape[1]), 0)
    return jnp.where(spots == slot, 1.0, 0.0).astype(jnp.bfloat16)


def pair_forces(weight_of, positions, momenta, kicked):
    beads, atoms = positions.shape[1:]
    tiles = atoms // TILE
    across = [positions[c].T for c in range(3)]

    def body(t, carry):
        where = pl.ds(pl.multiple_of(t * TILE, TILE), TILE)
        for b in range(beads):
            centre = [positions[c, b : b + 1, where] for c in range(3)]
            sums = [jnp.zeros((8, TILE), jnp.float32) for _ in range(3)]
            for m in range(tiles):
                apart = [
                    centre[c] - across[c][m * TILE : (m + 1) * TILE, b : b + 1] for c in range(3)
                ]
                square = apart[0] * apart[0] + apart[1] * apart[1] + apart[2] * apart[2]
                weight = jnp.exp(square * (-1.0 / pair_range))
                for c in range(3):
                    part = jnp.sum((weight * apart[c]).reshape(TILE // 8, 8, TILE), axis=0)
                    sums[c] = sums[c] + weight_of(t, m) * part
            for c in range(3):
                force = jnp.sum(sums[c], axis=0, keepdims=True)
                kicked[c, b : b + 1, where] = momenta[c, b : b + 1, where] + force
        return carry

    lax.fori_loop(0, tiles, body, 0)


def step_tables(bead_total):
    mode = np.arange(bead_total)
    angle = (mode[:, None] * mode[None, :] % bead_total) * (2.0 * math.pi / bead_total)
    middle = bead_total // 2
    scaled = math.sqrt(2.0 / bead_total)
    column = mode[:, None]
    matrix = np.where(
        column == 0,
        1.0 / math.sqrt(bead_total),
        np.where(
            column < middle,
            scaled * np.cos(angle),
            np.where(
                column == middle, np.cos(angle) / math.sqrt(bead_total), scaled * np.sin(angle)
            ),
        ),
    )
    half = 0.5 * time_step
    frequency = 2.0 * polymer_frequency * np.sin(mode * (math.pi / bead_total))
    cosine = np.cos(frequency * half)
    drift = np.where(mode == 0, half, np.sin(frequency * half) / np.where(mode == 0, 1.0, frequency))
    pull = frequency * np.sin(frequency * half)
    friction = np.where(mode == 0, centroid_friction, 2.0 * frequency)
    damping = np.exp(-friction * time_step)
    kick = np.sqrt(1.0 - damping * damping)
    factors = [
        [cosine * cosine - drift * damping * pull, drift * cosine * (1.0 + damping), drift * kick],
        [-cosine * pull * (1.0 + damping), cosine * damping * cosine - pull * drift, cosine * kick],
    ]
    tables = np.stack(
        [
            np.stack(
                [
                    matrix.T @ (row[0][:, None] * matrix),
                    matrix.T @ (row[1][:, None] * matrix),
                    matrix.T * row[2][None, :],
                ]
            )
            for row in factors
        ]
    )
    return tables.astype(np.float32), (float(factors[0][1][0]), float(factors[1][1][0]))


def step_kernel(
    planes, centre, neighbours, positions, momenta, noise, charges, route, cells, offsets, mixing, waves,
    drifted, force_q, force_p,
    own_momenta, own_charges, own_route, own_cells, own_offsets, own_mixing, own_waves,
    fields, sources, kicks, partial, landed, steps, track, along, total, near, filt,
    local_sem, field_send, field_recv, place_send, place_recv, noise_send, noise_recv,
    kick_send, kick_recv, part_send, part_recv,
):
    grid_rank = lax.axis_index("grid")
    bead_rank = lax.axis_index("bead")
    bead_count = lax.axis_size("bead")
    domains = partial.shape[0]
    beads = kicks.shape[2]

    others = hail()
    pairs = [
        (route, own_route), (charges, own_charges), (cells, own_cells), (offsets, own_offsets),
        (positions, sources.at[bead_rank, 0]), (momenta, own_momenta),
        (noise, sources.at[bead_rank, 1]), (mixing, own_mixing), (waves, own_waves),
    ]
    loads = [pltpu.make_async_copy(a, b, local_sem.at[i]) for i, (a, b) in enumerate(pairs)]
    for load in loads:
        load.start()
    for load in loads[0:4]:
        load.wait()

    rows = own_route[...]
    slot = slots_of(rows, BIN // planes)
    first = (rows * planes + own_cells[0:1]).astype(jnp.float32) + own_offsets[0:1]
    rest = own_cells[1:3].astype(jnp.float32) + own_offsets[1:3]
    own = jnp.concatenate([own_charges[...], first, rest], axis=0)
    halves = [each.astype(jnp.float32) for each in split3(own)]
    packed = jnp.concatenate(halves + [jnp.zeros_like(own)], axis=0).astype(jnp.bfloat16)
    got = lax.dot_general(packed, placement(slot), (NT, ((), ())), preferred_element_type=jnp.float32)
    fields[grid_rank] = (got[0:4] + got[4:8]) + got[8:12]

    pl.semaphore_wait(pltpu.get_barrier_semaphore(), others)
    field = shares("grid", lambda p: fields.at[grid_rank], lambda p: fields.at[p], field_send, field_recv)
    place = shares("bead", lambda p: positions, lambda p: sources.at[p, 0], place_send, place_recv)
    draw = shares("bead", lambda p: noise, lambda p: sources.at[p, 1], noise_send, noise_recv)
    kick = shares("bead", lambda p: kicks.at[bead_rank], lambda p: kicks.at[p], kick_send, kick_recv)

    def part(g, b, landing=False):
        return pltpu.make_async_remote_copy(
            src_ref=partial.at[g],
            dst_ref=landed.at[g, b] if landing else landed.at[grid_rank, bead_rank],
            send_sem=part_send.at[g, b],
            recv_sem=part_recv.at[g, b] if landing else part_recv.at[grid_rank, bead_rank],
            device_id=(g, b),
            device_id_type=MESH,
        )

    for each in (field, place, draw):
        each[0]()

    mesh_filter(total, filt)

    def weight_of(t, m):
        total = 0.0
        for k in range(neighbours.shape[1]):
            total += jnp.where(neighbours[t, k] == m, 0.5 * time_step * pair_strength, 0.0)
        return total

    loads[4].wait()
    loads[5].wait()
    pair_forces(weight_of, sources.at[bead_rank, 0], own_momenta, kicks.at[bead_rank])
    kick[0]()
    field[1]()

    def finished(d):
        for k in range(bead_count):
            mate = lax.rem(bead_rank + 1 + k, bead_count)

            @pl.when((d != grid_rank) | (mate != bead_rank))
            def _():
                part(d, mate).start()

    mesh_phases(
        fields, own_waves, partial, track, along, total, near, filt, loads[8].wait, finished
    )

    landed[grid_rank, bead_rank] = partial[grid_rank]
    where = placement(slot)
    for each in (place, draw, kick):
        each[1]()
    loads[6].wait()
    loads[7].wait()
    mix = own_mixing[bead_rank]

    def stepped(c):
        parts = [sources[k, 0, c] for k in range(bead_count)]
        parts += [kicks[k, c] for k in range(bead_count)]
        parts += [sources[k, 1, c] for k in range(bead_count)]
        got = jnp.dot(mix, jnp.concatenate(parts, axis=0), precision=highest, preferred_element_type=jnp.float32)
        steps[0, c] = got[0:beads]
        steps[1, c] = got[beads:]

    for component in range(3):
        stepped(component)
    leave = pltpu.make_async_copy(steps, drifted, local_sem.at[len(pairs)])
    leave.start()
    everyone(lambda g, b: part(g, b, True).wait_recv())
    forces = jnp.zeros(partial.shape[1:], jnp.float32)
    if domains <= 8:
        for d in range(domains):
            for k in range(bead_count):
                forces = forces + landed[d, k]
    else:
        def add(d, forces):
            for k in range(bead_count):
                forces = forces + landed[d, k]
            return forces
        forces = lax.fori_loop(0, domains, add, forces)
    halves = [each.astype(jnp.float32) for each in split3(forces)]
    packed = jnp.concatenate(halves + [jnp.zeros((16 - 9, forces.shape[1]), jnp.float32)], axis=0)
    got = jnp.dot(packed.astype(jnp.bfloat16), where, preferred_element_type=jnp.float32)
    force = (got[0:3] + got[3:6]) + got[6:9]
    force_q[...] = centre[0] * force
    force_p[...] = centre[1] * force
    leave.wait()
    for each in (field, place, draw, kick):
        each[2]()
    everyone(lambda g, b: part(g, b).wait_send())


def per_device(positions, momenta, noise, charges, slab_route, cells, offsets, nbr_tiles):
    grid_count = lax.axis_size("grid")
    bead_count = lax.axis_size("bead")
    beads, atoms = positions.shape[1:]
    slots = GX // BIN * CAP
    tables, centre = step_tables(beads * bead_count)
    shaped = tables.reshape(2, 3, bead_count, beads, -1).transpose(2, 0, 3, 1, 4)
    shaped = jnp.asarray(shaped.reshape(bead_count, 2 * beads, -1))
    centre = tuple(0.5 * time_step * value for value in centre)
    waves = wave_tables()
    vmem = pl.BlockSpec(memory_space=pltpu.VMEM)
    anywhere = pl.BlockSpec(memory_space=pl.ANY)
    dma = pltpu.SemaphoreType.DMA
    whole = lambda array: pltpu.VMEM(array.shape, array.dtype)
    f32 = lambda *shape: pltpu.VMEM(shape, jnp.float32)
    charges = charges.reshape(1, atoms)
    slab_route = slab_route.reshape(1, atoms)
    drifted, *force = pl.pallas_call(
        functools.partial(step_kernel, GX // grid_count, centre),
        out_shape=[
            jax.ShapeDtypeStruct((2, *positions.shape), jnp.float32),
            jax.ShapeDtypeStruct((3, atoms), jnp.float32),
            jax.ShapeDtypeStruct((3, atoms), jnp.float32),
        ],
        in_specs=[pl.BlockSpec(memory_space=pltpu.SMEM)] + [anywhere] * 9,
        out_specs=[anywhere, vmem, vmem],
        scratch_shapes=[
            whole(momenta), whole(charges), whole(slab_route), whole(cells), whole(offsets),
            whole(shaped), whole(waves),
            f32(grid_count, 4, slots),
            f32(bead_count, 2, *positions.shape),
            f32(bead_count, *positions.shape),
            f32(grid_count, 3, slots),
            f32(grid_count, bead_count, 3, slots),
            f32(2, *positions.shape),
            f32(grid_count, 9, 4, slots),
            f32(grid_count // 2, GX // BIN, 2, WAVES, 2 * CAP),
            f32(GZ // 128, (GX + WINDOW - BIN) * WAVES, 128),
            pltpu.VMEM((2, (GX + WINDOW - BIN) * WAVES, GZ), jnp.bfloat16),
            f32(2, GX, GZ),
            dma((10,)),
            dma((grid_count,)), dma((grid_count,)),
            *[dma((bead_count,)) for _ in range(6)],
            dma((grid_count, bead_count)), dma((grid_count, bead_count)),
        ],
        compiler_params=pltpu.CompilerParams(
            collective_id=0, has_side_effects=True, vmem_limit_bytes=60 * 1024 * 1024
        ),
    )(nbr_tiles, positions, momenta, noise, charges, slab_route, cells, offsets, shaped, waves)
    return tuple(drifted[i] + force[i][:, None, :] for i in range(2))


def solution(mesh):
    in_specs = (
        P(None, "bead", "grid"),
        P(None, "bead", "grid"),
        P(None, "bead", "grid"),
        P("grid"),
        P("grid", None),
        P(None, "grid"),
        P(None, "grid"),
        P("grid", None),
    )
    out_specs = (P(None, "bead", "grid"), P(None, "bead", "grid"))

    def step(*args):
        return tuple(per_device(*args))

    return jax.shard_map(step, mesh=mesh, in_specs=in_specs, out_specs=out_specs, check_vma=False)
```

```python
import functools
import math

import jax
import jax.numpy as jnp
import numpy as np
from jax import lax
from jax.experimental import pallas as pl
from jax.experimental.pallas import tpu as pltpu
from jax.sharding import PartitionSpec as P

GX = GY = GZ = 256
WAVES = 8
BIN = 32
WINDOW = 36
CAP = 128
PACK = 2
coulomb_scale = 100000.0
screen_width = 200.0

def spline(fraction):
    remain = 1.0 - fraction
    square = fraction * fraction
    cubic = square * fraction
    values = [
        remain * remain * remain / 6.0,
        (3.0 * cubic - 6.0 * square + 4.0) / 6.0,
        (-3.0 * cubic + 3.0 * square + 3.0 * fraction + 1.0) / 6.0,
        cubic / 6.0,
    ]
    slopes = [
        -0.5 * remain * remain,
        0.5 * (3.0 * square - 4.0 * fraction),
        0.5 * (-3.0 * square + 2.0 * fraction + 1.0),
        0.5 * square,
    ]
    return (values, slopes)

def real_waves(length):
    half = length // 2
    row = np.arange(length)
    wave = np.where(row <= half, row, row - half)
    angle = (wave[:, None] * np.arange(length)[None, :] % length) * (2.0 * math.pi / length)
    return np.where((row <= half)[:, None], np.cos(angle), np.sin(angle))

def split_table(table):
    high = table.astype(jnp.bfloat16)
    low = (table - high.astype(np.float64)).astype(jnp.bfloat16)
    return high, low

def split(value):
    high = value.astype(jnp.bfloat16)
    low = (value - high.astype(jnp.float32)).astype(jnp.bfloat16)
    return high, low

NN = ((1,), (0,))
NT = ((1,), (1,))

def dot3(left, right, dims):
    def one(a, b):
        return lax.dot_general(a, b, (dims, ((), ())), preferred_element_type=jnp.float32)
    return one(left[0], right[0]) + (one(left[0], right[1]) + one(left[1], right[0]))

def tracks(fields):
    lowest = jnp.floor(fields)
    values, slopes = spline(fields - lowest)
    return [lowest, *values, *slopes]


def stencil(cells, members, length):
    row = lax.broadcasted_iota(jnp.int32, (length, cells.shape[1]), 0).astype(jnp.int16)
    hits = []
    for offset in range(4):
        cell = ((cells + (offset - 1)) & (length - 1)).astype(jnp.int16)
        hits.append(row == cell)

    def dense(rows):
        out = jnp.zeros(row.shape, jnp.bfloat16)
        for offset in range(4):
            out = jnp.where(hits[offset], rows[offset], out)
        return out

    found = []
    for rows in members:
        halves = [split(each) for each in rows]
        found.append((dense([half[0] for half in halves]), dense([half[1] for half in halves])))
    return found


def window(cells, members):
    row = lax.broadcasted_iota(jnp.int32, (WINDOW, cells.shape[1]), 0)
    hits = [row == cells + offset for offset in range(4)]

    def dense(rows):
        out = jnp.zeros(row.shape, jnp.float32)
        for offset in range(4):
            out = jnp.where(hits[offset], rows[offset], out)
        return out

    return [dense(rows) for rows in members]


def wave_of(group, shape):
    row = lax.broadcasted_iota(jnp.int32, shape, 0)
    half = WAVES // 2
    odd = (group == 0) & (row == half)
    wave = jnp.where(odd, GY // 2, group * half + (row & (half - 1)))
    turn = jnp.where((row < half) | odd, 0, -(GY // 4))
    return wave, turn

def turned(phase):
    phase = phase & (GY - 1)
    angle = (GY // 4 - jnp.abs(phase - GY // 2)).astype(jnp.float32) * (2.0 * math.pi / GY)
    square = angle * angle
    total = 1.0 / 6227020800.0
    for power in (39916800.0, 362880.0, 5040.0, 120.0, 6.0, 1.0):
        sign = -1.0 if power in (39916800.0, 5040.0, 6.0) else 1.0
        total = total * square + sign / power
    return -(angle * total)

def lines(cells, members, group):
    wave, turn = wave_of(group, (WAVES, cells.shape[1]))
    phase = wave * (cells - 1) + turn
    found = [0.0 for _ in members]
    for offset in range(4):
        cosine = turned(phase)
        found = [total + rows[offset] * cosine for total, rows in zip(found, members)]
        phase = phase + wave
    return found


def mesh_filter(total, filt):
    bead_count = lax.axis_size("bead")
    device = lax.axis_index("grid") * bead_count + lax.axis_index("bead")
    groups = GY // WAVES
    parts = lax.axis_size("grid") * bead_count // groups
    group = lax.rem(device, groups)
    part = lax.div(device, groups)
    reach = -1.0 / (2.0 * screen_width * screen_width)
    row = lax.broadcasted_iota(jnp.int32, (GX, GZ), 0)
    col = lax.broadcasted_iota(jnp.int32, (GX, GZ), 1)
    wx = jnp.where(row <= GX // 2, row, row - GX // 2)
    wz = jnp.where(col <= GZ // 2, col, col - GZ // 2)
    square = (wx * wx + wz * wz).astype(jnp.float32)
    times = jnp.where((wx & (GX // 2 - 1)) == 0, 1.0, 2.0) * jnp.where((wz & (GZ // 2 - 1)) == 0, 1.0, 2.0)
    if parts > 1:
        times = jnp.where(lax.div(col * parts, GZ) == part, times, 0.0)
    plain = times * jnp.exp(square * reach)
    filt[0] = plain
    filt[1] = square
    total[...] = jnp.zeros_like(total)


def mesh_phases(fields, tables, out, track, along, total, near, filt, ready, finished):
    domains = fields.shape[0]
    bead_count = lax.axis_size("bead")
    device = lax.axis_index("grid") * bead_count + lax.axis_index("bead")
    fx, fxt, rt, back = [tables.at[i] for i in range(4)]
    group = lax.rem(device, GY // WAVES)
    bins = GX // BIN
    cells_all = GX * WAVES
    halo = (WINDOW - BIN) * WAVES
    pack = PACK
    packs = domains // pack
    unroll = min(4, packs)
    chunks = packs // unroll

    for d in range(domains) if domains <= 8 else ():
        for k, rows in enumerate(tracks(fields[d])):
            track[d, k] = rows
    if domains > 8:
        def fill(d, carry):
            for k, rows in enumerate(tracks(fields[d])):
                track[d, k] = rows
            return carry
        lax.fori_loop(0, domains, fill, 0)

    def rows_of(first, where, dim):
        def one(k):
            return jnp.concatenate(
                [track[first + i, k, dim:dim + 1, where] for i in range(pack)], axis=1
            )
        return one(0).astype(jnp.int32), [one(1 + k) for k in range(4)], [one(5 + k) for k in range(4)]

    def span(s):
        return pl.ds(pl.multiple_of(s * CAP, CAP), CAP)

    lanes = total.shape[2]
    tiles = total.shape[0]

    def load(rows):
        return jnp.concatenate([total[i, rows, :] for i in range(tiles)], axis=1)

    def store(rows, value):
        for i in range(tiles):
            total[i, rows, :] = value[:, i * lanes:(i + 1) * lanes]

    def spread(i, carry):
        for k in range(4):
            spread_bin(4 * i + k)
        return carry

    def spread_bin(step):
        s = step // chunks
        where = span(s)
        got = None
        for j in range(unroll):
            pair = (step % chunks) * unroll + j
            first = pair * pack
            cells, values, _ = rows_of(first, where, 1)
            x, = window(cells - s * BIN, [values])
            cells, values, slopes = rows_of(first, where, 2)
            y, yd = lines(cells, [values, slopes], group)
            along[pair, s, 0] = y
            along[pair, s, 1] = yd
            charge = jnp.concatenate([fields[first + i, 0:1, where] for i in range(pack)], axis=1)
            y = y * charge
            cells, values, _ = rows_of(first, where, 3)
            z, = stencil(cells, [values], GZ)
            rows = split(jnp.concatenate([x[i:i + 1] * y for i in range(WINDOW)], axis=0))
            more = dot3(rows, z, NT)
            got = more if got is None else got + more
        rows = pl.ds(pl.multiple_of(s * (BIN * WAVES), BIN * WAVES), WINDOW * WAVES)
        store(rows, load(rows) + got)

    lax.fori_loop(0, bins * chunks // 4, spread, 0)
    total[:, 0:halo, :] += total[:, cells_all:cells_all + halo, :]
    ready()

    chains = WAVES
    size = cells_all // chains

    def row_blocks(i):
        return [pl.ds(pl.multiple_of((i * chains + k) * size, size), size) for k in range(chains)]

    def forward(i, carry):
        at = row_blocks(i)
        got = [dot3(split(load(rows)), (rt[0], rt[1]), NN) for rows in at]
        for rows, each in zip(at, got):
            store(rows, each)
        return carry

    forward(0, 0)

    def middle(i, carry):
        at = [pl.ds(i * chains + k, GX, stride=WAVES) for k in range(chains)]
        got = [dot3((fx[0], fx[1]), split(load(rows)), NN) for rows in at]
        for k in range(chains):
            wave, _ = wave_of_row(group, i * chains + k)
            wave = jnp.full((1, GZ), wave, jnp.int32)
            wave_square = (wave * wave).astype(jnp.float32)
            count = jnp.where((wave & (GY // 2 - 1)) == 0, 1.0, 2.0)
            scale = count * jnp.exp(wave_square * (-1.0 / (2.0 * screen_width * screen_width)))
            scale = scale * (coulomb_scale / (GX * GY * GZ))
            m2 = filt[1] + wave_square
            got[k] = got[k] * jnp.where(m2 == 0.0, 0.0, filt[0] * scale / jnp.where(m2 == 0.0, 1.0, m2))
        got = [dot3((fxt[0], fxt[1]), split(each), NN) for each in got]
        for rows, each in zip(at, got):
            store(rows, each)
        return carry

    middle(0, 0)

    def inverse(i, carry):
        at = row_blocks(i)
        got = [dot3(split(load(rows)), (back[0], back[1]), NN) for rows in at]
        for rows, each in zip(at, got):
            high, low = split(each)
            near[0, rows, :] = high
            near[1, rows, :] = low
        return carry

    inverse(0, 0)
    near[:, cells_all:cells_all + halo, :] = near[:, 0:halo, :]

    half = min(8, bins)
    own_pack = lax.axis_index("grid") // pack

    def gather(step, carry):
        pair = lax.rem(own_pack + 1 + step // (bins // half), packs)
        first = pair * pack
        for j in range(half):
            s = (step % (bins // half)) * half + j
            where = span(s)
            rows = pl.ds(pl.multiple_of(s * (BIN * WAVES), BIN * WAVES), WINDOW * WAVES)
            field = (near[0, rows, :], near[1, rows, :])
            cells, values, slopes = rows_of(first, where, 1)
            x, xd = window(cells - s * BIN, [values, slopes])
            cells, values, slopes = rows_of(first, where, 3)
            z, zd = stencil(cells, [values, slopes], GZ)
            plain = dot3(field, z, NN)
            steep = dot3(field, zd, NN)
            f = [0.0, 0.0, 0.0]
            for i in range(WINDOW):
                q = plain[i * WAVES:(i + 1) * WAVES]
                f[0] = f[0] + q * xd[i:i + 1]
                f[1] = f[1] + q * x[i:i + 1]
                f[2] = f[2] + steep[i * WAVES:(i + 1) * WAVES] * x[i:i + 1]
            y, yd = along[pair, s, 0], along[pair, s, 1]
            f = [f[0] * y, f[1] * yd, f[2] * y]
            charge = jnp.concatenate([fields[first + i, 0:1, where] for i in range(pack)], axis=1)
            for c in range(3):
                force = -charge * jnp.sum(f[c], axis=0, keepdims=True)
                for i in range(pack):
                    out[first + i, pl.ds(c * bins + s, 1), :] = force[:, i * CAP:(i + 1) * CAP]

        @pl.when(step % (bins // half) == bins // half - 1)
        def _():
            finished(pair)

        return carry

    lax.fori_loop(0, packs * (bins // half), gather, 0)


def wave_of_row(group, row):
    half = WAVES // 2
    odd = (group == 0) & (row == half)
    wave = jnp.where(odd, GY // 2, group * half + (row & (half - 1)))
    return wave, odd


def wave_tables():
    table = real_waves(GX)
    shifted = np.roll(table, 1, axis=1)
    return jnp.stack([jnp.stack(split_table(t)) for t in (shifted, shifted.T, table.T, table)])


TILE = 128
highest = lax.Precision.HIGHEST
time_step = 0.5
polymer_frequency = 1.0
centroid_friction = 0.5
pair_strength = 1.0 / 128.0
pair_range = 4.0
MESH = pl.DeviceIdType.MESH


def everyone(act):
    grid_count, bead_count = lax.axis_size("grid"), lax.axis_size("bead")
    me = lax.axis_index("grid") * bead_count + lax.axis_index("bead")

    def one(step, carry):
        peer = lax.rem(me + step, grid_count * bead_count)
        act(lax.div(peer, bead_count), lax.rem(peer, bead_count))
        return carry

    lax.fori_loop(1, grid_count * bead_count, one, 0)
    return grid_count * bead_count - 1


def hail():
    barrier = pltpu.get_barrier_semaphore()

    def signal(g, b):
        pl.semaphore_signal(barrier, 1, device_id=(g, b), device_id_type=MESH)

    return everyone(signal)


def shares(name, source, target, send_sem, recv_sem):
    count = lax.axis_size(name)
    me = lax.axis_index(name)

    def copy(step, landing):
        peer = lax.rem(me + step, count)
        return pltpu.make_async_remote_copy(
            src_ref=source(peer),
            dst_ref=target(peer if landing else me),
            send_sem=send_sem.at[peer],
            recv_sem=recv_sem.at[peer if landing else me],
            device_id={name: peer},
            device_id_type=MESH,
        )

    def start():
        def one(step, carry):
            copy(step, False).start()
            return carry

        lax.fori_loop(1, count, one, 0)

    def wait():
        def one(step, carry):
            copy(step, True).wait_recv()
            return carry

        lax.fori_loop(1, count, one, 0)

    def drain():
        def one(step, carry):
            copy(step, False).wait_send()
            return carry

        lax.fori_loop(1, count, one, 0)

    return start, wait, drain


def split3(value):
    high = value.astype(jnp.bfloat16)
    rest = value - high.astype(jnp.float32)
    middle = rest.astype(jnp.bfloat16)
    return high, middle, (rest - middle.astype(jnp.float32)).astype(jnp.bfloat16)


def slots_of(route, per_bin):
    atoms = route.shape[1]
    bins = GX // BIN
    owner = lax.div(route, per_bin)
    bin_row = lax.broadcasted_iota(jnp.int32, (2 * bins, atoms), 0)
    mine = bin_row == owner
    before = lax.broadcasted_iota(jnp.int32, (atoms, atoms), 0)
    after = lax.broadcasted_iota(jnp.int32, (atoms, atoms), 1)
    earlier = jnp.where(before < after, 1.0, 0.0).astype(jnp.bfloat16)
    chosen = jnp.where(mine, 1.0, 0.0)
    rank = jnp.dot(chosen.astype(jnp.bfloat16), earlier, preferred_element_type=jnp.float32)
    rank = jnp.sum(chosen * rank, axis=0, keepdims=True)
    return owner * CAP + rank.astype(jnp.int32)


def placement(slot):
    spots = lax.broadcasted_iota(jnp.int32, (GX // BIN * CAP, slot.shape[1]), 0)
    return jnp.where(spots == slot, 1.0, 0.0).astype(jnp.bfloat16)


def pair_forces(weight_of, positions, momenta, kicked):
    beads, atoms = positions.shape[1:]
    tiles = atoms // TILE
    across = [positions[c].T for c in range(3)]

    def body(t, carry):
        where = pl.ds(pl.multiple_of(t * TILE, TILE), TILE)
        for b in range(beads):
            centre = [positions[c, b : b + 1, where] for c in range(3)]
            sums = [jnp.zeros((8, TILE), jnp.float32) for _ in range(3)]
            for m in range(tiles):
                apart = [
                    centre[c] - across[c][m * TILE : (m + 1) * TILE, b : b + 1] for c in range(3)
                ]
                square = apart[0] * apart[0] + apart[1] * apart[1] + apart[2] * apart[2]
                weight = jnp.exp(square * (-1.0 / pair_range))
                for c in range(3):
                    part = jnp.sum((weight * apart[c]).reshape(TILE // 8, 8, TILE), axis=0)
                    sums[c] = sums[c] + weight_of(t, m) * part
            for c in range(3):
                force = jnp.sum(sums[c], axis=0, keepdims=True)
                kicked[c, b : b + 1, where] = momenta[c, b : b + 1, where] + force
        return carry

    lax.fori_loop(0, tiles, body, 0)


def step_tables(bead_total):
    mode = np.arange(bead_total)
    angle = (mode[:, None] * mode[None, :] % bead_total) * (2.0 * math.pi / bead_total)
    middle = bead_total // 2
    scaled = math.sqrt(2.0 / bead_total)
    column = mode[:, None]
    matrix = np.where(
        column == 0,
        1.0 / math.sqrt(bead_total),
        np.where(
            column < middle,
            scaled * np.cos(angle),
            np.where(
                column == middle, np.cos(angle) / math.sqrt(bead_total), scaled * np.sin(angle)
            ),
        ),
    )
    half = 0.5 * time_step
    frequency = 2.0 * polymer_frequency * np.sin(mode * (math.pi / bead_total))
    cosine = np.cos(frequency * half)
    drift = np.where(mode == 0, half, np.sin(frequency * half) / np.where(mode == 0, 1.0, frequency))
    pull = frequency * np.sin(frequency * half)
    friction = np.where(mode == 0, centroid_friction, 2.0 * frequency)
    damping = np.exp(-friction * time_step)
    kick = np.sqrt(1.0 - damping * damping)
    factors = [
        [cosine * cosine - drift * damping * pull, drift * cosine * (1.0 + damping), drift * kick],
        [-cosine * pull * (1.0 + damping), cosine * damping * cosine - pull * drift, cosine * kick],
    ]
    tables = np.stack(
        [
            np.stack(
                [
                    matrix.T @ (row[0][:, None] * matrix),
                    matrix.T @ (row[1][:, None] * matrix),
                    matrix.T * row[2][None, :],
                ]
            )
            for row in factors
        ]
    )
    return tables.astype(np.float32), (float(factors[0][1][0]), float(factors[1][1][0]))


def step_kernel(
    planes, centre, neighbours, positions, momenta, noise, charges, route, cells, offsets, mixing, waves,
    drifted, force_q, force_p,
    own_momenta, own_charges, own_route, own_cells, own_offsets, own_mixing, own_waves,
    fields, sources, kicks, partial, landed, mates, level, last, steps, track, along, total, near, filt,
    local_sem, field_send, field_recv, place_send, place_recv, noise_send, noise_recv,
    kick_send, kick_recv, part_send, part_recv, mate_send, mate_recv, last_send, last_recv,
):
    grid_rank = lax.axis_index("grid")
    bead_rank = lax.axis_index("bead")
    bead_count = lax.axis_size("bead")
    domains = partial.shape[0]
    beads = kicks.shape[2]

    others = hail()
    pairs = [
        (route, own_route), (charges, own_charges), (cells, own_cells), (offsets, own_offsets),
        (positions, sources.at[bead_rank, 0]), (momenta, own_momenta),
        (noise, sources.at[bead_rank, 1]), (mixing, own_mixing), (waves, own_waves),
    ]
    loads = [pltpu.make_async_copy(a, b, local_sem.at[i]) for i, (a, b) in enumerate(pairs)]
    for load in loads:
        load.start()
    for load in loads[0:4]:
        load.wait()

    rows = own_route[...]
    slot = slots_of(rows, BIN // planes)
    first = (rows * planes + own_cells[0:1]).astype(jnp.float32) + own_offsets[0:1]
    rest = own_cells[1:3].astype(jnp.float32) + own_offsets[1:3]
    own = jnp.concatenate([own_charges[...], first, rest], axis=0)
    halves = [each.astype(jnp.float32) for each in split3(own)]
    packed = jnp.concatenate(halves + [jnp.zeros_like(own)], axis=0).astype(jnp.bfloat16)
    got = lax.dot_general(packed, placement(slot), (NT, ((), ())), preferred_element_type=jnp.float32)
    fields[grid_rank] = (got[0:4] + got[4:8]) + got[8:12]

    pl.semaphore_wait(pltpu.get_barrier_semaphore(), others)
    field = shares("grid", lambda p: fields.at[grid_rank], lambda p: fields.at[p], field_send, field_recv)
    place = shares("bead", lambda p: positions, lambda p: sources.at[p, 0], place_send, place_recv)
    draw = shares("bead", lambda p: noise, lambda p: sources.at[p, 1], noise_send, noise_recv)
    kick = shares("bead", lambda p: kicks.at[bead_rank], lambda p: kicks.at[p], kick_send, kick_recv)
    summed = shares("bead", lambda p: level, lambda p: last.at[p], last_send, last_recv)
    own_pack = lax.div(grid_rank, PACK)
    place_in = lax.rem(grid_rank, PACK)

    def far(g, landing=False):
        return pltpu.make_async_remote_copy(
            src_ref=partial.at[g],
            dst_ref=landed.at[g if landing else grid_rank],
            send_sem=part_send.at[g],
            recv_sem=part_recv.at[g if landing else grid_rank],
            device_id={"grid": g},
            device_id_type=MESH,
        )

    def close(step, landing=False):
        peer = lax.rem(place_in * bead_count + bead_rank + step, PACK * bead_count)
        i, b = lax.div(peer, bead_count), lax.rem(peer, bead_count)
        at = (i, b) if landing else (place_in, bead_rank)
        return pltpu.make_async_remote_copy(
            src_ref=partial.at[own_pack * PACK + i],
            dst_ref=mates.at[at],
            send_sem=mate_send.at[i, b],
            recv_sem=mate_recv.at[at],
            device_id=(own_pack * PACK + i, b),
            device_id_type=MESH,
        )

    def each_far(act):
        def one(step, carry):
            act(lax.rem((own_pack + 1) * PACK + step, domains))
            return carry

        lax.fori_loop(0, domains - PACK, one, 0)

    def each_close(act):
        def one(step, carry):
            act(step)
            return carry

        lax.fori_loop(1, PACK * bead_count, one, 0)

    for each in (field, place, draw):
        each[0]()

    mesh_filter(total, filt)

    def weight_of(t, m):
        total = 0.0
        for k in range(neighbours.shape[1]):
            total += jnp.where(neighbours[t, k] == m, 0.5 * time_step * pair_strength, 0.0)
        return total

    loads[4].wait()
    loads[5].wait()
    pair_forces(weight_of, sources.at[bead_rank, 0], own_momenta, kicks.at[bead_rank])
    kick[0]()
    field[1]()

    def finished(pair):
        @pl.when(pair != own_pack)
        def _():
            for i in range(PACK):
                far(pair * PACK + i).start()

        @pl.when(pair == own_pack)
        def _():
            each_close(lambda step: close(step).start())

    mesh_phases(
        fields, own_waves, partial, track, along, total, near, filt, loads[8].wait, finished
    )

    mates[place_in, bead_rank] = partial[grid_rank]
    each_far(lambda g: far(g, True).wait_recv())

    def add(step, forces):
        return forces + landed[lax.rem((own_pack + 1) * PACK + step, domains)]

    level[...] = lax.fori_loop(0, domains - PACK, add, jnp.zeros(level.shape, jnp.float32))
    summed[0]()
    where = placement(slot)
    for each in (place, draw, kick):
        each[1]()
    loads[6].wait()
    loads[7].wait()
    mix = own_mixing[bead_rank]

    def stepped(c):
        parts = [sources[k, 0, c] for k in range(bead_count)]
        parts += [kicks[k, c] for k in range(bead_count)]
        parts += [sources[k, 1, c] for k in range(bead_count)]
        got = jnp.dot(mix, jnp.concatenate(parts, axis=0), precision=highest, preferred_element_type=jnp.float32)
        steps[0, c] = got[0:beads]
        steps[1, c] = got[beads:]

    for component in range(3):
        stepped(component)
    leave = pltpu.make_async_copy(steps, drifted, local_sem.at[len(pairs)])
    leave.start()
    each_close(lambda step: close(step, True).wait_recv())
    forces = level[...]
    for k in range(bead_count):
        for i in range(PACK):
            forces = forces + mates[i, k]
    summed[1]()
    last[bead_rank] = jnp.zeros(level.shape, jnp.float32)
    for k in range(bead_count):
        forces = forces + last[k]
    bins = GX // BIN
    forces = jnp.concatenate(
        [
            jnp.concatenate([forces[c * bins + s : c * bins + s + 1] for s in range(bins)], axis=1)
            for c in range(3)
        ],
        axis=0,
    )
    halves = [each.astype(jnp.float32) for each in split3(forces)]
    packed = jnp.concatenate(halves + [jnp.zeros((16 - 9, forces.shape[1]), jnp.float32)], axis=0)
    got = jnp.dot(packed.astype(jnp.bfloat16), where, preferred_element_type=jnp.float32)
    force = (got[0:3] + got[3:6]) + got[6:9]
    force_q[...] = centre[0] * force
    force_p[...] = centre[1] * force
    leave.wait()
    for each in (field, place, draw, kick, summed):
        each[2]()
    each_far(lambda g: far(g).wait_send())
    each_close(lambda step: close(step).wait_send())


def per_device(positions, momenta, noise, charges, slab_route, cells, offsets, nbr_tiles):
    grid_count = lax.axis_size("grid")
    bead_count = lax.axis_size("bead")
    beads, atoms = positions.shape[1:]
    slots = GX // BIN * CAP
    sheet = (3 * (GX // BIN), CAP)
    tables, centre = step_tables(beads * bead_count)
    shaped = tables.reshape(2, 3, bead_count, beads, -1).transpose(2, 0, 3, 1, 4)
    shaped = jnp.asarray(shaped.reshape(bead_count, 2 * beads, -1))
    centre = tuple(0.5 * time_step * value for value in centre)
    waves = wave_tables()
    vmem = pl.BlockSpec(memory_space=pltpu.VMEM)
    anywhere = pl.BlockSpec(memory_space=pl.ANY)
    dma = pltpu.SemaphoreType.DMA
    whole = lambda array: pltpu.VMEM(array.shape, array.dtype)
    f32 = lambda *shape: pltpu.VMEM(shape, jnp.float32)
    charges = charges.reshape(1, atoms)
    slab_route = slab_route.reshape(1, atoms)
    drifted, *force = pl.pallas_call(
        functools.partial(step_kernel, GX // grid_count, centre),
        out_shape=[
            jax.ShapeDtypeStruct((2, *positions.shape), jnp.float32),
            jax.ShapeDtypeStruct((3, atoms), jnp.float32),
            jax.ShapeDtypeStruct((3, atoms), jnp.float32),
        ],
        in_specs=[pl.BlockSpec(memory_space=pltpu.SMEM)] + [anywhere] * 9,
        out_specs=[anywhere, vmem, vmem],
        scratch_shapes=[
            whole(momenta), whole(charges), whole(slab_route), whole(cells), whole(offsets),
            whole(shaped), whole(waves),
            f32(grid_count, 4, slots),
            f32(bead_count, 2, *positions.shape),
            f32(bead_count, *positions.shape),
            f32(grid_count, *sheet),
            f32(grid_count, *sheet),
            f32(PACK, bead_count, *sheet),
            f32(*sheet),
            f32(bead_count, *sheet),
            f32(2, *positions.shape),
            f32(grid_count, 9, 4, slots),
            f32(grid_count // 2, GX // BIN, 2, WAVES, 2 * CAP),
            f32(GZ // 128, (GX + WINDOW - BIN) * WAVES, 128),
            pltpu.VMEM((2, (GX + WINDOW - BIN) * WAVES, GZ), jnp.bfloat16),
            f32(2, GX, GZ),
            dma((10,)),
            dma((grid_count,)), dma((grid_count,)),
            *[dma((bead_count,)) for _ in range(6)],
            dma((grid_count,)), dma((grid_count,)),
            dma((PACK, bead_count)), dma((PACK, bead_count)),
            dma((bead_count,)), dma((bead_count,)),
        ],
        compiler_params=pltpu.CompilerParams(
            collective_id=0, has_side_effects=True, vmem_limit_bytes=60 * 1024 * 1024
        ),
    )(nbr_tiles, positions, momenta, noise, charges, slab_route, cells, offsets, shaped, waves)
    return tuple(drifted[i] + force[i][:, None, :] for i in range(2))


def solution(mesh):
    in_specs = (
        P(None, "bead", "grid"),
        P(None, "bead", "grid"),
        P(None, "bead", "grid"),
        P("grid"),
        P("grid", None),
        P(None, "grid"),
        P(None, "grid"),
        P("grid", None),
    )
    out_specs = (P(None, "bead", "grid"), P(None, "bead", "grid"))

    def step(*args):
        return tuple(per_device(*args))

    return jax.shard_map(step, mesh=mesh, in_specs=in_specs, out_specs=out_specs, check_vma=False)
```

```python
import functools
import math

import jax
import jax.numpy as jnp
import numpy as np
from jax import lax
from jax.experimental import pallas as pl
from jax.experimental.pallas import tpu as pltpu
from jax.sharding import PartitionSpec as P

GX = GY = GZ = 256
WAVES = 8
BIN = 32
WINDOW = 36
CAP = 128
PACK = 2
coulomb_scale = 100000.0
screen_width = 200.0

def spline(fraction):
    remain = 1.0 - fraction
    square = fraction * fraction
    cubic = square * fraction
    values = [
        remain * remain * remain / 6.0,
        (3.0 * cubic - 6.0 * square + 4.0) / 6.0,
        (-3.0 * cubic + 3.0 * square + 3.0 * fraction + 1.0) / 6.0,
        cubic / 6.0,
    ]
    slopes = [
        -0.5 * remain * remain,
        0.5 * (3.0 * square - 4.0 * fraction),
        0.5 * (-3.0 * square + 2.0 * fraction + 1.0),
        0.5 * square,
    ]
    return (values, slopes)

def real_waves(length):
    half = length // 2
    row = np.arange(length)
    wave = np.where(row <= half, row, row - half)
    angle = (wave[:, None] * np.arange(length)[None, :] % length) * (2.0 * math.pi / length)
    return np.where((row <= half)[:, None], np.cos(angle), np.sin(angle))

def split_table(table):
    high = table.astype(jnp.bfloat16)
    low = (table - high.astype(np.float64)).astype(jnp.bfloat16)
    return high, low

def split(value):
    high = value.astype(jnp.bfloat16)
    low = (value - high.astype(jnp.float32)).astype(jnp.bfloat16)
    return high, low

NN = ((1,), (0,))
NT = ((1,), (1,))

def dot3(left, right, dims):
    def one(a, b):
        return lax.dot_general(a, b, (dims, ((), ())), preferred_element_type=jnp.float32)
    return one(left[0], right[0]) + (one(left[0], right[1]) + one(left[1], right[0]))

def tracks(fields):
    lowest = jnp.floor(fields)
    values, slopes = spline(fields - lowest)
    return [lowest, *values, *slopes]


def stencil(cells, members, length):
    row = lax.broadcasted_iota(jnp.int32, (length, cells.shape[1]), 0).astype(jnp.int16)
    hits = []
    for offset in range(4):
        cell = ((cells + (offset - 1)) & (length - 1)).astype(jnp.int16)
        hits.append(row == cell)

    def dense(rows):
        out = jnp.zeros(row.shape, jnp.bfloat16)
        for offset in range(4):
            out = jnp.where(hits[offset], rows[offset], out)
        return out

    found = []
    for rows in members:
        halves = [split(each) for each in rows]
        found.append((dense([half[0] for half in halves]), dense([half[1] for half in halves])))
    return found


def window(cells, members):
    row = lax.broadcasted_iota(jnp.int32, (WINDOW, cells.shape[1]), 0)
    hits = [row == cells + offset for offset in range(4)]

    def dense(rows):
        out = jnp.zeros(row.shape, jnp.float32)
        for offset in range(4):
            out = jnp.where(hits[offset], rows[offset], out)
        return out

    return [dense(rows) for rows in members]


def wave_of(group, shape):
    row = lax.broadcasted_iota(jnp.int32, shape, 0)
    half = WAVES // 2
    odd = (group == 0) & (row == half)
    wave = jnp.where(odd, GY // 2, group * half + (row & (half - 1)))
    turn = jnp.where((row < half) | odd, 0, -(GY // 4))
    return wave, turn

def turned(phase):
    phase = phase & (GY - 1)
    angle = (GY // 4 - jnp.abs(phase - GY // 2)).astype(jnp.float32) * (2.0 * math.pi / GY)
    square = angle * angle
    total = 1.0 / 6227020800.0
    for power in (39916800.0, 362880.0, 5040.0, 120.0, 6.0, 1.0):
        sign = -1.0 if power in (39916800.0, 5040.0, 6.0) else 1.0
        total = total * square + sign / power
    return -(angle * total)

def lines(cells, members, group):
    wave, turn = wave_of(group, (WAVES, cells.shape[1]))
    phase = wave * (cells - 1) + turn
    found = [0.0 for _ in members]
    for offset in range(4):
        cosine = turned(phase)
        found = [total + rows[offset] * cosine for total, rows in zip(found, members)]
        phase = phase + wave
    return found


def mesh_filter(total, filt):
    bead_count = lax.axis_size("bead")
    device = lax.axis_index("grid") * bead_count + lax.axis_index("bead")
    groups = GY // WAVES
    parts = lax.axis_size("grid") * bead_count // groups
    group = lax.rem(device, groups)
    part = lax.div(device, groups)
    reach = -1.0 / (2.0 * screen_width * screen_width)
    row = lax.broadcasted_iota(jnp.int32, (GX, GZ), 0)
    col = lax.broadcasted_iota(jnp.int32, (GX, GZ), 1)
    wx = jnp.where(row <= GX // 2, row, row - GX // 2)
    wz = jnp.where(col <= GZ // 2, col, col - GZ // 2)
    square = (wx * wx + wz * wz).astype(jnp.float32)
    times = jnp.where((wx & (GX // 2 - 1)) == 0, 1.0, 2.0) * jnp.where((wz & (GZ // 2 - 1)) == 0, 1.0, 2.0)
    if parts > 1:
        times = jnp.where(lax.div(col * parts, GZ) == part, times, 0.0)
    plain = times * jnp.exp(square * reach)
    filt[0] = plain
    filt[1] = square
    total[...] = jnp.zeros_like(total)


def mesh_phases(fields, tables, out, track, along, total, near, filt, ready, filler, filled, finished):
    domains = fields.shape[0]
    bead_count = lax.axis_size("bead")
    device = lax.axis_index("grid") * bead_count + lax.axis_index("bead")
    fx, fxt, rt, back = [tables.at[i] for i in range(4)]
    group = lax.rem(device, GY // WAVES)
    bins = GX // BIN
    cells_all = GX * WAVES
    halo = (WINDOW - BIN) * WAVES
    pack = PACK
    packs = domains // pack
    unroll = min(4, packs)
    chunks = packs // unroll

    for d in range(domains) if domains <= 8 else ():
        for k, rows in enumerate(tracks(fields[d])):
            track[d, k] = rows
    if domains > 8:
        def fill(d, carry):
            for k, rows in enumerate(tracks(fields[d])):
                track[d, k] = rows
            return carry
        lax.fori_loop(0, domains, fill, 0)

    def rows_of(first, where, dim):
        def one(k):
            return jnp.concatenate(
                [track[first + i, k, dim:dim + 1, where] for i in range(pack)], axis=1
            )
        return one(0).astype(jnp.int32), [one(1 + k) for k in range(4)], [one(5 + k) for k in range(4)]

    def span(s):
        return pl.ds(pl.multiple_of(s * CAP, CAP), CAP)

    lanes = total.shape[2]
    tiles = total.shape[0]

    def load(rows):
        return jnp.concatenate([total[i, rows, :] for i in range(tiles)], axis=1)

    def store(rows, value):
        for i in range(tiles):
            total[i, rows, :] = value[:, i * lanes:(i + 1) * lanes]

    def spread(i, carry):
        for k in range(4):
            spread_bin(4 * i + k)
        return carry

    def spread_bin(step):
        s = step // chunks
        where = span(s)
        got = None
        for j in range(unroll):
            pair = (step % chunks) * unroll + j
            first = pair * pack
            cells, values, _ = rows_of(first, where, 1)
            x, = window(cells - s * BIN, [values])
            cells, values, slopes = rows_of(first, where, 2)
            y, yd = lines(cells, [values, slopes], group)
            along[pair, s, 0] = y
            along[pair, s, 1] = yd
            charge = jnp.concatenate([fields[first + i, 0:1, where] for i in range(pack)], axis=1)
            y = y * charge
            cells, values, _ = rows_of(first, where, 3)
            z, = stencil(cells, [values], GZ)
            rows = split(jnp.concatenate([x[i:i + 1] * y for i in range(WINDOW)], axis=0))
            more = dot3(rows, z, NT)
            got = more if got is None else got + more
        rows = pl.ds(pl.multiple_of(s * (BIN * WAVES), BIN * WAVES), WINDOW * WAVES)
        store(rows, load(rows) + got)

    lax.fori_loop(0, bins * chunks // 4, spread, 0)
    total[:, 0:halo, :] += total[:, cells_all:cells_all + halo, :]
    ready()

    chains = WAVES
    size = cells_all // chains

    def row_blocks(i):
        return [pl.ds(pl.multiple_of((i * chains + k) * size, size), size) for k in range(chains)]

    def forward(i, carry):
        at = row_blocks(i)
        got = [dot3(split(load(rows)), (rt[0], rt[1]), NN) for rows in at]
        for rows, each in zip(at, got):
            store(rows, each)
        return carry

    filler()
    forward(0, 0)

    def middle(i, carry):
        at = [pl.ds(i * chains + k, GX, stride=WAVES) for k in range(chains)]
        got = [dot3((fx[0], fx[1]), split(load(rows)), NN) for rows in at]
        for k in range(chains):
            wave, _ = wave_of_row(group, i * chains + k)
            wave = jnp.full((1, GZ), wave, jnp.int32)
            wave_square = (wave * wave).astype(jnp.float32)
            count = jnp.where((wave & (GY // 2 - 1)) == 0, 1.0, 2.0)
            scale = count * jnp.exp(wave_square * (-1.0 / (2.0 * screen_width * screen_width)))
            scale = scale * (coulomb_scale / (GX * GY * GZ))
            m2 = filt[1] + wave_square
            got[k] = got[k] * jnp.where(m2 == 0.0, 0.0, filt[0] * scale / jnp.where(m2 == 0.0, 1.0, m2))
        got = [dot3((fxt[0], fxt[1]), split(each), NN) for each in got]
        for rows, each in zip(at, got):
            store(rows, each)
        return carry

    middle(0, 0)

    def inverse(i, carry):
        at = row_blocks(i)
        got = [dot3(split(load(rows)), (back[0], back[1]), NN) for rows in at]
        for rows, each in zip(at, got):
            high, low = split(each)
            near[0, rows, :] = high
            near[1, rows, :] = low
        return carry

    inverse(0, 0)
    filled()
    near[:, cells_all:cells_all + halo, :] = near[:, 0:halo, :]

    half = min(8, bins)
    own_pack = lax.axis_index("grid") // pack

    def gather(step, carry):
        pair = lax.rem(own_pack + 1 + step // (bins // half), packs)
        first = pair * pack
        for j in range(half):
            s = (step % (bins // half)) * half + j
            where = span(s)
            rows = pl.ds(pl.multiple_of(s * (BIN * WAVES), BIN * WAVES), WINDOW * WAVES)
            field = (near[0, rows, :], near[1, rows, :])
            cells, values, slopes = rows_of(first, where, 1)
            x, xd = window(cells - s * BIN, [values, slopes])
            cells, values, slopes = rows_of(first, where, 3)
            z, zd = stencil(cells, [values, slopes], GZ)
            plain = dot3(field, z, NN)
            steep = dot3(field, zd, NN)
            f = [0.0, 0.0, 0.0]
            for i in range(WINDOW):
                q = plain[i * WAVES:(i + 1) * WAVES]
                f[0] = f[0] + q * xd[i:i + 1]
                f[1] = f[1] + q * x[i:i + 1]
                f[2] = f[2] + steep[i * WAVES:(i + 1) * WAVES] * x[i:i + 1]
            y, yd = along[pair, s, 0], along[pair, s, 1]
            f = [f[0] * y, f[1] * yd, f[2] * y]
            charge = jnp.concatenate([fields[first + i, 0:1, where] for i in range(pack)], axis=1)
            for c in range(3):
                force = -charge * jnp.sum(f[c], axis=0, keepdims=True)
                for i in range(pack):
                    out[first + i, pl.ds(c * bins + s, 1), :] = force[:, i * CAP:(i + 1) * CAP]

        @pl.when(step % (bins // half) == bins // half - 1)
        def _():
            finished(pair)

        return carry

    lax.fori_loop(0, packs * (bins // half), gather, 0)


def wave_of_row(group, row):
    half = WAVES // 2
    odd = (group == 0) & (row == half)
    wave = jnp.where(odd, GY // 2, group * half + (row & (half - 1)))
    return wave, odd


def wave_tables():
    table = real_waves(GX)
    shifted = np.roll(table, 1, axis=1)
    return jnp.stack([jnp.stack(split_table(t)) for t in (shifted, shifted.T, table.T, table)])


TILE = 128
highest = lax.Precision.HIGHEST
time_step = 0.5
polymer_frequency = 1.0
centroid_friction = 0.5
pair_strength = 1.0 / 128.0
pair_range = 4.0
MESH = pl.DeviceIdType.MESH


def everyone(act):
    grid_count, bead_count = lax.axis_size("grid"), lax.axis_size("bead")
    me = lax.axis_index("grid") * bead_count + lax.axis_index("bead")

    def one(step, carry):
        peer = lax.rem(me + step, grid_count * bead_count)
        act(lax.div(peer, bead_count), lax.rem(peer, bead_count))
        return carry

    lax.fori_loop(1, grid_count * bead_count, one, 0)
    return grid_count * bead_count - 1


def hail():
    barrier = pltpu.get_barrier_semaphore()

    def signal(g, b):
        pl.semaphore_signal(barrier, 1, device_id=(g, b), device_id_type=MESH)

    return everyone(signal)


def shares(name, source, target, send_sem, recv_sem):
    count = lax.axis_size(name)
    me = lax.axis_index(name)

    def copy(step, landing):
        peer = lax.rem(me + step, count)
        return pltpu.make_async_remote_copy(
            src_ref=source(peer),
            dst_ref=target(peer if landing else me),
            send_sem=send_sem.at[peer],
            recv_sem=recv_sem.at[peer if landing else me],
            device_id={name: peer},
            device_id_type=MESH,
        )

    def start():
        def one(step, carry):
            copy(step, False).start()
            return carry

        lax.fori_loop(1, count, one, 0)

    def wait():
        def one(step, carry):
            copy(step, True).wait_recv()
            return carry

        lax.fori_loop(1, count, one, 0)

    def drain():
        def one(step, carry):
            copy(step, False).wait_send()
            return carry

        lax.fori_loop(1, count, one, 0)

    return start, wait, drain


def split3(value):
    high = value.astype(jnp.bfloat16)
    rest = value - high.astype(jnp.float32)
    middle = rest.astype(jnp.bfloat16)
    return high, middle, (rest - middle.astype(jnp.float32)).astype(jnp.bfloat16)


def slots_of(route, per_bin):
    atoms = route.shape[1]
    bins = GX // BIN
    owner = lax.div(route, per_bin)
    bin_row = lax.broadcasted_iota(jnp.int32, (2 * bins, atoms), 0)
    mine = bin_row == owner
    before = lax.broadcasted_iota(jnp.int32, (atoms, atoms), 0)
    after = lax.broadcasted_iota(jnp.int32, (atoms, atoms), 1)
    earlier = jnp.where(before < after, 1.0, 0.0).astype(jnp.bfloat16)
    chosen = jnp.where(mine, 1.0, 0.0)
    rank = jnp.dot(chosen.astype(jnp.bfloat16), earlier, preferred_element_type=jnp.float32)
    rank = jnp.sum(chosen * rank, axis=0, keepdims=True)
    return owner * CAP + rank.astype(jnp.int32)


def placement(slot):
    spots = lax.broadcasted_iota(jnp.int32, (GX // BIN * CAP, slot.shape[1]), 0)
    return jnp.where(spots == slot, 1.0, 0.0).astype(jnp.bfloat16)


def pair_forces(weight_of, positions, momenta, kicked, chosen):
    beads, atoms = positions.shape[1:]
    across = [positions[c].T for c in range(3)]
    spans = [slice(t * TILE, (t + 1) * TILE) for t in range(atoms // TILE)]
    weights = [[weight_of(t, m) for m in range(len(spans))] for t in chosen]
    for b in range(beads):
        centres = [[positions[c, b : b + 1, spans[t]] for c in range(3)] for t in chosen]
        sums = [[jnp.zeros((8, TILE), jnp.float32) for _ in range(3)] for _ in chosen]
        for m, span in enumerate(spans):
            columns = [jnp.broadcast_to(across[c][span, b : b + 1], (TILE, TILE)) for c in range(3)]
            for i in range(len(chosen)):
                apart = [centres[i][c] - columns[c] for c in range(3)]
                square = apart[0] * apart[0] + apart[1] * apart[1] + apart[2] * apart[2]
                weight = jnp.exp(square * (-1.0 / pair_range))
                for c in range(3):
                    part = jnp.sum((weight * apart[c]).reshape(TILE // 8, 8, TILE), axis=0)
                    sums[i][c] = sums[i][c] + weights[i][m] * part
        for i, t in enumerate(chosen):
            for c in range(3):
                force = jnp.sum(sums[i][c], axis=0, keepdims=True)
                kicked[c, b : b + 1, spans[t]] = momenta[c, b : b + 1, spans[t]] + force


def step_tables(bead_total):
    mode = np.arange(bead_total)
    angle = (mode[:, None] * mode[None, :] % bead_total) * (2.0 * math.pi / bead_total)
    middle = bead_total // 2
    scaled = math.sqrt(2.0 / bead_total)
    column = mode[:, None]
    matrix = np.where(
        column == 0,
        1.0 / math.sqrt(bead_total),
        np.where(
            column < middle,
            scaled * np.cos(angle),
            np.where(
                column == middle, np.cos(angle) / math.sqrt(bead_total), scaled * np.sin(angle)
            ),
        ),
    )
    half = 0.5 * time_step
    frequency = 2.0 * polymer_frequency * np.sin(mode * (math.pi / bead_total))
    cosine = np.cos(frequency * half)
    drift = np.where(mode == 0, half, np.sin(frequency * half) / np.where(mode == 0, 1.0, frequency))
    pull = frequency * np.sin(frequency * half)
    friction = np.where(mode == 0, centroid_friction, 2.0 * frequency)
    damping = np.exp(-friction * time_step)
    kick = np.sqrt(1.0 - damping * damping)
    factors = [
        [cosine * cosine - drift * damping * pull, drift * cosine * (1.0 + damping), drift * kick],
        [-cosine * pull * (1.0 + damping), cosine * damping * cosine - pull * drift, cosine * kick],
    ]
    tables = np.stack(
        [
            np.stack(
                [
                    matrix.T @ (row[0][:, None] * matrix),
                    matrix.T @ (row[1][:, None] * matrix),
                    matrix.T * row[2][None, :],
                ]
            )
            for row in factors
        ]
    )
    return tables.astype(np.float32), (float(factors[0][1][0]), float(factors[1][1][0]))


def step_kernel(
    planes, centre, neighbours, positions, momenta, noise, charges, route, cells, offsets, mixing, waves,
    drifted, force_q, force_p,
    own_momenta, own_charges, own_route, own_cells, own_offsets, own_mixing, own_waves,
    fields, sources, kicks, partial, landed, mates, level, last, steps, track, along, total, near, filt,
    local_sem, field_send, field_recv, place_send, place_recv, noise_send, noise_recv,
    kick_send, kick_recv, part_send, part_recv, mate_send, mate_recv, last_send, last_recv,
):
    grid_rank = lax.axis_index("grid")
    bead_rank = lax.axis_index("bead")
    bead_count = lax.axis_size("bead")
    domains = partial.shape[0]
    beads = kicks.shape[2]

    others = hail()
    pairs = [
        (route, own_route), (charges, own_charges), (cells, own_cells), (offsets, own_offsets),
        (positions, sources.at[bead_rank, 0]), (momenta, own_momenta),
        (noise, sources.at[bead_rank, 1]), (mixing, own_mixing), (waves, own_waves),
    ]
    loads = [pltpu.make_async_copy(a, b, local_sem.at[i]) for i, (a, b) in enumerate(pairs)]
    for load in loads:
        load.start()
    for load in loads[0:4]:
        load.wait()

    rows = own_route[...]
    slot = slots_of(rows, BIN // planes)
    first = (rows * planes + own_cells[0:1]).astype(jnp.float32) + own_offsets[0:1]
    rest = own_cells[1:3].astype(jnp.float32) + own_offsets[1:3]
    own = jnp.concatenate([own_charges[...], first, rest], axis=0)
    halves = [each.astype(jnp.float32) for each in split3(own)]
    packed = jnp.concatenate(halves + [jnp.zeros_like(own)], axis=0).astype(jnp.bfloat16)
    got = lax.dot_general(packed, placement(slot), (NT, ((), ())), preferred_element_type=jnp.float32)
    fields[grid_rank] = (got[0:4] + got[4:8]) + got[8:12]

    pl.semaphore_wait(pltpu.get_barrier_semaphore(), others)
    field = shares("grid", lambda p: fields.at[grid_rank], lambda p: fields.at[p], field_send, field_recv)
    place = shares("bead", lambda p: positions, lambda p: sources.at[p, 0], place_send, place_recv)
    draw = shares("bead", lambda p: noise, lambda p: sources.at[p, 1], noise_send, noise_recv)
    kick = shares("bead", lambda p: kicks.at[bead_rank], lambda p: kicks.at[p], kick_send, kick_recv)
    summed = shares("bead", lambda p: level, lambda p: last.at[p], last_send, last_recv)
    own_pack = lax.div(grid_rank, PACK)
    place_in = lax.rem(grid_rank, PACK)

    def far(g, landing=False):
        return pltpu.make_async_remote_copy(
            src_ref=partial.at[g],
            dst_ref=landed.at[g if landing else grid_rank],
            send_sem=part_send.at[g],
            recv_sem=part_recv.at[g if landing else grid_rank],
            device_id={"grid": g},
            device_id_type=MESH,
        )

    def close(step, landing=False):
        peer = lax.rem(place_in * bead_count + bead_rank + step, PACK * bead_count)
        i, b = lax.div(peer, bead_count), lax.rem(peer, bead_count)
        at = (i, b) if landing else (place_in, bead_rank)
        return pltpu.make_async_remote_copy(
            src_ref=partial.at[own_pack * PACK + i],
            dst_ref=mates.at[at],
            send_sem=mate_send.at[i, b],
            recv_sem=mate_recv.at[at],
            device_id=(own_pack * PACK + i, b),
            device_id_type=MESH,
        )

    def each_far(act):
        def one(step, carry):
            act(lax.rem((own_pack + 1) * PACK + step, domains))
            return carry

        lax.fori_loop(0, domains - PACK, one, 0)

    def each_close(act):
        def one(step, carry):
            act(step)
            return carry

        lax.fori_loop(1, PACK * bead_count, one, 0)

    for each in (field, place, draw):
        each[0]()

    mesh_filter(total, filt)

    def weight_of(t, m):
        total = 0.0
        for k in range(neighbours.shape[1]):
            total += jnp.where(neighbours[t, k] == m, 0.5 * time_step * pair_strength, 0.0)
        return total

    loads[4].wait()
    loads[5].wait()

    def pair(chosen):
        pair_forces(
            weight_of, sources.at[bead_rank, 0], own_momenta, kicks.at[bead_rank], chosen
        )

    tiles = own_momenta.shape[2] // TILE
    early = tiles - tiles // 4
    pair(range(early))
    field[1]()

    def finished(pair):
        @pl.when(pair != own_pack)
        def _():
            for i in range(PACK):
                far(pair * PACK + i).start()

        @pl.when(pair == own_pack)
        def _():
            each_close(lambda step: close(step).start())

    mesh_phases(
        fields, own_waves, partial, track, along, total, near, filt, loads[8].wait,
        lambda: pair(range(early, tiles)), kick[0], finished,
    )

    mates[place_in, bead_rank] = partial[grid_rank]
    each_far(lambda g: far(g, True).wait_recv())

    def add(step, forces):
        return forces + landed[lax.rem((own_pack + 1) * PACK + step, domains)]

    level[...] = lax.fori_loop(0, domains - PACK, add, jnp.zeros(level.shape, jnp.float32))
    summed[0]()
    where = placement(slot)
    for each in (place, draw, kick):
        each[1]()
    loads[6].wait()
    loads[7].wait()
    mix = own_mixing[bead_rank]

    def stepped(c):
        parts = [sources[k, 0, c] for k in range(bead_count)]
        parts += [kicks[k, c] for k in range(bead_count)]
        parts += [sources[k, 1, c] for k in range(bead_count)]
        got = jnp.dot(mix, jnp.concatenate(parts, axis=0), precision=highest, preferred_element_type=jnp.float32)
        steps[0, c] = got[0:beads]
        steps[1, c] = got[beads:]

    for component in range(3):
        stepped(component)
    leave = pltpu.make_async_copy(steps, drifted, local_sem.at[len(pairs)])
    leave.start()
    each_close(lambda step: close(step, True).wait_recv())
    forces = level[...]
    for k in range(bead_count):
        for i in range(PACK):
            forces = forces + mates[i, k]
    summed[1]()
    last[bead_rank] = jnp.zeros(level.shape, jnp.float32)
    for k in range(bead_count):
        forces = forces + last[k]
    bins = GX // BIN
    forces = jnp.concatenate(
        [
            jnp.concatenate([forces[c * bins + s : c * bins + s + 1] for s in range(bins)], axis=1)
            for c in range(3)
        ],
        axis=0,
    )
    halves = [each.astype(jnp.float32) for each in split3(forces)]
    packed = jnp.concatenate(halves + [jnp.zeros((16 - 9, forces.shape[1]), jnp.float32)], axis=0)
    got = jnp.dot(packed.astype(jnp.bfloat16), where, preferred_element_type=jnp.float32)
    force = (got[0:3] + got[3:6]) + got[6:9]
    force_q[...] = centre[0] * force
    force_p[...] = centre[1] * force
    leave.wait()
    for each in (field, place, draw, kick, summed):
        each[2]()
    each_far(lambda g: far(g).wait_send())
    each_close(lambda step: close(step).wait_send())


def per_device(positions, momenta, noise, charges, slab_route, cells, offsets, nbr_tiles):
    grid_count = lax.axis_size("grid")
    bead_count = lax.axis_size("bead")
    beads, atoms = positions.shape[1:]
    slots = GX // BIN * CAP
    sheet = (3 * (GX // BIN), CAP)
    tables, centre = step_tables(beads * bead_count)
    shaped = tables.reshape(2, 3, bead_count, beads, -1).transpose(2, 0, 3, 1, 4)
    shaped = jnp.asarray(shaped.reshape(bead_count, 2 * beads, -1))
    centre = tuple(0.5 * time_step * value for value in centre)
    waves = wave_tables()
    vmem = pl.BlockSpec(memory_space=pltpu.VMEM)
    anywhere = pl.BlockSpec(memory_space=pl.ANY)
    dma = pltpu.SemaphoreType.DMA
    whole = lambda array: pltpu.VMEM(array.shape, array.dtype)
    f32 = lambda *shape: pltpu.VMEM(shape, jnp.float32)
    charges = charges.reshape(1, atoms)
    slab_route = slab_route.reshape(1, atoms)
    drifted, *force = pl.pallas_call(
        functools.partial(step_kernel, GX // grid_count, centre),
        out_shape=[
            jax.ShapeDtypeStruct((2, *positions.shape), jnp.float32),
            jax.ShapeDtypeStruct((3, atoms), jnp.float32),
            jax.ShapeDtypeStruct((3, atoms), jnp.float32),
        ],
        in_specs=[pl.BlockSpec(memory_space=pltpu.SMEM)] + [anywhere] * 9,
        out_specs=[anywhere, vmem, vmem],
        scratch_shapes=[
            whole(momenta), whole(charges), whole(slab_route), whole(cells), whole(offsets),
            whole(shaped), whole(waves),
            f32(grid_count, 4, slots),
            f32(bead_count, 2, *positions.shape),
            f32(bead_count, *positions.shape),
            f32(grid_count, *sheet),
            f32(grid_count, *sheet),
            f32(PACK, bead_count, *sheet),
            f32(*sheet),
            f32(bead_count, *sheet),
            f32(2, *positions.shape),
            f32(grid_count, 9, 4, slots),
            f32(grid_count // 2, GX // BIN, 2, WAVES, 2 * CAP),
            f32(GZ // 128, (GX + WINDOW - BIN) * WAVES, 128),
            pltpu.VMEM((2, (GX + WINDOW - BIN) * WAVES, GZ), jnp.bfloat16),
            f32(2, GX, GZ),
            dma((10,)),
            dma((grid_count,)), dma((grid_count,)),
            *[dma((bead_count,)) for _ in range(6)],
            dma((grid_count,)), dma((grid_count,)),
            dma((PACK, bead_count)), dma((PACK, bead_count)),
            dma((bead_count,)), dma((bead_count,)),
        ],
        compiler_params=pltpu.CompilerParams(
            collective_id=0, has_side_effects=True, vmem_limit_bytes=60 * 1024 * 1024
        ),
    )(nbr_tiles, positions, momenta, noise, charges, slab_route, cells, offsets, shaped, waves)
    return tuple(drifted[i] + force[i][:, None, :] for i in range(2))


def solution(mesh):
    in_specs = (
        P(None, "bead", "grid"),
        P(None, "bead", "grid"),
        P(None, "bead", "grid"),
        P("grid"),
        P("grid", None),
        P(None, "grid"),
        P(None, "grid"),
        P("grid", None),
    )
    out_specs = (P(None, "bead", "grid"), P(None, "bead", "grid"))

    def step(*args):
        return tuple(per_device(*args))

    return jax.shard_map(step, mesh=mesh, in_specs=in_specs, out_specs=out_specs, check_vma=False)
```

```python
import functools
import math

import jax
import jax.numpy as jnp
import numpy as np
from jax import lax
from jax.experimental import pallas as pl
from jax.experimental.pallas import tpu as pltpu
from jax.sharding import PartitionSpec as P

GX = GY = GZ = 256
WAVES = 8
BIN = 32
WINDOW = 36
CAP = 128
PACK = 2
coulomb_scale = 100000.0
screen_width = 200.0

def spline(fraction):
    remain = 1.0 - fraction
    square = fraction * fraction
    cubic = square * fraction
    values = [
        remain * remain * remain / 6.0,
        (3.0 * cubic - 6.0 * square + 4.0) / 6.0,
        (-3.0 * cubic + 3.0 * square + 3.0 * fraction + 1.0) / 6.0,
        cubic / 6.0,
    ]
    slopes = [
        -0.5 * remain * remain,
        0.5 * (3.0 * square - 4.0 * fraction),
        0.5 * (-3.0 * square + 2.0 * fraction + 1.0),
        0.5 * square,
    ]
    return (values, slopes)

def real_waves(length):
    half = length // 2
    row = np.arange(length)
    wave = np.where(row <= half, row, row - half)
    angle = (wave[:, None] * np.arange(length)[None, :] % length) * (2.0 * math.pi / length)
    return np.where((row <= half)[:, None], np.cos(angle), np.sin(angle))

def split_table(table):
    high = table.astype(jnp.bfloat16)
    low = (table - high.astype(np.float64)).astype(jnp.bfloat16)
    return high, low

def split(value):
    high = value.astype(jnp.bfloat16)
    low = (value - high.astype(jnp.float32)).astype(jnp.bfloat16)
    return high, low

NN = ((1,), (0,))
NT = ((1,), (1,))

def dot3(left, right, dims):
    def one(a, b):
        return lax.dot_general(a, b, (dims, ((), ())), preferred_element_type=jnp.float32)
    return one(left[0], right[0]) + (one(left[0], right[1]) + one(left[1], right[0]))

def tracks(fields):
    lowest = jnp.floor(fields)
    values, slopes = spline(fields - lowest)
    return [lowest, *values, *slopes]


def stencil(cells, members, length):
    row = lax.broadcasted_iota(jnp.int32, (length, cells.shape[1]), 0).astype(jnp.int16)
    hits = []
    for offset in range(4):
        cell = ((cells + (offset - 1)) & (length - 1)).astype(jnp.int16)
        hits.append(row == cell)

    def dense(rows):
        out = jnp.zeros(row.shape, jnp.bfloat16)
        for offset in range(4):
            out = jnp.where(hits[offset], rows[offset], out)
        return out

    found = []
    for rows in members:
        halves = [split(each) for each in rows]
        found.append((dense([half[0] for half in halves]), dense([half[1] for half in halves])))
    return found


def window(cells, members):
    row = lax.broadcasted_iota(jnp.int32, (WINDOW, cells.shape[1]), 0)
    hits = [row == cells + offset for offset in range(4)]

    def dense(rows):
        out = jnp.zeros(row.shape, jnp.float32)
        for offset in range(4):
            out = jnp.where(hits[offset], rows[offset], out)
        return out

    return [dense(rows) for rows in members]


def wave_of(group, shape):
    row = lax.broadcasted_iota(jnp.int32, shape, 0)
    half = WAVES // 2
    odd = (group == 0) & (row == half)
    wave = jnp.where(odd, GY // 2, group * half + (row & (half - 1)))
    turn = jnp.where((row < half) | odd, 0, -(GY // 4))
    return wave, turn

def turned(phase):
    phase = phase & (GY - 1)
    angle = (GY // 4 - jnp.abs(phase - GY // 2)).astype(jnp.float32) * (2.0 * math.pi / GY)
    square = angle * angle
    total = 1.0 / 6227020800.0
    for power in (39916800.0, 362880.0, 5040.0, 120.0, 6.0, 1.0):
        sign = -1.0 if power in (39916800.0, 5040.0, 6.0) else 1.0
        total = total * square + sign / power
    return -(angle * total)

def lines(cells, members, group):
    wave, turn = wave_of(group, (WAVES, cells.shape[1]))
    phase = wave * (cells - 1) + turn
    found = [0.0 for _ in members]
    for offset in range(4):
        cosine = turned(phase)
        found = [total + rows[offset] * cosine for total, rows in zip(found, members)]
        phase = phase + wave
    return found


def mesh_filter(total, filt):
    bead_count = lax.axis_size("bead")
    device = lax.axis_index("grid") * bead_count + lax.axis_index("bead")
    groups = GY // WAVES
    parts = lax.axis_size("grid") * bead_count // groups
    group = lax.rem(device, groups)
    part = lax.div(device, groups)
    reach = -1.0 / (2.0 * screen_width * screen_width)
    row = lax.broadcasted_iota(jnp.int32, (GX, GZ), 0)
    col = lax.broadcasted_iota(jnp.int32, (GX, GZ), 1)
    wx = jnp.where(row <= GX // 2, row, row - GX // 2)
    wz = jnp.where(col <= GZ // 2, col, col - GZ // 2)
    square = (wx * wx + wz * wz).astype(jnp.float32)
    times = jnp.where((wx & (GX // 2 - 1)) == 0, 1.0, 2.0) * jnp.where((wz & (GZ // 2 - 1)) == 0, 1.0, 2.0)
    if parts > 1:
        times = jnp.where(lax.div(col * parts, GZ) == part, times, 0.0)
    plain = times * jnp.exp(square * reach)
    filt[0] = plain
    filt[1] = square
    total[...] = jnp.zeros_like(total)


def mesh_phases(fields, tables, out, track, along, total, near, filt, ready, filler, filled, finished):
    domains = fields.shape[0]
    bead_count = lax.axis_size("bead")
    device = lax.axis_index("grid") * bead_count + lax.axis_index("bead")
    fx, fxt, rt, back = [tables.at[i] for i in range(4)]
    group = lax.rem(device, GY // WAVES)
    bins = GX // BIN
    cells_all = GX * WAVES
    halo = (WINDOW - BIN) * WAVES
    pack = PACK
    packs = domains // pack
    unroll = min(4, packs)
    chunks = packs // unroll

    for d in range(domains) if domains <= 8 else ():
        for k, rows in enumerate(tracks(fields[d])):
            track[d, k] = rows
    if domains > 8:
        def fill(d, carry):
            for k, rows in enumerate(tracks(fields[d])):
                track[d, k] = rows
            return carry
        lax.fori_loop(0, domains, fill, 0)

    def rows_of(first, where, dim):
        def one(k):
            return jnp.concatenate(
                [track[first + i, k, dim:dim + 1, where] for i in range(pack)], axis=1
            )
        return one(0).astype(jnp.int32), [one(1 + k) for k in range(4)], [one(5 + k) for k in range(4)]

    def span(s):
        return pl.ds(pl.multiple_of(s * CAP, CAP), CAP)

    lanes = total.shape[2]
    tiles = total.shape[0]

    def load(rows):
        return jnp.concatenate([total[i, rows, :] for i in range(tiles)], axis=1)

    def store(rows, value):
        for i in range(tiles):
            total[i, rows, :] = value[:, i * lanes:(i + 1) * lanes]

    def spread(i, carry):
        for k in range(4):
            spread_bin(4 * i + k)
        return carry

    def spread_bin(step):
        s = step // chunks
        where = span(s)
        got = None
        for j in range(unroll):
            pair = (step % chunks) * unroll + j
            first = pair * pack
            cells, values, _ = rows_of(first, where, 1)
            x, = window(cells - s * BIN, [values])
            cells, values, slopes = rows_of(first, where, 2)
            y, yd = lines(cells, [values, slopes], group)
            along[pair, s, 0] = y
            along[pair, s, 1] = yd
            charge = jnp.concatenate([fields[first + i, 0:1, where] for i in range(pack)], axis=1)
            y = y * charge
            cells, values, _ = rows_of(first, where, 3)
            z, = stencil(cells, [values], GZ)
            rows = split(jnp.concatenate([x[i:i + 1] * y for i in range(WINDOW)], axis=0))
            more = dot3(rows, z, NT)
            got = more if got is None else got + more
        rows = pl.ds(pl.multiple_of(s * (BIN * WAVES), BIN * WAVES), WINDOW * WAVES)
        store(rows, load(rows) + got)

    lax.fori_loop(0, bins * chunks // 4, spread, 0)
    total[:, 0:halo, :] += total[:, cells_all:cells_all + halo, :]
    ready()

    chains = WAVES
    size = cells_all // chains

    def row_blocks(i):
        return [pl.ds(pl.multiple_of((i * chains + k) * size, size), size) for k in range(chains)]

    def forward(i, carry):
        at = row_blocks(i)
        got = [dot3(split(load(rows)), (rt[0], rt[1]), NN) for rows in at]
        for rows, each in zip(at, got):
            store(rows, each)
        return carry

    filler()
    forward(0, 0)

    def middle(i, carry):
        at = [pl.ds(i * chains + k, GX, stride=WAVES) for k in range(chains)]
        got = [dot3((fx[0], fx[1]), split(load(rows)), NN) for rows in at]
        for k in range(chains):
            wave, _ = wave_of_row(group, i * chains + k)
            wave = jnp.full((1, GZ), wave, jnp.int32)
            wave_square = (wave * wave).astype(jnp.float32)
            count = jnp.where((wave & (GY // 2 - 1)) == 0, 1.0, 2.0)
            scale = count * jnp.exp(wave_square * (-1.0 / (2.0 * screen_width * screen_width)))
            scale = scale * (coulomb_scale / (GX * GY * GZ))
            m2 = filt[1] + wave_square
            got[k] = got[k] * jnp.where(m2 == 0.0, 0.0, filt[0] * scale / jnp.where(m2 == 0.0, 1.0, m2))
        got = [dot3((fxt[0], fxt[1]), split(each), NN) for each in got]
        for rows, each in zip(at, got):
            store(rows, each)
        return carry

    middle(0, 0)

    def inverse(i, carry):
        at = row_blocks(i)
        got = [dot3(split(load(rows)), (back[0], back[1]), NN) for rows in at]
        for rows, each in zip(at, got):
            high, low = split(each)
            near[0, rows, :] = high
            near[1, rows, :] = low
        return carry

    inverse(0, 0)
    filled()
    near[:, cells_all:cells_all + halo, :] = near[:, 0:halo, :]

    half = min(8, bins)
    own_pack = lax.axis_index("grid") // pack

    def gather(step, carry):
        pair = lax.rem(own_pack + 1 + step // (bins // half), packs)
        first = pair * pack
        for j in range(half):
            s = (step % (bins // half)) * half + j
            where = span(s)
            rows = pl.ds(pl.multiple_of(s * (BIN * WAVES), BIN * WAVES), WINDOW * WAVES)
            field = (near[0, rows, :], near[1, rows, :])
            cells, values, slopes = rows_of(first, where, 1)
            x, xd = window(cells - s * BIN, [values, slopes])
            cells, values, slopes = rows_of(first, where, 3)
            z, zd = stencil(cells, [values, slopes], GZ)
            plain = dot3(field, z, NN)
            steep = dot3(field, zd, NN)
            f = [0.0, 0.0, 0.0]
            for i in range(WINDOW):
                q = plain[i * WAVES:(i + 1) * WAVES]
                f[0] = f[0] + q * xd[i:i + 1]
                f[1] = f[1] + q * x[i:i + 1]
                f[2] = f[2] + steep[i * WAVES:(i + 1) * WAVES] * x[i:i + 1]
            y, yd = along[pair, s, 0], along[pair, s, 1]
            f = [f[0] * y, f[1] * yd, f[2] * y]
            charge = jnp.concatenate([fields[first + i, 0:1, where] for i in range(pack)], axis=1)
            for c in range(3):
                force = -charge * jnp.sum(f[c], axis=0, keepdims=True)
                for i in range(pack):
                    out[first + i, pl.ds(c * bins + s, 1), :] = force[:, i * CAP:(i + 1) * CAP]

        @pl.when(step % (bins // half) == bins // half - 1)
        def _():
            finished(pair)

        return carry

    lax.fori_loop(0, packs * (bins // half), gather, 0)


def wave_of_row(group, row):
    half = WAVES // 2
    odd = (group == 0) & (row == half)
    wave = jnp.where(odd, GY // 2, group * half + (row & (half - 1)))
    return wave, odd


def wave_tables():
    table = real_waves(GX)
    shifted = np.roll(table, 1, axis=1)
    return jnp.stack([jnp.stack(split_table(t)) for t in (shifted, shifted.T, table.T, table)])


TILE = 128
highest = lax.Precision.HIGHEST
time_step = 0.5
polymer_frequency = 1.0
centroid_friction = 0.5
pair_strength = 1.0 / 128.0
pair_range = 4.0
MESH = pl.DeviceIdType.MESH


def everyone(act):
    grid_count, bead_count = lax.axis_size("grid"), lax.axis_size("bead")
    me = lax.axis_index("grid") * bead_count + lax.axis_index("bead")

    def one(step, carry):
        peer = lax.rem(me + step, grid_count * bead_count)
        act(lax.div(peer, bead_count), lax.rem(peer, bead_count))
        return carry

    lax.fori_loop(1, grid_count * bead_count, one, 0)
    return grid_count * bead_count - 1


def hail():
    barrier = pltpu.get_barrier_semaphore()

    def signal(g, b):
        pl.semaphore_signal(barrier, 1, device_id=(g, b), device_id_type=MESH)

    return everyone(signal)


def shares(name, source, target, send_sem, recv_sem):
    count = lax.axis_size(name)
    me = lax.axis_index(name)

    def copy(step, landing):
        peer = lax.rem(me + step, count)
        return pltpu.make_async_remote_copy(
            src_ref=source(peer),
            dst_ref=target(peer if landing else me),
            send_sem=send_sem.at[peer],
            recv_sem=recv_sem.at[peer if landing else me],
            device_id={name: peer},
            device_id_type=MESH,
        )

    def start():
        def one(step, carry):
            copy(step, False).start()
            return carry

        lax.fori_loop(1, count, one, 0)

    def wait():
        def one(step, carry):
            copy(step, True).wait_recv()
            return carry

        lax.fori_loop(1, count, one, 0)

    def drain():
        def one(step, carry):
            copy(step, False).wait_send()
            return carry

        lax.fori_loop(1, count, one, 0)

    return start, wait, drain


def split3(value):
    high = value.astype(jnp.bfloat16)
    rest = value - high.astype(jnp.float32)
    middle = rest.astype(jnp.bfloat16)
    return high, middle, (rest - middle.astype(jnp.float32)).astype(jnp.bfloat16)


def slots_of(route, per_bin):
    atoms = route.shape[1]
    bins = GX // BIN
    owner = lax.div(route, per_bin)
    bin_row = lax.broadcasted_iota(jnp.int32, (2 * bins, atoms), 0)
    mine = bin_row == owner
    before = lax.broadcasted_iota(jnp.int32, (atoms, atoms), 0)
    after = lax.broadcasted_iota(jnp.int32, (atoms, atoms), 1)
    earlier = jnp.where(before < after, 1.0, 0.0).astype(jnp.bfloat16)
    chosen = jnp.where(mine, 1.0, 0.0)
    rank = jnp.dot(chosen.astype(jnp.bfloat16), earlier, preferred_element_type=jnp.float32)
    rank = jnp.sum(chosen * rank, axis=0, keepdims=True)
    return owner * CAP + rank.astype(jnp.int32)


def placement(slot):
    spots = lax.broadcasted_iota(jnp.int32, (GX // BIN * CAP, slot.shape[1]), 0)
    return jnp.where(spots == slot, 1.0, 0.0).astype(jnp.bfloat16)


def pair_forces(weight_of, positions, momenta, kicked, chosen):
    beads, atoms = positions.shape[1:]
    halved = 1.0 / math.sqrt(pair_range)
    across = [(positions[c] * halved).T for c in range(3)]
    spans = [slice(t * TILE, (t + 1) * TILE) for t in range(atoms // TILE)]
    weights = [[weight_of(t, m) for m in range(len(spans))] for t in chosen]
    for b in range(beads):
        centres = [[positions[c, b : b + 1, spans[t]] * halved for c in range(3)] for t in chosen]
        sums = [[jnp.zeros((8, TILE), jnp.float32) for _ in range(3)] for _ in chosen]
        for m, span in enumerate(spans):
            columns = [jnp.broadcast_to(across[c][span, b : b + 1], (TILE, TILE)) for c in range(3)]
            for i in range(len(chosen)):
                apart = [centres[i][c] - columns[c] for c in range(3)]
                square = apart[0] * apart[0] + apart[1] * apart[1] + apart[2] * apart[2]
                weight = jnp.exp(-square)
                for c in range(3):
                    part = jnp.sum((weight * apart[c]).reshape(TILE // 8, 8, TILE), axis=0)
                    sums[i][c] = sums[i][c] + weights[i][m] * part
        for i, t in enumerate(chosen):
            for c in range(3):
                force = jnp.sum(sums[i][c], axis=0, keepdims=True)
                kicked[c, b : b + 1, spans[t]] = momenta[c, b : b + 1, spans[t]] + force


def step_tables(bead_total):
    mode = np.arange(bead_total)
    angle = (mode[:, None] * mode[None, :] % bead_total) * (2.0 * math.pi / bead_total)
    middle = bead_total // 2
    scaled = math.sqrt(2.0 / bead_total)
    column = mode[:, None]
    matrix = np.where(
        column == 0,
        1.0 / math.sqrt(bead_total),
        np.where(
            column < middle,
            scaled * np.cos(angle),
            np.where(
                column == middle, np.cos(angle) / math.sqrt(bead_total), scaled * np.sin(angle)
            ),
        ),
    )
    half = 0.5 * time_step
    frequency = 2.0 * polymer_frequency * np.sin(mode * (math.pi / bead_total))
    cosine = np.cos(frequency * half)
    drift = np.where(mode == 0, half, np.sin(frequency * half) / np.where(mode == 0, 1.0, frequency))
    pull = frequency * np.sin(frequency * half)
    friction = np.where(mode == 0, centroid_friction, 2.0 * frequency)
    damping = np.exp(-friction * time_step)
    kick = np.sqrt(1.0 - damping * damping)
    factors = [
        [cosine * cosine - drift * damping * pull, drift * cosine * (1.0 + damping), drift * kick],
        [-cosine * pull * (1.0 + damping), cosine * damping * cosine - pull * drift, cosine * kick],
    ]
    tables = np.stack(
        [
            np.stack(
                [
                    matrix.T @ (row[0][:, None] * matrix),
                    matrix.T @ (row[1][:, None] * matrix),
                    matrix.T * row[2][None, :],
                ]
            )
            for row in factors
        ]
    )
    return tables.astype(np.float32), (float(factors[0][1][0]), float(factors[1][1][0]))


def step_kernel(
    planes, centre, neighbours, positions, momenta, noise, charges, route, cells, offsets, mixing, waves,
    drifted, force_q, force_p,
    own_momenta, own_charges, own_route, own_cells, own_offsets, own_mixing, own_waves,
    fields, sources, kicks, partial, landed, mates, level, last, steps, track, along, total, near, filt,
    local_sem, field_send, field_recv, place_send, place_recv, noise_send, noise_recv,
    kick_send, kick_recv, part_send, part_recv, mate_send, mate_recv, last_send, last_recv,
):
    grid_rank = lax.axis_index("grid")
    bead_rank = lax.axis_index("bead")
    bead_count = lax.axis_size("bead")
    domains = partial.shape[0]
    beads = kicks.shape[2]

    others = hail()
    pairs = [
        (route, own_route), (charges, own_charges), (cells, own_cells), (offsets, own_offsets),
        (positions, sources.at[bead_rank, 0]), (momenta, own_momenta),
        (noise, sources.at[bead_rank, 1]), (mixing, own_mixing), (waves, own_waves),
    ]
    loads = [pltpu.make_async_copy(a, b, local_sem.at[i]) for i, (a, b) in enumerate(pairs)]
    for load in loads:
        load.start()
    for load in loads[0:4]:
        load.wait()

    rows = own_route[...]
    slot = slots_of(rows, BIN // planes)
    first = (rows * planes + own_cells[0:1]).astype(jnp.float32) + own_offsets[0:1]
    rest = own_cells[1:3].astype(jnp.float32) + own_offsets[1:3]
    own = jnp.concatenate([own_charges[...], first, rest], axis=0)
    halves = [each.astype(jnp.float32) for each in split3(own)]
    packed = jnp.concatenate(halves + [jnp.zeros_like(own)], axis=0).astype(jnp.bfloat16)
    got = lax.dot_general(packed, placement(slot), (NT, ((), ())), preferred_element_type=jnp.float32)
    fields[grid_rank] = (got[0:4] + got[4:8]) + got[8:12]

    pl.semaphore_wait(pltpu.get_barrier_semaphore(), others)
    field = shares("grid", lambda p: fields.at[grid_rank], lambda p: fields.at[p], field_send, field_recv)
    place = shares("bead", lambda p: positions, lambda p: sources.at[p, 0], place_send, place_recv)
    draw = shares("bead", lambda p: noise, lambda p: sources.at[p, 1], noise_send, noise_recv)
    kick = shares("bead", lambda p: kicks.at[bead_rank], lambda p: kicks.at[p], kick_send, kick_recv)
    summed = shares("bead", lambda p: level, lambda p: last.at[p], last_send, last_recv)
    own_pack = lax.div(grid_rank, PACK)
    place_in = lax.rem(grid_rank, PACK)

    def far(g, landing=False):
        return pltpu.make_async_remote_copy(
            src_ref=partial.at[g],
            dst_ref=landed.at[g if landing else grid_rank],
            send_sem=part_send.at[g],
            recv_sem=part_recv.at[g if landing else grid_rank],
            device_id={"grid": g},
            device_id_type=MESH,
        )

    def close(step, landing=False):
        peer = lax.rem(place_in * bead_count + bead_rank + step, PACK * bead_count)
        i, b = lax.div(peer, bead_count), lax.rem(peer, bead_count)
        at = (i, b) if landing else (place_in, bead_rank)
        return pltpu.make_async_remote_copy(
            src_ref=partial.at[own_pack * PACK + i],
            dst_ref=mates.at[at],
            send_sem=mate_send.at[i, b],
            recv_sem=mate_recv.at[at],
            device_id=(own_pack * PACK + i, b),
            device_id_type=MESH,
        )

    def each_far(act):
        def one(step, carry):
            act(lax.rem((own_pack + 1) * PACK + step, domains))
            return carry

        lax.fori_loop(0, domains - PACK, one, 0)

    def each_close(act):
        def one(step, carry):
            act(step)
            return carry

        lax.fori_loop(1, PACK * bead_count, one, 0)

    for each in (field, place, draw):
        each[0]()

    mesh_filter(total, filt)

    def weight_of(t, m):
        total = 0.0
        for k in range(neighbours.shape[1]):
            total += jnp.where(neighbours[t, k] == m, 0.5 * time_step * pair_strength * math.sqrt(pair_range), 0.0)
        return total

    loads[4].wait()
    loads[5].wait()

    def pair(chosen):
        pair_forces(
            weight_of, sources.at[bead_rank, 0], own_momenta, kicks.at[bead_rank], chosen
        )

    tiles = own_momenta.shape[2] // TILE
    early = tiles - tiles // 4
    pair(range(early))
    field[1]()

    def finished(pair):
        @pl.when(pair != own_pack)
        def _():
            for i in range(PACK):
                far(pair * PACK + i).start()

        @pl.when(pair == own_pack)
        def _():
            each_close(lambda step: close(step).start())

    mesh_phases(
        fields, own_waves, partial, track, along, total, near, filt, loads[8].wait,
        lambda: pair(range(early, tiles)), kick[0], finished,
    )

    mates[place_in, bead_rank] = partial[grid_rank]
    each_far(lambda g: far(g, True).wait_recv())

    def add(step, forces):
        return forces + landed[lax.rem((own_pack + 1) * PACK + step, domains)]

    level[...] = lax.fori_loop(0, domains - PACK, add, jnp.zeros(level.shape, jnp.float32))
    summed[0]()
    where = placement(slot)
    for each in (place, draw, kick):
        each[1]()
    loads[6].wait()
    loads[7].wait()
    mix = own_mixing[bead_rank]

    def stepped(c):
        parts = [sources[k, 0, c] for k in range(bead_count)]
        parts += [kicks[k, c] for k in range(bead_count)]
        parts += [sources[k, 1, c] for k in range(bead_count)]
        got = jnp.dot(mix, jnp.concatenate(parts, axis=0), precision=highest, preferred_element_type=jnp.float32)
        steps[0, c] = got[0:beads]
        steps[1, c] = got[beads:]

    for component in range(3):
        stepped(component)
    leave = pltpu.make_async_copy(steps, drifted, local_sem.at[len(pairs)])
    leave.start()
    each_close(lambda step: close(step, True).wait_recv())
    forces = level[...]
    for k in range(bead_count):
        for i in range(PACK):
            forces = forces + mates[i, k]
    summed[1]()
    last[bead_rank] = jnp.zeros(level.shape, jnp.float32)
    for k in range(bead_count):
        forces = forces + last[k]
    bins = GX // BIN
    forces = jnp.concatenate(
        [
            jnp.concatenate([forces[c * bins + s : c * bins + s + 1] for s in range(bins)], axis=1)
            for c in range(3)
        ],
        axis=0,
    )
    halves = [each.astype(jnp.float32) for each in split3(forces)]
    packed = jnp.concatenate(halves + [jnp.zeros((16 - 9, forces.shape[1]), jnp.float32)], axis=0)
    got = jnp.dot(packed.astype(jnp.bfloat16), where, preferred_element_type=jnp.float32)
    force = (got[0:3] + got[3:6]) + got[6:9]
    force_q[...] = centre[0] * force
    force_p[...] = centre[1] * force
    leave.wait()
    for each in (field, place, draw, kick, summed):
        each[2]()
    each_far(lambda g: far(g).wait_send())
    each_close(lambda step: close(step).wait_send())


def per_device(positions, momenta, noise, charges, slab_route, cells, offsets, nbr_tiles):
    grid_count = lax.axis_size("grid")
    bead_count = lax.axis_size("bead")
    beads, atoms = positions.shape[1:]
    slots = GX // BIN * CAP
    sheet = (3 * (GX // BIN), CAP)
    tables, centre = step_tables(beads * bead_count)
    shaped = tables.reshape(2, 3, bead_count, beads, -1).transpose(2, 0, 3, 1, 4)
    shaped = jnp.asarray(shaped.reshape(bead_count, 2 * beads, -1))
    centre = tuple(0.5 * time_step * value for value in centre)
    waves = wave_tables()
    vmem = pl.BlockSpec(memory_space=pltpu.VMEM)
    anywhere = pl.BlockSpec(memory_space=pl.ANY)
    dma = pltpu.SemaphoreType.DMA
    whole = lambda array: pltpu.VMEM(array.shape, array.dtype)
    f32 = lambda *shape: pltpu.VMEM(shape, jnp.float32)
    charges = charges.reshape(1, atoms)
    slab_route = slab_route.reshape(1, atoms)
    drifted, *force = pl.pallas_call(
        functools.partial(step_kernel, GX // grid_count, centre),
        out_shape=[
            jax.ShapeDtypeStruct((2, *positions.shape), jnp.float32),
            jax.ShapeDtypeStruct((3, atoms), jnp.float32),
            jax.ShapeDtypeStruct((3, atoms), jnp.float32),
        ],
        in_specs=[pl.BlockSpec(memory_space=pltpu.SMEM)] + [anywhere] * 9,
        out_specs=[anywhere, vmem, vmem],
        scratch_shapes=[
            whole(momenta), whole(charges), whole(slab_route), whole(cells), whole(offsets),
            whole(shaped), whole(waves),
            f32(grid_count, 4, slots),
            f32(bead_count, 2, *positions.shape),
            f32(bead_count, *positions.shape),
            f32(grid_count, *sheet),
            f32(grid_count, *sheet),
            f32(PACK, bead_count, *sheet),
            f32(*sheet),
            f32(bead_count, *sheet),
            f32(2, *positions.shape),
            f32(grid_count, 9, 4, slots),
            f32(grid_count // 2, GX // BIN, 2, WAVES, 2 * CAP),
            f32(GZ // 128, (GX + WINDOW - BIN) * WAVES, 128),
            pltpu.VMEM((2, (GX + WINDOW - BIN) * WAVES, GZ), jnp.bfloat16),
            f32(2, GX, GZ),
            dma((10,)),
            dma((grid_count,)), dma((grid_count,)),
            *[dma((bead_count,)) for _ in range(6)],
            dma((grid_count,)), dma((grid_count,)),
            dma((PACK, bead_count)), dma((PACK, bead_count)),
            dma((bead_count,)), dma((bead_count,)),
        ],
        compiler_params=pltpu.CompilerParams(
            collective_id=0, has_side_effects=True, vmem_limit_bytes=60 * 1024 * 1024
        ),
    )(nbr_tiles, positions, momenta, noise, charges, slab_route, cells, offsets, shaped, waves)
    return tuple(drifted[i] + force[i][:, None, :] for i in range(2))


def solution(mesh):
    in_specs = (
        P(None, "bead", "grid"),
        P(None, "bead", "grid"),
        P(None, "bead", "grid"),
        P("grid"),
        P("grid", None),
        P(None, "grid"),
        P(None, "grid"),
        P("grid", None),
    )
    out_specs = (P(None, "bead", "grid"), P(None, "bead", "grid"))

    def step(*args):
        return tuple(per_device(*args))

    return jax.shard_map(step, mesh=mesh, in_specs=in_specs, out_specs=out_specs, check_vma=False)
```
